32 devices in a mesh: segment: 16 (over z, x, core), slab: 2 (over y).
Axes of the slice: x: 2, y: 2, z: 4, core: 2. Of those that a mesh axis runs over, the one named last changes fastest.
Arguments:
- fwd_in: bfloat16 [16, 2, 32, 4, 4, 128], P('segment', None, None, 'slab'), may hold values from -6 to 6
- back_out: bfloat16 [16, 2, 32, 4, 4, 128], P('segment', None, None, 'slab'), may hold values from -6 to 6
- back_grad: bfloat16 [16, 2, 32, 4, 4, 128], P('segment', None, None, 'slab'), may hold values from -6 to 6
- batch_next: bfloat16 [2, 32, 4, 4, 128], P(None, None, 'slab'), may hold values from -6 to 6
- loss_grad: bfloat16 [2, 2, 32, 4, 4, 128], P(None, None, None, 'slab'), may hold values from -6 to 6
- weights: bfloat16 [16, 2, 32, 864], P('segment'), may hold values from -0.21875 to 0.21875
Outputs:
- fwd_out: bfloat16 [16, 2, 32, 4, 4, 128], P('segment', None, None, 'slab')
- back_acts: bfloat16 [16, 2, 32, 4, 4, 128], P('segment', None, None, 'slab')
- back_grads: bfloat16 [16, 2, 32, 4, 4, 128], P('segment', None, None, 'slab')
- weight_grads: float32 [16, 2, 32, 864], P('segment', None, None, 'slab')
The draws below stay inside these ranges and needn't reach their ends.
All inputs are finite; a program needn't handle non-finite values.
Results may differ from the reference program's by a relative error of at most 0.012.
Values may be sent and summed in bfloat16 or wider, within the bound.
A program may use at most 64 MiB of HBM per device.

```python
import jax
import jax.numpy as jnp
from jax import lax

C = 32
PLANE_H = 4
PLANE_W = 128
SEGMENTS = 16
DEPTH = 4
CELLS = 2048


def steps_of(key, dims, cuts, least, high):
    gain = 1.0
    for dim, parts in cuts:
        steps = jax.random.uniform(jax.random.fold_in(jax.random.fold_in(key, 6), dim), (parts,), jnp.float32, least / len(cuts), high / len(cuts))
        gain = gain * jnp.repeat(jnp.exp(steps), dims[dim] // parts).reshape((-1,) + (1,) * (len(dims) - 1 - dim))
    return gain


def noise(rng, dims, scale, bound, split=(), kind=jnp.bfloat16):
    array = scale * jax.random.normal(rng, dims, jnp.float32)
    if split:
        array = array * steps_of(rng, dims, split, -0.22, 0.18)
    return jnp.clip(array, -bound, bound).astype(kind)


def setup_inputs(seed: int = 0) -> dict:
    streams_of = jax.random.split(jax.random.key(seed), 7)
    return {
        "fwd_in": noise(streams_of[0], (SEGMENTS, 2, C, DEPTH, PLANE_H, PLANE_W), 1.0, 6.0, ((0, 16), (3, 2))),
        "back_out": noise(streams_of[1], (SEGMENTS, 2, C, DEPTH, PLANE_H, PLANE_W), 1.0, 6.0, ((0, 16), (3, 2))),
        "back_grad": noise(streams_of[2], (SEGMENTS, 2, C, DEPTH, PLANE_H, PLANE_W), 1.0, 6.0, ((0, 16), (3, 2))),
        "batch_next": noise(streams_of[3], (2, C, DEPTH, PLANE_H, PLANE_W), 1.0, 6.0, ((2, 2),)),
        "loss_grad": noise(streams_of[4], (2, 2, C, DEPTH, PLANE_H, PLANE_W), 1.0, 6.0, ((3, 2),)),
        "weights": noise(streams_of[5], (SEGMENTS, 2, C, 27 * C), (27 * C) ** -0.5, 0.21875, ((0, 16),)),
    }


def silu_round(value):
    return jax.nn.silu(value.astype(jnp.float32)).astype(jnp.bfloat16)

def silu_slope(value):
    wide = value.astype(jnp.float32)
    sig = jax.nn.sigmoid(wide)
    return sig * (1.0 + wide * (1.0 - sig))

def kernel_of(flat):
    chan = flat.shape[0]
    return flat.reshape(chan, chan, 3, 3, 3)

def conv_full(field, flat):
    out = lax.conv_general_dilated(field[None], kernel_of(flat), (1, 1, 1), ((1, 1), (1, 1), (1, 1)), dimension_numbers=('NCDHW', 'OIDHW', 'NCDHW'), preferred_element_type=jnp.float32)
    return out[0]

def conv_back(grad, flat):
    turned = jnp.flip(kernel_of(flat), (2, 3, 4)).transpose(1, 0, 2, 3, 4)
    out = lax.conv_general_dilated(grad[None], turned, (1, 1, 1), ((1, 1), (1, 1), (1, 1)), dimension_numbers=('NCDHW', 'OIDHW', 'NCDHW'), preferred_element_type=jnp.float32)
    return out[0]

def weight_grad(grad, field):
    padded = jnp.pad(field, ((0, 0), (1, 1), (1, 1), (1, 1)))
    out = lax.conv_general_dilated(padded[:, None], grad[:, None], (1, 1, 1), 'VALID', dimension_numbers=('NCDHW', 'OIDHW', 'NCDHW'), preferred_element_type=jnp.float32)
    out = out.transpose(1, 0, 2, 3, 4)
    return out.reshape(out.shape[0], -1)

def section(inputs):
    fin, back_pair, back_cot, wts = inputs
    x1 = fin[0]
    x2 = fin[1]
    y1 = (x1.astype(jnp.float32) + conv_full(silu_round(x2), wts[0])).astype(jnp.bfloat16)
    y2 = (x2.astype(jnp.float32) + conv_full(silu_round(y1), wts[1])).astype(jnp.bfloat16)
    out1 = back_pair[0]
    out2 = back_pair[1]
    grad1 = back_cot[0]
    grad2 = back_cot[1]
    hidden = silu_round(out1)
    rec2 = (out2.astype(jnp.float32) - conv_full(hidden, wts[1])).astype(jnp.bfloat16)
    act2 = silu_round(rec2)
    rec1 = (out1.astype(jnp.float32) - conv_full(act2, wts[0])).astype(jnp.bfloat16)
    grad_one = (grad1.astype(jnp.float32) + silu_slope(out1) * conv_back(grad2, wts[1])).astype(jnp.bfloat16)
    grad_two = (grad2.astype(jnp.float32) + silu_slope(rec2) * conv_back(grad_one, wts[0])).astype(jnp.bfloat16)
    scale = float(CELLS) ** (-0.5)
    dweights = jnp.stack([weight_grad(grad_one, act2), weight_grad(grad2, hidden)]) * scale
    return (jnp.stack([y1, y2]), jnp.stack([rec1, rec2]), jnp.stack([grad_one, grad_two]), dweights)

def reference(fwd_in, back_out, back_grad, batch_next, loss_grad, weights):
    fout1, rec1, din1, dw1 = lax.map(section, (fwd_in, back_out, back_grad, weights))
    fin2 = jnp.concatenate([batch_next[None], fout1[:-1]], axis=0)
    acts2 = jnp.concatenate([rec1[1:], fout1[-1:]], axis=0)
    grads2 = jnp.concatenate([din1[1:], loss_grad[0][None]], axis=0)
    fout2, rec2, din2, dw2 = lax.map(section, (fin2, acts2, grads2, weights))
    back_acts = jnp.concatenate([rec2[1:], fout2[-1:]], axis=0)
    back_grads = jnp.concatenate([din2[1:], loss_grad[1][None]], axis=0)
    return (fout2, back_acts, back_grads, dw1 + dw2)
```

```python
import functools

import jax
import jax.numpy as jnp
from jax import lax
from jax.experimental import pallas as pl
from jax.experimental.pallas import tpu as pltpu
from jax.sharding import PartitionSpec as P

MESH = pl.DeviceIdType.MESH
F, G, FT, GT = range(4)
X1, X2, O1, O2, G1, G2 = range(6)
Y1, Y2, R1, R2, E1, E2 = range(6)
PX, PH, PD, PY, PU, PE = range(6)


def sigmoid(v):
    return 1.0 / (1.0 + jnp.exp(-v))


def silu(v):
    return v / (1.0 + jnp.exp(-v))


def slope(v):
    sig = sigmoid(v)
    return sig * (1.0 + v * (1.0 - sig))


def kernel(
    dims, fwd_hbm, bout_hbm, bgrad_hbm, nxt_hbm, loss_hbm, kern_hbm, fout, backs, grads, dw,
    fwd, bout, bgrad, nxt, loss, kern, kt, w, dt, pad, stage, second, made, nat, acc, g3, dsum, dpart, dgot,
    halo_s, halo_r, seg_s, seg_r, out_s, d_s, d_r, in_s,
):
    C, D, H, W, segs, n, scale = dims
    DH, HW = D * H, H * W
    cs = C // n
    LW = pl.cdiv(3 * C, 128) * 128
    f32, bf16 = jnp.float32, jnp.bfloat16
    seg = lax.axis_index("segment")
    slab = lax.axis_index("slab")
    has_prev, has_next = seg > 0, seg < segs - 1
    is_first, is_last = seg == 0, seg == segs - 1
    prev_seg = lax.rem(seg + segs - 1, segs)
    next_seg = lax.rem(seg + 1, segs)
    lane_no = lax.broadcasted_iota(jnp.int32, (C, W), 1)

    fetches = [
        pltpu.make_async_copy(src, dst, in_s.at[i])
        for i, (src, dst) in enumerate(
            [
                (bgrad_hbm, bgrad), (bout_hbm, bout), (fwd_hbm, fwd),
                (kern_hbm, kern), (nxt_hbm, nxt), (loss_hbm, loss),
            ]
        )
    ]
    for fetch in fetches:
        fetch.start()

    barrier = pltpu.get_barrier_semaphore()

    @pl.when(has_prev)
    def _():
        pl.semaphore_signal(barrier, inc=1, device_id={"segment": prev_seg}, device_id_type=MESH)

    @pl.when(has_next)
    def _():
        pl.semaphore_signal(barrier, inc=1, device_id={"segment": next_seg}, device_id_type=MESH)

    for k in range(1, n):
        pl.semaphore_signal(
            barrier, inc=1, device_id={"slab": lax.rem(slab + k, n)}, device_id_type=MESH
        )

    def lane(q, hh):
        return (q * (H + 2) + hh) * W

    zero = jnp.zeros((C, W), bf16)
    for t in range(2):
        for k in range(6):
            for q in range(D + 2):
                for hh in (0, H + 1):
                    pad[t, k, :, pl.ds(lane(q, hh), W)] = zero

    @pl.when(slab == 0)
    def _():
        for t in range(2):
            for k in range(6):
                pad[t, k, :, pl.ds(lane(0, 1), HW)] = jnp.zeros((C, HW), bf16)

    @pl.when(slab == n - 1)
    def _():
        for t in range(2):
            for k in range(6):
                pad[t, k, :, pl.ds(lane(D + 1, 1), HW)] = jnp.zeros((C, HW), bf16)

    def load_stage(slot, ref, s):
        stage[slot] = ref[s].astype(f32)

    def staged(slot, r):
        return stage[slot, pl.ds(r, C, stride=DH), :]

    def prepare_weights():
        fetches[3].wait()
        wide = kern[...].astype(f32)
        kt[...] = jnp.concatenate([wide, jnp.zeros((LW - 2 * C, 27 * C), f32)], axis=0).T

        def tap(t):
            return kt[pl.ds(t, C, stride=27), :]

        for a in range(3):
            for c in range(3):
                block = jnp.concatenate([tap(9 * a + 3 * b + c) for b in range(3)], axis=0).T
                for f in range(2):
                    w[F + f, a, c * C : (c + 1) * C, :] = block[f * C : (f + 1) * C].astype(bf16)
                for f in range(2):
                    turned = jnp.concatenate(
                        [
                            tap(9 * (2 - a) + 3 * (2 - b) + 2 - c)[:, f * C : (f + 1) * C]
                            for b in range(3)
                        ],
                        axis=1,
                    )
                    w[FT + f, a, c * C : (c + 1) * C, :] = turned.astype(bf16)

    def load_pair(i, slot, ref):
        fetches[i].wait()
        for s in range(2):
            load_stage(slot + s, ref, s)

    def halo(t, k, up):
        src_q, dst_q = (D, 0) if up else (1, D + 1)
        target = lax.rem(slab + (1 if up else n - 1), n)
        return pltpu.make_async_remote_copy(
            src_ref=pad.at[t, k, :, pl.ds(lane(src_q, 1), HW)],
            dst_ref=pad.at[t, k, :, pl.ds(lane(dst_q, 1), HW)],
            send_sem=halo_s.at[t, k, up],
            recv_sem=halo_r.at[t, k, up],
            device_id={"slab": target},
            device_id_type=MESH,
        )

    def halo_start(t, k):
        @pl.when(slab < n - 1)
        def _():
            halo(t, k, 1).start()

        @pl.when(slab > 0)
        def _():
            halo(t, k, 0).start()

    def halo_arrived(t, k):
        @pl.when(slab > 0)
        def _():
            halo(t, k, 1).wait_recv()

        @pl.when(slab < n - 1)
        def _():
            halo(t, k, 0).wait_recv()

    def halo_sent(t, k):
        @pl.when(slab < n - 1)
        def _():
            halo(t, k, 1).wait_send()

        @pl.when(slab > 0)
        def _():
            halo(t, k, 0).wait_send()

    def to_next(k):
        return pltpu.make_async_remote_copy(
            src_ref=made.at[0, k], dst_ref=second.at[X1 + k],
            send_sem=seg_s.at[0, k], recv_sem=seg_r.at[0, k],
            device_id={"segment": next_seg}, device_id_type=MESH,
        )

    def to_prev(k):
        return pltpu.make_async_remote_copy(
            src_ref=made.at[0, k], dst_ref=second.at[k],
            send_sem=seg_s.at[0, k], recv_sem=seg_r.at[0, k],
            device_id={"segment": prev_seg}, device_id_type=MESH,
        )

    def out_prev(k):
        dst = backs.at[k - R1] if k < E1 else grads.at[k - E1]
        return pltpu.make_async_remote_copy(
            src_ref=nat.at[k], dst_ref=dst,
            send_sem=seg_s.at[1, k], recv_sem=seg_r.at[1, k],
            device_id={"segment": prev_seg}, device_id_type=MESH,
        )

    def own_out(k):
        return pltpu.make_async_copy(nat.at[k], fout.at[k], out_s.at[k])

    def last_act(k):
        return pltpu.make_async_copy(nat.at[k], backs.at[k], out_s.at[2 + k])

    def last_grad(k):
        return pltpu.make_async_copy(loss.at[2 + k], grads.at[k], out_s.at[4 + k])

    def put(t, k, r, value):
        d, h = divmod(r, H)
        pad[t, k, :, pl.ds(lane(d + 1, h + 1), W)] = value.astype(bf16)

    def tall(t, k, q):
        return jnp.concatenate([pad[t, k, :, pl.ds(lane(q, b), HW)] for b in range(3)], axis=0)

    def conv_local(t, k, m, slot):
        for p in range(D):
            total = None
            for a in range(3):
                if 1 <= p + a <= D:
                    part = jnp.dot(w[m, a], tall(t, k, p + a), preferred_element_type=f32)
                    total = part if total is None else total + part
            acc[slot, :, pl.ds(p * HW, HW)] = total

    def conv_finish(t, k, m, slot):
        for p in range(D):
            total = acc[slot, :, pl.ds(p * HW, HW)]
            for a in range(3):
                if not 1 <= p + a <= D:
                    total += jnp.dot(w[m, a], tall(t, k, p + a), preferred_element_type=f32)
            for h in range(H):
                y = total[:, h * W : (h + 1) * W]
                left = jnp.where(lane_no == 0, 0.0, pltpu.roll(y[:C], 1, 1))
                right = jnp.where(lane_no == W - 1, 0.0, pltpu.roll(y[2 * C :], W - 1, 1))
                yield p * H + h, y[C : 2 * C] + left + right

    def widen(j, r, v):
        at = pl.ds(r * W, W)
        g3[j, 0:C, at] = jnp.where(lane_no == W - 1, 0.0, pltpu.roll(v, W - 1, 1)).astype(bf16)
        g3[j, C : 2 * C, at] = v.astype(bf16)
        g3[j, 2 * C : 3 * C, at] = jnp.where(lane_no == 0, 0.0, pltpu.roll(v, 1, 1)).astype(bf16)

    def wgrad(t, k, j):
        total = None
        for p in range(D):
            lhs = jnp.concatenate([tall(t, k, p + a) for a in range(3)], axis=0)
            part = lax.dot_general(
                lhs, g3[j, :, pl.ds(p * HW, HW)], (((1,), (1,)), ((), ())),
                preferred_element_type=f32,
            )
            total = part if total is None else total + part
        if t == 0:
            dsum[j] = total
            return
        total += dsum[j]
        total = jnp.concatenate([total, jnp.zeros((9 * C, LW - 3 * C), f32)], axis=1)
        for q in range(n):
            for ab in range(9):
                dpart[j, q, ab] = total[ab * C + q * cs : ab * C + (q + 1) * cs]
        for q in range(1, n):
            share(j, q).start()

    def share(j, q):
        target = lax.rem(slab + q, n)
        return pltpu.make_async_remote_copy(
            src_ref=dpart.at[j, target], dst_ref=dgot.at[j, q],
            send_sem=d_s.at[j, q], recv_sem=d_r.at[j, q],
            device_id={"slab": target}, device_id_type=MESH,
        )

    def keep(t, k, r, value):
        held = value.astype(bf16)
        made[t, k, :, pl.ds(r * W, W)] = held
        wide = held.astype(f32)
        if t == 1:
            stage[k, pl.ds(r, C, stride=DH), :] = wide
        return wide

    def send_made(t, k):
        if t == 0:
            if k < R1:
                @pl.when(has_next)
                def _():
                    to_next(k).start()

                @pl.when(is_last)
                def _():
                    second[O1 + k] = made[0, k]
            else:
                @pl.when(has_prev)
                def _():
                    to_prev(k).start()
            return
        nat[k] = stage[k].astype(bf16)
        if k < R1:
            own_out(k).start()

            @pl.when(is_last)
            def _():
                last_act(k).start()
        else:
            @pl.when(has_prev)
            def _():
                out_prev(k).start()

    def tick(t, get, ready):
        if t == 0:
            load_pair(0, G1, bgrad)
        ready(G2)
        for r in range(DH):
            put(t, PD, r, get(G2, r))
        if t == 0:
            peers = has_prev.astype(jnp.int32) + has_next.astype(jnp.int32) + n - 1
            pl.semaphore_wait(barrier, peers)
        halo_start(t, PD)
        if t == 0:
            load_pair(1, O1, bout)
        ready(O1)
        for r in range(DH):
            put(t, PH, r, silu(get(O1, r)))
        halo_start(t, PH)
        if t == 0:
            load_pair(2, X1, fwd)
        ready(X2)
        for r in range(DH):
            put(t, PX, r, silu(get(X2, r)))
        halo_start(t, PX)
        if t == 0:
            prepare_weights()
        conv_local(t, PD, GT, 0)
        conv_local(t, PH, G, 1)
        conv_local(t, PX, F, 2)
        for r in range(DH):
            widen(1, r, get(G2, r))

        ready(G1)
        halo_arrived(t, PD)
        for r, out in conv_finish(t, PD, GT, 0):
            put(t, PE, r, keep(t, E1, r, get(G1, r) + slope(get(O1, r)) * out))
        halo_start(t, PE)
        send_made(t, E1)
        ready(O2)
        halo_arrived(t, PH)
        for r, out in conv_finish(t, PH, G, 1):
            put(t, PU, r, silu(keep(t, R2, r, get(O2, r) - out)))
        halo_start(t, PU)
        send_made(t, R2)
        ready(X1)
        halo_arrived(t, PX)
        for r, out in conv_finish(t, PX, F, 2):
            put(t, PY, r, silu(keep(t, Y1, r, get(X1, r) + out)))
        halo_start(t, PY)
        send_made(t, Y1)

        conv_local(t, PE, FT, 0)
        conv_local(t, PU, F, 1)
        conv_local(t, PY, G, 2)
        wgrad(t, PH, 1)
        for r in range(DH):
            widen(0, r, made[t, E1, :, pl.ds(r * W, W)].astype(f32))

        halo_arrived(t, PE)
        for r, out in conv_finish(t, PE, FT, 0):
            v = made[t, R2, :, pl.ds(r * W, W)].astype(f32)
            keep(t, E2, r, get(G2, r) + slope(v) * out)
        send_made(t, E2)
        halo_arrived(t, PU)
        if t == 1:
            wgrad(t, PU, 0)
        for r, out in conv_finish(t, PU, F, 1):
            keep(t, R1, r, get(O1, r) - out)
        send_made(t, R1)
        halo_arrived(t, PY)
        for r, out in conv_finish(t, PY, G, 2):
            keep(t, Y2, r, get(X2, r) + out)
        send_made(t, Y2)
        if t == 0:
            wgrad(t, PU, 0)

    tick(0, staged, lambda k: None)

    fetches[4].wait()
    fetches[5].wait()

    @pl.when(is_first)
    def _():
        for s in range(2):
            load_stage(X1 + s, nxt, s)
            for r in range(DH):
                second[X1 + s, :, pl.ds(r * W, W)] = staged(X1 + s, r).astype(bf16)

    @pl.when(is_last)
    def _():
        for s in range(2):
            last_grad(s).start()
            load_stage(G1 + s, loss, s)
            for r in range(DH):
                second[G1 + s, :, pl.ds(r * W, W)] = staged(G1 + s, r).astype(bf16)

    def arrived(k):
        if k <= X2:
            @pl.when(has_prev)
            def _():
                to_next(k).wait_recv()
        else:
            @pl.when(has_next)
            def _():
                to_prev(k).wait_recv()

    tick(1, lambda k, r: second[k, :, pl.ds(r * W, W)].astype(f32), arrived)

    for j in (1, 0):
        for q in range(1, n):
            share(j, q).wait_recv()
        total = dpart[j, slab]
        for q in range(1, n):
            total += dgot[j, q]
        total *= scale
        for ab in range(9):
            for c in range(3):
                tap = total[ab] if c == 0 else pltpu.roll(total[ab], LW - c * C, 1)
                dt[j, pl.ds(3 * ab + c, cs, stride=27), :] = tap
        dw[j] = dt[j].T[:C]

    for t in range(2):
        for k in range(6):
            halo_sent(t, k)
    for j in range(2):
        for q in range(1, n):
            share(j, q).wait_send()
    for k in (Y1, Y2):
        own_out(k).wait()

    @pl.when(is_last)
    def _():
        for k in (Y1, Y2):
            last_act(k).wait()
            last_grad(k).wait()

    @pl.when(has_next)
    def _():
        for k in (Y1, Y2):
            to_next(k).wait_send()
        for k in (R1, R2, E1, E2):
            out_prev(k).wait_recv()

    @pl.when(has_prev)
    def _():
        for k in (R1, R2, E1, E2):
            to_prev(k).wait_send()
            out_prev(k).wait_send()


def write_out(*refs):
    srcs, dsts, sems = refs[:4], refs[4:8], refs[8]
    writes = [pltpu.make_async_copy(a, b, sems.at[i]) for i, (a, b) in enumerate(zip(srcs, dsts))]
    for write in writes:
        write.start()
    for write in writes:
        write.wait()


def local(segs, n, fwd_in, back_out, back_grad, batch_next, loss_grad, weights):
    _, _, C, D, H, W = fwd_in.shape
    rows = C * D * H
    cs = C // n
    f32, bf16 = jnp.float32, jnp.bfloat16
    scale = float(D * n * H * W) ** (-0.5)
    vmem = pl.BlockSpec(memory_space=pltpu.VMEM)
    hbm = pl.BlockSpec(memory_space=pltpu.HBM)
    wide = pl.cdiv(3 * C, 128) * 128
    anywhere = pl.BlockSpec(memory_space=pl.ANY)
    pair = jax.ShapeDtypeStruct((2, rows, W), bf16)
    share = jax.ShapeDtypeStruct((2, C, 27 * cs), f32)
    dma = pltpu.SemaphoreType.DMA
    fout, backs, grads, dw = pl.pallas_call(
        functools.partial(kernel, (C, D, H, W, segs, n, scale)),
        out_shape=tuple(pltpu.VMEM(x.shape, x.dtype) for x in (pair, pair, pair, share)),
        in_specs=[hbm] * 6,
        out_specs=(vmem, vmem, vmem, vmem),
        scratch_shapes=[
            pltpu.VMEM((2, rows, W), bf16),
            pltpu.VMEM((2, rows, W), bf16),
            pltpu.VMEM((2, rows, W), bf16),
            pltpu.VMEM((2, rows, W), bf16),
            pltpu.VMEM((4, rows, W), bf16),
            pltpu.VMEM((2 * C, 27 * C), bf16),
            pltpu.VMEM((27 * C, wide), f32),
            pltpu.VMEM((4, 3, 3 * C, 3 * C), bf16),
            pltpu.VMEM((2, 27 * cs, wide), f32),
            pltpu.VMEM((2, 6, C, (D + 2) * (H + 2) * W), bf16),
            pltpu.VMEM((6, rows, W), f32),
            pltpu.VMEM((6, C, D * H * W), bf16),
            pltpu.VMEM((2, 6, C, D * H * W), bf16),
            pltpu.VMEM((6, rows, W), bf16),
            pltpu.VMEM((3, 3 * C, D * H * W), f32),
            pltpu.VMEM((2, 3 * C, D * H * W), bf16),
            pltpu.VMEM((2, 9 * C, 3 * C), f32),
            pltpu.VMEM((2, n, 9, cs, wide), f32),
            pltpu.VMEM((2, n, 9, cs, wide), f32),
            dma((2, 6, 2)),
            dma((2, 6, 2)),
            dma((2, 6)),
            dma((2, 6)),
            dma((6,)),
            dma((2, n)),
            dma((2, n)),
            dma((6,)),
        ],
        compiler_params=pltpu.CompilerParams(
            collective_id=0, has_side_effects=True, vmem_limit_bytes=48 << 20
        ),
        name="petra",
    )(
        *[
            pltpu.with_memory_space_constraint(x, pltpu.HBM)
            for x in (
                fwd_in.reshape(2, rows, W),
                back_out.reshape(2, rows, W),
                back_grad.reshape(2, rows, W),
                batch_next.reshape(2, rows, W),
                loss_grad.reshape(4, rows, W),
                weights.reshape(2 * C, 27 * C),
            )
        ]
    )
    fout, backs, grads, dw = pl.pallas_call(
        write_out,
        out_shape=(pair, pair, pair, share),
        in_specs=[vmem] * 4,
        out_specs=(hbm,) * 4,
        scratch_shapes=[dma((4,))],
        compiler_params=pltpu.CompilerParams(vmem_limit_bytes=4 << 20),
        name="write_out",
    )(fout, backs, grads, dw)
    shape = fwd_in.shape
    return fout.reshape(shape), backs.reshape(shape), grads.reshape(shape), dw[None]


def solution(mesh):
    field = P("segment", None, None, "slab", None, None)
    return jax.shard_map(
        functools.partial(local, mesh.shape["segment"], mesh.shape["slab"]),
        mesh=mesh,
        in_specs=(
            field,
            field,
            field,
            P(None, None, "slab", None, None),
            P(None, None, None, "slab", None, None),
            P("segment", None, None, None),
        ),
        out_specs=(field, field, field, P("segment", None, None, "slab")),
        check_vma=False,
    )
```

```python
import functools

import jax
import jax.numpy as jnp
from jax import lax
from jax.experimental import pallas as pl
from jax.experimental.pallas import tpu as pltpu
from jax.sharding import PartitionSpec as P

MESH = pl.DeviceIdType.MESH
F, G, FT, GT = range(4)
X1, X2, O1, O2, G1, G2 = range(6)
Y1, Y2, R1, R2, E1, E2 = range(6)
PX, PH, PD, PY, PU, PE = range(6)


def sigmoid(v):
    return 1.0 / (1.0 + jnp.exp(-v))


def silu(v):
    return v / (1.0 + jnp.exp(-v))


def slope(v):
    sig = sigmoid(v)
    return sig * (1.0 + v * (1.0 - sig))


def kernel(
    dims, fwd_hbm, bout_hbm, bgrad_hbm, nxt_hbm, loss_hbm, kern_hbm, fout, backs, grads, dw,
    fwd, bout, bgrad, nxt, loss, kern, kt, w, dt, pad, stage, second, edge, made, nat, acc, g3,
    dsum, dpart, dgot, halo_s, halo_r, seg_s, seg_r, edge_s, edge_r, out_s, d_s, d_r, in_s, ready_s,
):
    C, D, H, W, segs, n, scale = dims
    DH, HW = D * H, H * W
    cs = C // n
    LW = pl.cdiv(3 * C, 128) * 128
    f32, bf16 = jnp.float32, jnp.bfloat16
    seg = lax.axis_index("segment")
    slab = lax.axis_index("slab")
    has_prev, has_next = seg > 0, seg < segs - 1
    is_first, is_last = seg == 0, seg == segs - 1
    has_below, has_above = slab > 0, slab < n - 1
    prev_seg = lax.rem(seg + segs - 1, segs)
    next_seg = lax.rem(seg + 1, segs)
    below, above = lax.rem(slab + n - 1, n), lax.rem(slab + 1, n)
    lane_no = lax.broadcasted_iota(jnp.int32, (C, W), 1)

    barrier = pltpu.get_barrier_semaphore()

    for k in range(1, n):
        pl.semaphore_signal(
            barrier, inc=1, device_id={"slab": lax.rem(slab + k, n)}, device_id_type=MESH
        )

    @pl.when(has_prev)
    def _():
        pl.semaphore_signal(barrier, inc=1, device_id={"segment": prev_seg}, device_id_type=MESH)

    @pl.when(has_next)
    def _():
        pl.semaphore_signal(barrier, inc=1, device_id={"segment": next_seg}, device_id_type=MESH)

    fetches = [
        pltpu.make_async_copy(src, dst, in_s.at[i])
        for i, (src, dst) in enumerate(
            [
                (bgrad_hbm, bgrad), (bout_hbm, bout), (fwd_hbm, fwd),
                (kern_hbm, kern), (nxt_hbm, nxt), (loss_hbm, loss),
            ]
        )
    ]
    for fetch in fetches:
        fetch.start()

    def lane(q, hh):
        return ((q + 2) * (H + 2) + hh) * W

    zero = jnp.zeros((C, W), bf16)
    for t in range(2):
        for k in range(6):
            reach = 2 if t == 1 and k in (PH, PD) else 1
            for q in range(-reach, D + reach):
                for hh in (0, H + 1):
                    pad[t, k, :, pl.ds(lane(q, hh), W)] = zero

    @pl.when(slab == 0)
    def _():
        for t in range(2):
            for k in range(6):
                pad[t, k, :, pl.ds(lane(-1, 1), HW)] = jnp.zeros((C, HW), bf16)

    @pl.when(slab == n - 1)
    def _():
        for t in range(2):
            for k in range(6):
                pad[t, k, :, pl.ds(lane(D, 1), HW)] = jnp.zeros((C, HW), bf16)

    def load_stage(slot, ref, s):
        stage[slot] = ref[s].astype(f32)

    def staged(slot, r):
        return stage[slot, pl.ds(r, C, stride=DH), :]

    def prepare_weights():
        fetches[3].wait()
        wide = kern[...].astype(f32)
        kt[...] = jnp.concatenate([wide, jnp.zeros((LW - 2 * C, 27 * C), f32)], axis=0).T

        def tap(t):
            return kt[pl.ds(t, C, stride=27), :]

        for a in range(3):
            for c in range(3):
                block = jnp.concatenate([tap(9 * a + 3 * b + c) for b in range(3)], axis=0).T
                for f in range(2):
                    w[F + f, a, c * C : (c + 1) * C, :] = block[f * C : (f + 1) * C].astype(bf16)
                for f in range(2):
                    turned = jnp.concatenate(
                        [
                            tap(9 * (2 - a) + 3 * (2 - b) + 2 - c)[:, f * C : (f + 1) * C]
                            for b in range(3)
                        ],
                        axis=1,
                    )
                    w[FT + f, a, c * C : (c + 1) * C, :] = turned.astype(bf16)

    def load_pair(i, slot, ref):
        fetches[i].wait()
        for s in range(2):
            load_stage(slot + s, ref, s)

    def halo(t, k, side):
        src_q, dst_q = (D - 1, -1) if side == 0 else (0, D)
        return pltpu.make_async_remote_copy(
            src_ref=pad.at[t, k, :, pl.ds(lane(src_q, 1), HW)],
            dst_ref=pad.at[t, k, :, pl.ds(lane(dst_q, 1), HW)],
            send_sem=halo_s.at[t, k, side],
            recv_sem=halo_r.at[t, k, side],
            device_id={"slab": above if side == 0 else below},
            device_id_type=MESH,
        )

    def by_side(to):
        return ((0, has_above), (1, has_below)) if to else ((0, has_below), (1, has_above))

    def halo_start(t, k):
        for side, there in by_side(True):
            @pl.when(there)
            def _():
                halo(t, k, side).start()

    def halo_arrived(t, k):
        for side, there in by_side(False):
            @pl.when(there)
            def _():
                halo(t, k, side).wait_recv()

    def halo_sent(t, k):
        for side, there in by_side(True):
            @pl.when(there)
            def _():
                halo(t, k, side).wait_send()

    def to_seg(k):
        return pltpu.make_async_remote_copy(
            src_ref=made.at[0, k], dst_ref=second.at[k],
            send_sem=seg_s.at[0, k], recv_sem=seg_r.at[0, k],
            device_id={"segment": next_seg if k <= X2 else prev_seg}, device_id_type=MESH,
        )

    def edge_planes(k):
        return 2 if k in (O1, G2) else 1

    def edge_copy(src, k, side, target, which):
        planes = edge_planes(k)
        src_at, dst_at = ((D - planes) * HW, (2 - planes) * HW) if side == 0 else (0, 0)
        return pltpu.make_async_remote_copy(
            src_ref=src.at[:, pl.ds(src_at, planes * HW)],
            dst_ref=edge.at[k, side, :, pl.ds(dst_at, planes * HW)],
            send_sem=edge_s.at[which, k, side], recv_sem=edge_r.at[k, side],
            device_id={"segment": target, "slab": above if side == 0 else below},
            device_id_type=MESH,
        )

    def edge_start(src, k, target, which):
        for side, there in by_side(True):
            @pl.when(there)
            def _():
                edge_copy(src, k, side, target, which).start()

    def edge_sent(src, k, target, which):
        for side, there in by_side(True):
            @pl.when(there)
            def _():
                edge_copy(src, k, side, target, which).wait_send()

    def out_prev(k):
        dst = backs.at[k - R1] if k < E1 else grads.at[k - E1]
        return pltpu.make_async_remote_copy(
            src_ref=nat.at[k], dst_ref=dst,
            send_sem=seg_s.at[1, k], recv_sem=seg_r.at[1, k],
            device_id={"segment": prev_seg}, device_id_type=MESH,
        )

    def own_out(k):
        return pltpu.make_async_copy(nat.at[k], fout.at[k], out_s.at[k])

    def last_act(k):
        return pltpu.make_async_copy(nat.at[k], backs.at[k], out_s.at[2 + k])

    def last_grad(k):
        return pltpu.make_async_copy(loss.at[2 + k], grads.at[k], out_s.at[4 + k])

    def put(t, k, r, value):
        d, h = divmod(r, H)
        pad[t, k, :, pl.ds(lane(d, h + 1), W)] = value.astype(bf16)

    def tall(t, k, q):
        return jnp.concatenate([pad[t, k, :, pl.ds(lane(q, b), HW)] for b in range(3)], axis=0)

    def taps(t, k, m, p, which):
        total = None
        for a in which:
            part = jnp.dot(w[m, a], tall(t, k, p + a - 1), preferred_element_type=f32)
            total = part if total is None else total + part
        return total

    def inner(p):
        return [a for a in range(3) if 0 <= p + a - 1 < D]

    def outer(p):
        return [a for a in range(3) if not 0 <= p + a - 1 < D]

    def conv_local(t, k, m, slot):
        for p in range(D):
            acc[slot, :, pl.ds(p * HW, HW)] = taps(t, k, m, p, inner(p))

    def rows_of(total):
        for h in range(H):
            y = total[:, h * W : (h + 1) * W]
            left = jnp.where(lane_no == 0, 0.0, pltpu.roll(y[:C], 1, 1))
            right = jnp.where(lane_no == W - 1, 0.0, pltpu.roll(y[2 * C :], W - 1, 1))
            yield h, y[C : 2 * C] + left + right

    def conv_finish(t, k, m, slot):
        for p in range(D):
            total = acc[slot, :, pl.ds(p * HW, HW)]
            if outer(p):
                total += taps(t, k, m, p, outer(p))
            for h, out in rows_of(total):
                yield p * H + h, out

    def conv_whole(t, k, m):
        for p in range(D):
            for h, out in rows_of(taps(t, k, m, p, range(3))):
                yield p * H + h, out

    def conv_plane(t, k, m, p):
        yield from rows_of(taps(t, k, m, p, range(3)))

    def widen(j, r, v):
        at = pl.ds(r * W, W)
        g3[j, 0:C, at] = jnp.where(lane_no == W - 1, 0.0, pltpu.roll(v, W - 1, 1)).astype(bf16)
        g3[j, C : 2 * C, at] = v.astype(bf16)
        g3[j, 2 * C : 3 * C, at] = jnp.where(lane_no == 0, 0.0, pltpu.roll(v, 1, 1)).astype(bf16)

    def wgrad(t, k, j):
        total = None
        for p in range(D):
            lhs = jnp.concatenate([tall(t, k, p + a - 1) for a in range(3)], axis=0)
            part = lax.dot_general(
                lhs, g3[j, :, pl.ds(p * HW, HW)], (((1,), (1,)), ((), ())),
                preferred_element_type=f32,
            )
            total = part if total is None else total + part
        if t == 0:
            dsum[j] = total
            return
        total += dsum[j]
        total = jnp.concatenate([total, jnp.zeros((9 * C, LW - 3 * C), f32)], axis=1)
        for q in range(n):
            for ab in range(9):
                dpart[j, q, ab] = total[ab * C + q * cs : ab * C + (q + 1) * cs]
        for q in range(1, n):
            share(j, q).start()

    def share(j, q):
        target = lax.rem(slab + q, n)
        return pltpu.make_async_remote_copy(
            src_ref=dpart.at[j, target], dst_ref=dgot.at[j, q],
            send_sem=d_s.at[j, q], recv_sem=d_r.at[j, q],
            device_id={"slab": target}, device_id_type=MESH,
        )

    def keep(t, k, r, value):
        held = value.astype(bf16)
        made[t, k, :, pl.ds(r * W, W)] = held
        wide = held.astype(f32)
        if t == 1:
            stage[k, pl.ds(r, C, stride=DH), :] = wide
        return wide

    def hand_on(k):
        src = made.at[0, k]
        if k <= X2:
            @pl.when(has_next)
            def _():
                to_seg(k).start()
                if k == Y2:
                    edge_start(src, X2, next_seg, 0)

            @pl.when(is_last)
            def _():
                edge_start(src, O1 + k, seg, 1)
                second[O1 + k] = made[0, k]
        else:
            @pl.when(has_prev)
            def _():
                to_seg(k).start()
                edge_start(src, k, prev_seg, 0)

    def give_out(k):
        nat[k] = stage[k].astype(bf16)
        if k < R1:
            own_out(k).start()

            @pl.when(is_last)
            def _():
                last_act(k).start()
        else:
            @pl.when(has_prev)
            def _():
                out_prev(k).start()

    def arrived(k):
        @pl.when(has_prev if k <= X2 else has_next)
        def _():
            to_seg(k).wait_recv()

    def edge_arrived(k, side):
        edge_copy(made.at[0, k], k, side, seg, 0).wait_recv()

    load_pair(0, G1, bgrad)
    for r in range(DH):
        put(0, PD, r, staged(G2, r))
    peers = has_prev.astype(jnp.int32) + has_next.astype(jnp.int32) + n - 1
    pl.semaphore_wait(barrier, peers)
    halo_start(0, PD)

    @pl.when(has_prev)
    def _():
        pl.semaphore_signal(
            ready_s.at[1], inc=1, device_id={"segment": prev_seg}, device_id_type=MESH
        )

    @pl.when(has_next)
    def _():
        pl.semaphore_signal(
            ready_s.at[0], inc=1, device_id={"segment": next_seg}, device_id_type=MESH
        )

    load_pair(1, O1, bout)
    for r in range(DH):
        put(0, PH, r, silu(staged(O1, r)))
    halo_start(0, PH)
    load_pair(2, X1, fwd)
    for r in range(DH):
        put(0, PX, r, silu(staged(X2, r)))
    halo_start(0, PX)
    prepare_weights()
    conv_local(0, PD, GT, 0)
    conv_local(0, PH, G, 1)
    conv_local(0, PX, F, 2)
    for r in range(DH):
        widen(1, r, staged(G2, r))

    fetches[4].wait()
    fetches[5].wait()

    @pl.when(is_first)
    def _():
        for s in range(2):
            load_stage(6 + s, nxt, s)
            for r in range(DH):
                second[X1 + s, :, pl.ds(r * W, W)] = staged(6 + s, r).astype(bf16)
        edge_start(second.at[X2], X2, seg, 1)

    @pl.when(is_last)
    def _():
        for s in range(2):
            last_grad(s).start()
            load_stage(6 + s, loss, s)
            for r in range(DH):
                second[G1 + s, :, pl.ds(r * W, W)] = staged(6 + s, r).astype(bf16)
            edge_start(second.at[G1 + s], G1 + s, seg, 1)

    @pl.when(has_prev)
    def _():
        pl.semaphore_wait(ready_s.at[0], 1)

    @pl.when(has_next)
    def _():
        pl.semaphore_wait(ready_s.at[1], 1)

    halo_arrived(0, PD)
    for r, out in conv_finish(0, PD, GT, 0):
        put(0, PE, r, keep(0, E1, r, staged(G1, r) + slope(staged(O1, r)) * out))
    halo_start(0, PE)
    hand_on(E1)
    halo_arrived(0, PH)
    for r, out in conv_finish(0, PH, G, 1):
        put(0, PU, r, silu(keep(0, R2, r, staged(O2, r) - out)))
    halo_start(0, PU)
    hand_on(R2)
    halo_arrived(0, PX)
    for r, out in conv_finish(0, PX, F, 2):
        put(0, PY, r, silu(keep(0, Y1, r, staged(X1, r) + out)))
    halo_start(0, PY)
    hand_on(Y1)

    conv_local(0, PE, FT, 0)
    conv_local(0, PU, F, 1)
    conv_local(0, PY, G, 2)
    wgrad(0, PH, 1)
    for r in range(DH):
        widen(0, r, made[0, E1, :, pl.ds(r * W, W)].astype(f32))

    halo_arrived(0, PE)
    for r, out in conv_finish(0, PE, FT, 0):
        v = made[0, R2, :, pl.ds(r * W, W)].astype(f32)
        keep(0, E2, r, staged(G2, r) + slope(v) * out)
    hand_on(E2)
    halo_arrived(0, PU)
    for r, out in conv_finish(0, PU, F, 1):
        keep(0, R1, r, staged(O1, r) - out)
    hand_on(R1)
    halo_arrived(0, PY)
    for r, out in conv_finish(0, PY, G, 2):
        keep(0, Y2, r, staged(X2, r) + out)
    hand_on(Y2)
    wgrad(0, PU, 0)

    def got(k, r):
        return second[k, :, pl.ds(r * W, W)].astype(f32)

    def near(k, side, h):
        return edge[k, side, :, pl.ds((HW if side == 0 else 0) + h * W, W)].astype(f32)

    def edge_q(side, j):
        return -2 + j if side == 0 else D + j

    arrived(G2)
    for d in range(D):
        pad[1, PD, :, pl.ds(lane(d, 1), HW)] = second[G2, :, pl.ds(d * HW, HW)]
    conv_local(1, PD, GT, 0)
    for r in range(DH):
        widen(1, r, got(G2, r))
    arrived(O1)
    for r in range(DH):
        put(1, PH, r, silu(got(O1, r)))
    conv_local(1, PH, G, 1)

    for side, there in by_side(False):
        @pl.when(there)
        def _():
            edge_arrived(G2, side)
            for j in range(2):
                pad[1, PD, :, pl.ds(lane(edge_q(side, j), 1), HW)] = (
                    edge[G2, side, :, pl.ds(j * HW, HW)]
                )
            edge_arrived(O1, side)
            for j in range(2):
                for h in range(H):
                    v = edge[O1, side, :, pl.ds((j * H + h) * W, W)].astype(f32)
                    pad[1, PH, :, pl.ds(lane(edge_q(side, j), h + 1), W)] = silu(v).astype(bf16)

    arrived(G1)
    for r, out in conv_finish(1, PD, GT, 0):
        put(1, PE, r, keep(1, E1, r, got(G1, r) + slope(got(O1, r)) * out))
    arrived(O2)
    for r, out in conv_finish(1, PH, G, 1):
        put(1, PU, r, silu(keep(1, R2, r, got(O2, r) - out)))

    for side, there in by_side(False):
        @pl.when(there)
        def _():
            p = -1 if side == 0 else D
            edge_arrived(G1, side)
            for h, out in conv_plane(1, PD, GT, p):
                value = near(G1, side, h) + slope(near(O1, side, h)) * out
                pad[1, PE, :, pl.ds(lane(p, h + 1), W)] = value.astype(bf16)
            edge_arrived(O2, side)
            for h, out in conv_plane(1, PH, G, p):
                value = (near(O2, side, h) - out).astype(bf16).astype(f32)
                pad[1, PU, :, pl.ds(lane(p, h + 1), W)] = silu(value).astype(bf16)

    for r, out in conv_whole(1, PE, FT):
        v = made[1, R2, :, pl.ds(r * W, W)].astype(f32)
        keep(1, E2, r, got(G2, r) + slope(v) * out)
    give_out(E2)
    for r, out in conv_whole(1, PU, F):
        keep(1, R1, r, got(O1, r) - out)
    give_out(R1)
    give_out(E1)
    give_out(R2)
    for r in range(DH):
        widen(0, r, made[1, E1, :, pl.ds(r * W, W)].astype(f32))
    wgrad(1, PU, 0)

    arrived(X2)
    for r in range(DH):
        put(1, PX, r, silu(got(X2, r)))
    for side, there in by_side(False):
        @pl.when(there)
        def _():
            edge_arrived(X2, side)
            q = -1 if side == 0 else D
            for h in range(H):
                pad[1, PX, :, pl.ds(lane(q, h + 1), W)] = silu(near(X2, side, h)).astype(bf16)
    arrived(X1)
    for r, out in conv_whole(1, PX, F):
        put(1, PY, r, silu(keep(1, Y1, r, got(X1, r) + out)))
    halo_start(1, PY)
    give_out(Y1)
    conv_local(1, PY, G, 2)
    wgrad(1, PH, 1)

    halo_arrived(1, PY)
    for r, out in conv_finish(1, PY, G, 2):
        keep(1, Y2, r, got(X2, r) + out)
    give_out(Y2)

    for j in (0, 1):
        for q in range(1, n):
            share(j, q).wait_recv()
        total = dpart[j, slab]
        for q in range(1, n):
            total += dgot[j, q]
        total *= scale
        for ab in range(9):
            for c in range(3):
                tap = total[ab] if c == 0 else pltpu.roll(total[ab], LW - c * C, 1)
                dt[j, pl.ds(3 * ab + c, cs, stride=27), :] = tap
        dw[j] = dt[j].T[:C]

    for k in range(6):
        halo_sent(0, k)
    halo_sent(1, PY)
    for j in range(2):
        for q in range(1, n):
            share(j, q).wait_send()
    for k in (Y1, Y2):
        own_out(k).wait()

    @pl.when(is_first)
    def _():
        edge_sent(second.at[X2], X2, seg, 1)

    @pl.when(is_last)
    def _():
        for k in (Y1, Y2):
            last_act(k).wait()
            last_grad(k).wait()
            edge_sent(made.at[0, k], O1 + k, seg, 1)
            edge_sent(second.at[G1 + k], G1 + k, seg, 1)

    @pl.when(has_next)
    def _():
        for k in (Y1, Y2):
            to_seg(k).wait_send()
        edge_sent(made.at[0, Y2], X2, next_seg, 0)
        for k in (R1, R2, E1, E2):
            out_prev(k).wait_recv()

    @pl.when(has_prev)
    def _():
        for k in (R1, R2, E1, E2):
            to_seg(k).wait_send()
            edge_sent(made.at[0, k], k, prev_seg, 0)
            out_prev(k).wait_send()


def write_out(*refs):
    srcs, dsts, sems = refs[:4], refs[4:8], refs[8]
    writes = [pltpu.make_async_copy(a, b, sems.at[i]) for i, (a, b) in enumerate(zip(srcs, dsts))]
    for write in writes:
        write.start()
    for write in writes:
        write.wait()


def local(segs, n, fwd_in, back_out, back_grad, batch_next, loss_grad, weights):
    _, _, C, D, H, W = fwd_in.shape
    rows = C * D * H
    cs = C // n
    f32, bf16 = jnp.float32, jnp.bfloat16
    scale = float(D * n * H * W) ** (-0.5)
    vmem = pl.BlockSpec(memory_space=pltpu.VMEM)
    hbm = pl.BlockSpec(memory_space=pltpu.HBM)
    wide = pl.cdiv(3 * C, 128) * 128
    anywhere = pl.BlockSpec(memory_space=pl.ANY)
    pair = jax.ShapeDtypeStruct((2, rows, W), bf16)
    share = jax.ShapeDtypeStruct((2, C, 27 * cs), f32)
    dma = pltpu.SemaphoreType.DMA
    fout, backs, grads, dw = pl.pallas_call(
        functools.partial(kernel, (C, D, H, W, segs, n, scale)),
        out_shape=tuple(pltpu.VMEM(x.shape, x.dtype) for x in (pair, pair, pair, share)),
        in_specs=[hbm] * 6,
        out_specs=(vmem, vmem, vmem, vmem),
        scratch_shapes=[
            pltpu.VMEM((2, rows, W), bf16),
            pltpu.VMEM((2, rows, W), bf16),
            pltpu.VMEM((2, rows, W), bf16),
            pltpu.VMEM((2, rows, W), bf16),
            pltpu.VMEM((4, rows, W), bf16),
            pltpu.VMEM((2 * C, 27 * C), bf16),
            pltpu.VMEM((27 * C, wide), f32),
            pltpu.VMEM((4, 3, 3 * C, 3 * C), bf16),
            pltpu.VMEM((2, 27 * cs, wide), f32),
            pltpu.VMEM((2, 6, C, (D + 4) * (H + 2) * W), bf16),
            pltpu.VMEM((8, rows, W), f32),
            pltpu.VMEM((6, C, D * H * W), bf16),
            pltpu.VMEM((6, 2, C, 2 * H * W), bf16),
            pltpu.VMEM((2, 6, C, D * H * W), bf16),
            pltpu.VMEM((6, rows, W), bf16),
            pltpu.VMEM((3, 3 * C, D * H * W), f32),
            pltpu.VMEM((2, 3 * C, D * H * W), bf16),
            pltpu.VMEM((2, 9 * C, 3 * C), f32),
            pltpu.VMEM((2, n, 9, cs, wide), f32),
            pltpu.VMEM((2, n, 9, cs, wide), f32),
            dma((2, 6, 2)),
            dma((2, 6, 2)),
            dma((2, 6)),
            dma((2, 6)),
            dma((2, 6, 2)),
            dma((6, 2)),
            dma((6,)),
            dma((2, n)),
            dma((2, n)),
            dma((6,)),
            pltpu.SemaphoreType.REGULAR((2,)),
        ],
        compiler_params=pltpu.CompilerParams(
            collective_id=0, has_side_effects=True, vmem_limit_bytes=48 << 20
        ),
        name="petra",
    )(
        *[
            pltpu.with_memory_space_constraint(x, pltpu.HBM)
            for x in (
                fwd_in.reshape(2, rows, W),
                back_out.reshape(2, rows, W),
                back_grad.reshape(2, rows, W),
                batch_next.reshape(2, rows, W),
                loss_grad.reshape(4, rows, W),
                weights.reshape(2 * C, 27 * C),
            )
        ]
    )
    fout, backs, grads, dw = pl.pallas_call(
        write_out,
        out_shape=(pair, pair, pair, share),
        in_specs=[vmem] * 4,
        out_specs=(hbm,) * 4,
        scratch_shapes=[dma((4,))],
        compiler_params=pltpu.CompilerParams(vmem_limit_bytes=4 << 20),
        name="write_out",
    )(fout, backs, grads, dw)
    shape = fwd_in.shape
    return fout.reshape(shape), backs.reshape(shape), grads.reshape(shape), dw[None]


def solution(mesh):
    field = P("segment", None, None, "slab", None, None)
    return jax.shard_map(
        functools.partial(local, mesh.shape["segment"], mesh.shape["slab"]),
        mesh=mesh,
        in_specs=(
            field,
            field,
            field,
            P(None, None, "slab", None, None),
            P(None, None, None, "slab", None, None),
            P("segment", None, None, None),
        ),
        out_specs=(field, field, field, P("segment", None, None, "slab")),
        check_vma=False,
    )
```

```python
import functools

import jax
import jax.numpy as jnp
from jax import lax
from jax.experimental import pallas as pl
from jax.experimental.pallas import tpu as pltpu
from jax.sharding import PartitionSpec as P

MESH = pl.DeviceIdType.MESH
F, G, FT, GT = range(4)
X1, X2, O1, O2, G1, G2 = range(6)
Y1, Y2, R1, R2, E1, E2 = range(6)
PX, PH, PD, PY, PU, PE = range(6)


def sigmoid(v):
    return 1.0 / (1.0 + jnp.exp(-v))


def silu(v):
    return v / (1.0 + jnp.exp(-v))


def slope(v):
    sig = sigmoid(v)
    return sig * (1.0 + v * (1.0 - sig))


def kernel(
    dims, fwd_hbm, bout_hbm, bgrad_hbm, nxt_hbm, loss_hbm, kern_hbm, fout, backs, grads, dw,
    fwd, bout, bgrad, nxt, loss, kern, kt, w, dt, pad, stage, second, edge, rest, made, nat, acc,
    g3, dsum, dpart, dgot, halo_s, halo_r, seg_s, seg_r, back_s, back_r, edge_s, edge_r, pass_s,
    out_s, d_s, d_r, in_s, ready_s,
):
    C, D, H, W, segs, n, scale = dims
    DH, HW = D * H, H * W
    cs = C // n
    LW = pl.cdiv(3 * C, 128) * 128
    f32, bf16 = jnp.float32, jnp.bfloat16
    seg = lax.axis_index("segment")
    slab = lax.axis_index("slab")
    has_prev, has_next = seg > 0, seg < segs - 1
    is_first, is_last = seg == 0, seg == segs - 1
    prev_seg = lax.rem(seg + segs - 1, segs)
    next_seg = lax.rem(seg + 1, segs)
    lane_no = lax.broadcasted_iota(jnp.int32, (C, W), 1)

    if n == 2:
        sides = [(None, 1 - slab, 0, 1 - slab)]
        toward = [(None, slab, 0, 1 - slab)]
    else:
        below, above = lax.rem(slab + n - 1, n), lax.rem(slab + 1, n)
        sides = [(slab > 0, 0, 0, below), (slab < n - 1, 1, 1, above)]
        toward = [(slab < n - 1, 0, 0, above), (slab > 0, 1, 1, below)]

    def over(rows, act):
        for there, side, slot, peer in rows:
            if there is None:
                act(side, slot, peer)
            else:
                pl.when(there)(functools.partial(act, side, slot, peer))

    def near_q(side):
        return side * (D + 1) - 1

    barrier = pltpu.get_barrier_semaphore()

    for k in range(1, n):
        pl.semaphore_signal(
            barrier, inc=1, device_id={"slab": lax.rem(slab + k, n)}, device_id_type=MESH
        )

    @pl.when(has_prev)
    def _():
        pl.semaphore_signal(barrier, inc=1, device_id={"segment": prev_seg}, device_id_type=MESH)

    @pl.when(has_next)
    def _():
        pl.semaphore_signal(barrier, inc=1, device_id={"segment": next_seg}, device_id_type=MESH)

    fetches = [
        pltpu.make_async_copy(src, dst, in_s.at[i])
        for i, (src, dst) in enumerate(
            [
                (bgrad_hbm, bgrad), (bout_hbm, bout), (fwd_hbm, fwd),
                (kern_hbm, kern), (nxt_hbm, nxt), (loss_hbm, loss),
            ]
        )
    ]
    for fetch in fetches:
        fetch.start()

    def lanes(at, size):
        return pl.ds(at if isinstance(at, int) else pl.multiple_of(at, W), size)

    def lane(q, hh):
        return ((q + 2) * (H + 2) + hh) * W

    zero = jnp.zeros((C, W), bf16)
    for t in range(2):
        for k in range(6):
            reach = 2 if t == 1 and k in (PH, PD) else 1
            for q in range(-reach, D + reach):
                for hh in (0, H + 1):
                    pad[t, k, :, pl.ds(lane(q, hh), W)] = zero

    for q, missing in ((-1, slab == 0), (D, slab == n - 1)):
        @pl.when(missing)
        def _():
            for t in range(2):
                for k in range(6):
                    pad[t, k, :, pl.ds(lane(q, 1), HW)] = jnp.zeros((C, HW), bf16)

    def load_stage(slot, ref, s):
        stage[slot] = ref[s].astype(f32)

    def staged(slot, r):
        return stage[slot, pl.ds(r, C, stride=DH), :]

    def prepare_weights():
        fetches[3].wait()
        wide = kern[...].astype(f32)
        kt[...] = jnp.concatenate([wide, jnp.zeros((LW - 2 * C, 27 * C), f32)], axis=0).T

        def tap(t):
            return kt[pl.ds(t, C, stride=27), :]

        for a in range(3):
            for c in range(3):
                block = jnp.concatenate([tap(9 * a + 3 * b + c) for b in range(3)], axis=0).T
                for f in range(2):
                    w[F + f, a, c * C : (c + 1) * C, :] = block[f * C : (f + 1) * C].astype(bf16)
                for f in range(2):
                    turned = jnp.concatenate(
                        [
                            tap(9 * (2 - a) + 3 * (2 - b) + 2 - c)[:, f * C : (f + 1) * C]
                            for b in range(3)
                        ],
                        axis=1,
                    )
                    w[FT + f, a, c * C : (c + 1) * C, :] = turned.astype(bf16)

    def load_pair(i, slot, ref):
        fetches[i].wait()
        for s in range(2):
            load_stage(slot + s, ref, s)

    def halo(t, k, side, slot, peer):
        if k == PU:
            src = made.at[t, R2, :, lanes((1 - side) * (D - 1) * HW, HW)]
            dst = rest.at[slot]
        else:
            src = pad.at[t, k, :, lanes(lane((1 - side) * (D - 1), 1), HW)]
            dst = pad.at[t, k, :, lanes(lane(near_q(side), 1), HW)]
        return pltpu.make_async_remote_copy(
            src_ref=src, dst_ref=dst, send_sem=halo_s.at[slot], recv_sem=halo_r.at[6 if t else k, slot],
            device_id={"slab": peer}, device_id_type=MESH,
        )

    def halo_start(t, k):
        over(toward, lambda side, slot, peer: halo(t, k, side, slot, peer).start())

    def halo_arrived(t, k):
        over(sides, lambda side, slot, peer: halo(t, k, side, slot, peer).wait_recv())

    def to_seg(k):
        return pltpu.make_async_remote_copy(
            src_ref=made.at[0, k], dst_ref=second.at[k],
            send_sem=seg_s.at[1 if k <= X2 else 0], recv_sem=seg_r.at[k],
            device_id={"segment": next_seg if k <= X2 else prev_seg}, device_id_type=MESH,
        )

    def edge_part(k, side, slot):
        planes = 2 if k in (O1, G2) else 1
        return planes, edge.at[k, slot, :, lanes((2 - planes) * (1 - side) * HW, planes * HW)]

    def edge_copy(src, k, target, which, side, slot, peer):
        planes, dst = edge_part(k, side, slot)
        return pltpu.make_async_remote_copy(
            src_ref=src.at[:, lanes((1 - side) * (D - planes) * HW, planes * HW)], dst_ref=dst,
            send_sem=edge_s.at[which, slot], recv_sem=edge_r.at[k - 1, slot],
            device_id={"segment": target, "slab": peer}, device_id_type=MESH,
        )

    def edge_start(src, k, target, which):
        over(toward, lambda *side: edge_copy(src, k, target, which, *side).start())

    def edge_arrived(k, side, slot, peer):
        edge_copy(made.at[0, k], k, seg, 0, side, slot, peer).wait_recv()

    def pass_on(k, side, slot, peer):
        if k == G1:
            src = pad.at[0, PE, :, lanes(lane(near_q(side), 1), HW)]
        else:
            src = rest.at[slot]
        return pltpu.make_async_remote_copy(
            src_ref=src, dst_ref=edge_part(k, side, slot)[1],
            send_sem=pass_s.at[slot], recv_sem=edge_r.at[k - 1, slot],
            device_id={"segment": prev_seg}, device_id_type=MESH,
        )

    def pass_start(k):
        @pl.when(has_prev)
        def _():
            over(sides, lambda *side: pass_on(k, *side).start())

    def drain(sem, src):
        pltpu.make_async_remote_copy(
            src_ref=src, dst_ref=src, send_sem=sem, recv_sem=sem,
            device_id={"slab": lax.rem(slab + 1, n)}, device_id_type=MESH,
        ).wait_send()

    def planes_of(count):
        return pad.at[0, 0, :, pl.ds(0, count * HW)]

    def out_prev(k):
        dst = backs.at[k - R1] if k < E1 else grads.at[k - E1]
        return pltpu.make_async_remote_copy(
            src_ref=nat.at[k], dst_ref=dst, send_sem=back_s.at[0], recv_sem=back_r.at[0],
            device_id={"segment": prev_seg}, device_id_type=MESH,
        )

    def own_out(k):
        return pltpu.make_async_copy(nat.at[k], fout.at[k], out_s.at[0])

    def last_act(k):
        return pltpu.make_async_copy(nat.at[k], backs.at[k], out_s.at[1])

    def last_grad(k):
        return pltpu.make_async_copy(loss.at[2 + k], grads.at[k], out_s.at[1])

    def put(t, k, r, value):
        d, h = divmod(r, H)
        put_at(t, k, d, h, value)

    def put_at(t, k, q, h, value):
        pad[t, k, :, lanes(lane(q, h + 1), W)] = value.astype(bf16)

    def tall(t, k, q):
        return jnp.concatenate([pad[t, k, :, lanes(lane(q, b), HW)] for b in range(3)], axis=0)

    def taps(t, k, m, p, which):
        total = None
        for a in which:
            part = jnp.dot(w[m, a], tall(t, k, p + a - 1), preferred_element_type=f32)
            total = part if total is None else total + part
        return total

    def inner(p):
        return [a for a in range(3) if 0 <= p + a - 1 < D]

    def conv_local(t, k, m, slot):
        for p in range(D):
            acc[slot, :, pl.ds(p * HW, HW)] = taps(t, k, m, p, inner(p))

    def rows_of(total):
        for h in range(H):
            y = total[:, h * W : (h + 1) * W]
            left = jnp.where(lane_no == 0, 0.0, pltpu.roll(y[:C], 1, 1))
            right = jnp.where(lane_no == W - 1, 0.0, pltpu.roll(y[2 * C :], W - 1, 1))
            yield h, y[C : 2 * C] + left + right

    def conv_finish(t, k, m, slot):
        def outer(side, at, peer):
            here = lanes(side * (D - 1) * HW, HW)
            acc[slot, :, here] += jnp.dot(
                w[m, 2 * side], tall(t, k, near_q(side)), preferred_element_type=f32
            )

        over(sides, outer)
        for p in range(D):
            for h, out in rows_of(acc[slot, :, pl.ds(p * HW, HW)]):
                yield p * H + h, out

    def conv_whole(t, k, m):
        for p in range(D):
            for h, out in rows_of(taps(t, k, m, p, range(3))):
                yield p * H + h, out

    def widen(j, r, v):
        at = pl.ds(r * W, W)
        g3[j, 0:C, at] = jnp.where(lane_no == W - 1, 0.0, pltpu.roll(v, W - 1, 1)).astype(bf16)
        g3[j, C : 2 * C, at] = v.astype(bf16)
        g3[j, 2 * C : 3 * C, at] = jnp.where(lane_no == 0, 0.0, pltpu.roll(v, 1, 1)).astype(bf16)

    def product(lhs, j, p):
        return lax.dot_general(
            lhs, g3[j, :, lanes(p * HW, HW)], (((1,), (1,)), ((), ())), preferred_element_type=f32
        )

    def wgrad_inner(t, k, j):
        parts = [None] * 3
        for p in range(D):
            which = inner(p)
            part = product(jnp.concatenate([tall(t, k, p + a - 1) for a in which], axis=0), j, p)
            for i, a in enumerate(which):
                block = part[i * 3 * C : (i + 1) * 3 * C]
                parts[a] = block if parts[a] is None else parts[a] + block
        for a in range(3):
            here = pl.ds(a * 3 * C, 3 * C)
            if t == 0:
                dsum[j, here] = parts[a]
            else:
                dsum[j, here] += parts[a]

    def wgrad_outer(t, k, j):
        def outer(side, slot, peer):
            at = side * 6 * C
            here = pl.ds(at if isinstance(at, int) else pl.multiple_of(at, 8), 3 * C)
            dsum[j, here] += product(tall(t, k, near_q(side)), j, side * (D - 1))

        over(sides, outer)

    def wgrad_share(j):
        total = dsum[j]
        total = jnp.concatenate([total, jnp.zeros((9 * C, LW - 3 * C), f32)], axis=1)
        for q in range(n):
            for ab in range(9):
                dpart[j, q, ab] = total[ab * C + q * cs : ab * C + (q + 1) * cs]
        for q in range(1, n):
            share(j, q).start()

    def share(j, q):
        target = lax.rem(slab + q, n)
        return pltpu.make_async_remote_copy(
            src_ref=dpart.at[j, target], dst_ref=dgot.at[j, q],
            send_sem=d_s.at[q - 1], recv_sem=d_r.at[j, q - 1],
            device_id={"slab": target}, device_id_type=MESH,
        )

    def keep(t, k, r, value):
        held = value.astype(bf16)
        made[t, k, :, pl.ds(r * W, W)] = held
        wide = held.astype(f32)
        if t == 1:
            stage[k, pl.ds(r, C, stride=DH), :] = wide
        return wide

    def hand_on(k):
        src = made.at[0, k]
        if k <= X2:
            @pl.when(has_next)
            def _():
                to_seg(k).start()
                if k == Y2:
                    edge_start(src, X2, next_seg, 1)

            @pl.when(is_last)
            def _():
                edge_start(src, O1 + k, seg, 2)
                second[O1 + k] = made[0, k]
        else:
            @pl.when(has_prev)
            def _():
                to_seg(k).start()
                if k in (O1, G2):
                    edge_start(src, k, prev_seg, 0)

    def give_out(k):
        nat[k] = stage[k].astype(bf16)
        if k < R1:
            own_out(k).start()

            @pl.when(is_last)
            def _():
                last_act(k).start()
        else:
            @pl.when(has_prev)
            def _():
                out_prev(k).start()

    def arrived(k):
        @pl.when(has_prev if k <= X2 else has_next)
        def _():
            to_seg(k).wait_recv()

    load_pair(0, G1, bgrad)
    for r in range(DH):
        put(0, PD, r, staged(G2, r))
    peers = has_prev.astype(jnp.int32) + has_next.astype(jnp.int32) + n - 1
    pl.semaphore_wait(barrier, peers)
    halo_start(0, PD)

    @pl.when(has_prev)
    def _():
        pl.semaphore_signal(
            ready_s.at[1], inc=1, device_id={"segment": prev_seg}, device_id_type=MESH
        )

    @pl.when(has_next)
    def _():
        pl.semaphore_signal(
            ready_s.at[0], inc=1, device_id={"segment": next_seg}, device_id_type=MESH
        )

    load_pair(1, O1, bout)
    for r in range(DH):
        put(0, PH, r, silu(staged(O1, r)))
    halo_start(0, PH)
    load_pair(2, X1, fwd)
    for r in range(DH):
        put(0, PX, r, silu(staged(X2, r)))
    halo_start(0, PX)
    prepare_weights()
    conv_local(0, PD, GT, 0)
    conv_local(0, PH, G, 1)
    conv_local(0, PX, F, 2)
    for r in range(DH):
        widen(1, r, staged(G2, r))
    wgrad_inner(0, PH, 1)

    fetches[4].wait()
    fetches[5].wait()

    @pl.when(is_first)
    def _():
        for s in range(2):
            load_stage(6 + s, nxt, s)
            for r in range(DH):
                second[X1 + s, :, pl.ds(r * W, W)] = staged(6 + s, r).astype(bf16)
        edge_start(second.at[X2], X2, seg, 2)

    @pl.when(is_last)
    def _():
        for s in range(2):
            last_grad(s).start()
            load_stage(6 + s, loss, s)
            for r in range(DH):
                second[G1 + s, :, pl.ds(r * W, W)] = staged(6 + s, r).astype(bf16)
            edge_start(second.at[G1 + s], G1 + s, seg, 2)

    @pl.when(has_prev)
    def _():
        pl.semaphore_wait(ready_s.at[0], 1)

    @pl.when(has_next)
    def _():
        pl.semaphore_wait(ready_s.at[1], 1)

    halo_arrived(0, PD)
    for r, out in conv_finish(0, PD, GT, 0):
        put(0, PE, r, keep(0, E1, r, staged(G1, r) + slope(staged(O1, r)) * out))
    halo_start(0, PE)
    hand_on(E1)
    conv_local(0, PE, FT, 0)
    for r in range(DH):
        widen(0, r, made[0, E1, :, pl.ds(r * W, W)].astype(f32))
    halo_arrived(0, PH)
    for r, out in conv_finish(0, PH, G, 1):
        put(0, PU, r, silu(keep(0, R2, r, staged(O2, r) - out)))
    halo_start(0, PU)
    hand_on(R2)
    conv_local(0, PU, F, 1)
    wgrad_outer(0, PH, 1)
    halo_arrived(0, PX)
    for r, out in conv_finish(0, PX, F, 2):
        put(0, PY, r, silu(keep(0, Y1, r, staged(X1, r) + out)))
    halo_start(0, PY)
    hand_on(Y1)
    conv_local(0, PY, G, 2)
    wgrad_inner(0, PU, 0)

    halo_arrived(0, PE)
    pass_start(G1)
    for r, out in conv_finish(0, PE, FT, 0):
        v = made[0, R2, :, pl.ds(r * W, W)].astype(f32)
        keep(0, E2, r, staged(G2, r) + slope(v) * out)
    hand_on(E2)
    halo_arrived(0, PU)

    def rest_in(side, slot, peer):
        for h in range(H):
            v = rest[slot, :, pl.ds(h * W, W)].astype(f32)
            put_at(0, PU, near_q(side), h, silu(v))

    over(sides, rest_in)
    for r, out in conv_finish(0, PU, F, 1):
        keep(0, R1, r, staged(O1, r) - out)
    hand_on(R1)
    pass_start(O2)
    halo_arrived(0, PY)
    for r, out in conv_finish(0, PY, G, 2):
        keep(0, Y2, r, staged(X2, r) + out)
    hand_on(Y2)
    wgrad_outer(0, PU, 0)

    def got(k, r):
        return second[k, :, pl.ds(r * W, W)].astype(f32)

    def near(k, side, slot, h):
        return edge[k, slot, :, lanes((1 - side) * HW + h * W, W)].astype(f32)

    def forward():
        arrived(X2)
        for r in range(DH):
            put(1, PX, r, silu(got(X2, r)))
        conv_local(1, PX, F, 2)
        arrived(X1)

        def edges(side, slot, peer):
            edge_arrived(X2, side, slot, peer)
            for h in range(H):
                put_at(1, PX, near_q(side), h, silu(near(X2, side, slot, h)))

        over(sides, edges)
        for r, out in conv_finish(1, PX, F, 2):
            put(1, PY, r, silu(keep(1, Y1, r, got(X1, r) + out)))
        halo_start(1, PY)
        give_out(Y1)
        conv_local(1, PY, G, 2)

    odd = lax.rem(seg, 2) == 1
    pl.when(odd)(forward)

    arrived(G2)
    for d in range(D):
        pad[1, PD, :, pl.ds(lane(d, 1), HW)] = second[G2, :, pl.ds(d * HW, HW)]
    conv_local(1, PD, GT, 0)
    for r in range(DH):
        widen(1, r, got(G2, r))
    arrived(O1)
    for r in range(DH):
        put(1, PH, r, silu(got(O1, r)))
    conv_local(1, PH, G, 1)
    wgrad_inner(1, PH, 1)

    def edges_in(side, slot, peer):
        edge_arrived(G2, side, slot, peer)
        for j in range(2):
            pad[1, PD, :, lanes(lane(side * (D + 2) - 2 + j, 1), HW)] = (
                edge[G2, slot, :, pl.ds(j * HW, HW)]
            )
        edge_arrived(O1, side, slot, peer)
        for j in range(2):
            for h in range(H):
                v = edge[O1, slot, :, pl.ds((j * H + h) * W, W)].astype(f32)
                put_at(1, PH, side * (D + 2) - 2 + j, h, silu(v))

    over(sides, edges_in)
    arrived(G1)
    for r, out in conv_finish(1, PD, GT, 0):
        put(1, PE, r, keep(1, E1, r, got(G1, r) + slope(got(O1, r)) * out))
    arrived(O2)
    for r, out in conv_finish(1, PH, G, 1):
        put(1, PU, r, silu(keep(1, R2, r, got(O2, r) - out)))

    def beyond(side, slot, peer):
        edge_arrived(G1, side, slot, peer)
        edge_arrived(O2, side, slot, peer)
        q = near_q(side)
        turned, plain = taps(1, PD, GT, q, range(3)), taps(1, PH, G, q, range(3))
        for h, out in rows_of(turned):
            value = near(G1, side, slot, h) + slope(near(O1, side, slot, h)) * out
            put_at(1, PE, q, h, value)
        for h, out in rows_of(plain):
            value = (near(O2, side, slot, h) - out).astype(bf16).astype(f32)
            put_at(1, PU, q, h, silu(value))

    over(sides, beyond)
    wgrad_outer(1, PH, 1)
    wgrad_share(1)
    for r in range(DH):
        widen(0, r, made[1, E1, :, pl.ds(r * W, W)].astype(f32))
    wgrad_inner(1, PU, 0)
    wgrad_outer(1, PU, 0)
    wgrad_share(0)
    give_out(E1)
    give_out(R2)

    pl.when(jnp.logical_not(odd))(forward)

    for r, out in conv_whole(1, PE, FT):
        v = made[1, R2, :, pl.ds(r * W, W)].astype(f32)
        keep(1, E2, r, got(G2, r) + slope(v) * out)
    give_out(E2)
    for r, out in conv_whole(1, PU, F):
        keep(1, R1, r, got(O1, r) - out)
    give_out(R1)

    halo_arrived(1, PY)
    for r, out in conv_finish(1, PY, G, 2):
        keep(1, Y2, r, got(X2, r) + out)
    give_out(Y2)

    for j in (1, 0):
        for q in range(1, n):
            share(j, q).wait_recv()
        total = dpart[j, slab]
        for q in range(1, n):
            total += dgot[j, q]
        total *= scale
        for ab in range(9):
            for c in range(3):
                tap = total[ab] if c == 0 else pltpu.roll(total[ab], LW - c * C, 1)
                dt[j, pl.ds(3 * ab + c, cs, stride=27), :] = tap
        dw[j] = dt[j].T[:C]

    over(toward, lambda side, slot, peer: drain(halo_s.at[slot], planes_of(7)))
    for q in range(1, n):
        drain(d_s.at[q - 1], dpart.at[:, 0])
    pltpu.make_async_copy(nat.at[pl.ds(Y1, 2)], fout, out_s.at[0]).wait()

    @pl.when(is_first)
    def _():
        over(toward, lambda side, slot, peer: drain(edge_s.at[2, slot], planes_of(1)))

    @pl.when(is_last)
    def _():
        pltpu.make_async_copy(nat.at[pl.ds(0, 4)], nat.at[pl.ds(0, 4)], out_s.at[1]).wait()
        over(toward, lambda side, slot, peer: drain(edge_s.at[2, slot], planes_of(6)))

    @pl.when(has_next)
    def _():
        drain(seg_s.at[1], made.at[0, pl.ds(0, 2)])
        over(toward, lambda side, slot, peer: drain(edge_s.at[1, slot], planes_of(1)))
        drain(back_r.at[0], nat.at[pl.ds(R1, 4)])

    @pl.when(has_prev)
    def _():
        drain(seg_s.at[0], made.at[0, pl.ds(0, 4)])
        over(toward, lambda side, slot, peer: drain(edge_s.at[0, slot], planes_of(4)))
        over(sides, lambda side, slot, peer: drain(pass_s.at[slot], planes_of(2)))
        drain(back_s.at[0], nat.at[pl.ds(R1, 4)])


def write_out(*refs):
    srcs, dsts, sems = refs[:4], refs[4:8], refs[8]
    writes = [pltpu.make_async_copy(a, b, sems.at[i]) for i, (a, b) in enumerate(zip(srcs, dsts))]
    for write in writes:
        write.start()
    for write in writes:
        write.wait()


def local(segs, n, fwd_in, back_out, back_grad, batch_next, loss_grad, weights):
    _, _, C, D, H, W = fwd_in.shape
    rows = C * D * H
    cs = C // n
    ends = 1 if n == 2 else 2
    f32, bf16 = jnp.float32, jnp.bfloat16
    scale = float(D * n * H * W) ** (-0.5)
    vmem = pl.BlockSpec(memory_space=pltpu.VMEM)
    hbm = pl.BlockSpec(memory_space=pltpu.HBM)
    wide = pl.cdiv(3 * C, 128) * 128
    anywhere = pl.BlockSpec(memory_space=pl.ANY)
    pair = jax.ShapeDtypeStruct((2, rows, W), bf16)
    share = jax.ShapeDtypeStruct((2, C, 27 * cs), f32)
    dma = pltpu.SemaphoreType.DMA
    fout, backs, grads, dw = pl.pallas_call(
        functools.partial(kernel, (C, D, H, W, segs, n, scale)),
        out_shape=tuple(pltpu.VMEM(x.shape, x.dtype) for x in (pair, pair, pair, share)),
        in_specs=[hbm] * 6,
        out_specs=(vmem, vmem, vmem, vmem),
        scratch_shapes=[
            pltpu.VMEM((2, rows, W), bf16),
            pltpu.VMEM((2, rows, W), bf16),
            pltpu.VMEM((2, rows, W), bf16),
            pltpu.VMEM((2, rows, W), bf16),
            pltpu.VMEM((4, rows, W), bf16),
            pltpu.VMEM((2 * C, 27 * C), bf16),
            pltpu.VMEM((27 * C, wide), f32),
            pltpu.VMEM((4, 3, 3 * C, 3 * C), bf16),
            pltpu.VMEM((2, 27 * cs, wide), f32),
            pltpu.VMEM((2, 6, C, (D + 4) * (H + 2) * W), bf16),
            pltpu.VMEM((8, rows, W), f32),
            pltpu.VMEM((6, C, D * H * W), bf16),
            pltpu.VMEM((6, ends, C, 2 * H * W), bf16),
            pltpu.VMEM((ends, C, H * W), bf16),
            pltpu.VMEM((2, 6, C, D * H * W), bf16),
            pltpu.VMEM((6, rows, W), bf16),
            pltpu.VMEM((3, 3 * C, D * H * W), f32),
            pltpu.VMEM((2, 3 * C, D * H * W), bf16),
            pltpu.VMEM((2, 9 * C, 3 * C), f32),
            pltpu.VMEM((2, n, 9, cs, wide), f32),
            pltpu.VMEM((2, n, 9, cs, wide), f32),
            dma((ends,)),
            dma((7, ends)),
            dma((2,)),
            dma((6,)),
            dma((1,)),
            dma((1,)),
            dma((3, ends)),
            dma((5, ends)),
            dma((ends,)),
            dma((2,)),
            dma((n - 1,)),
            dma((2, n - 1)),
            dma((6,)),
            pltpu.SemaphoreType.REGULAR((2,)),
        ],
        compiler_params=pltpu.CompilerParams(
            collective_id=0, has_side_effects=True, vmem_limit_bytes=48 << 20
        ),
        name="petra",
    )(
        *[
            pltpu.with_memory_space_constraint(x, pltpu.HBM)
            for x in (
                fwd_in.reshape(2, rows, W),
                back_out.reshape(2, rows, W),
                back_grad.reshape(2, rows, W),
                batch_next.reshape(2, rows, W),
                loss_grad.reshape(4, rows, W),
                weights.reshape(2 * C, 27 * C),
            )
        ]
    )
    fout, backs, grads, dw = pl.pallas_call(
        write_out,
        out_shape=(pair, pair, pair, share),
        in_specs=[vmem] * 4,
        out_specs=(hbm,) * 4,
        scratch_shapes=[dma((4,))],
        compiler_params=pltpu.CompilerParams(vmem_limit_bytes=4 << 20),
        name="write_out",
    )(fout, backs, grads, dw)
    shape = fwd_in.shape
    return fout.reshape(shape), backs.reshape(shape), grads.reshape(shape), dw[None]


def solution(mesh):
    field = P("segment", None, None, "slab", None, None)
    return jax.shard_map(
        functools.partial(local, mesh.shape["segment"], mesh.shape["slab"]),
        mesh=mesh,
        in_specs=(
            field,
            field,
            field,
            P(None, None, "slab", None, None),
            P(None, None, None, "slab", None, None),
            P("segment", None, None, None),
        ),
        out_specs=(field, field, field, P("segment", None, None, "slab")),
        check_vma=False,
    )
```

```python
import functools

import jax
import jax.numpy as jnp
from jax import lax
from jax.experimental import pallas as pl
from jax.experimental.pallas import tpu as pltpu
from jax.sharding import PartitionSpec as P

MESH = pl.DeviceIdType.MESH
F, G, FT, GT = range(4)
X1, X2, O1, O2, G1, G2 = range(6)
Y1, Y2, R1, R2, E1, E2 = range(6)
PX, PH, PD, PY, PU, PE = range(6)


def sigmoid(v):
    return 1.0 / (1.0 + jnp.exp(-v))


def silu(v):
    return v / (1.0 + jnp.exp(-v))


def slope(v):
    sig = sigmoid(v)
    return sig * (1.0 + v * (1.0 - sig))


def kernel(
    dims, fwd_hbm, bout_hbm, bgrad_hbm, nxt_hbm, loss_hbm, kern_hbm, fout, backs, grads, dw,
    fwd, bout, bgrad, nxt, loss, kern, kt, w, dt, pad, stage, second, edge, rest, made, nat, acc,
    g3, dsum, dpart, dgot, halo_s, halo_r, seg_s, seg_r, back_s, back_r, edge_s, edge_r, pass_s,
    out_s, d_s, d_r, in_s, ready_s,
):
    C, D, H, W, segs, n, scale = dims
    DH, HW = D * H, H * W
    cs = C // n
    LW = pl.cdiv(3 * C, 128) * 128
    f32, bf16 = jnp.float32, jnp.bfloat16
    seg = lax.axis_index("segment")
    slab = lax.axis_index("slab")
    has_prev, has_next = seg > 0, seg < segs - 1
    is_first, is_last = seg == 0, seg == segs - 1
    prev_seg = lax.rem(seg + segs - 1, segs)
    next_seg = lax.rem(seg + 1, segs)
    lane_no = lax.broadcasted_iota(jnp.int32, (C, W), 1)

    if n == 2:
        sides = [(None, 1 - slab, 0, 1 - slab)]
        toward = [(None, slab, 0, 1 - slab)]
    else:
        below, above = lax.rem(slab + n - 1, n), lax.rem(slab + 1, n)
        sides = [(slab > 0, 0, 0, below), (slab < n - 1, 1, 1, above)]
        toward = [(slab < n - 1, 0, 0, above), (slab > 0, 1, 1, below)]

    def over(rows, act):
        for there, side, slot, peer in rows:
            if there is None:
                act(side, slot, peer)
            else:
                pl.when(there)(functools.partial(act, side, slot, peer))

    def near_q(side):
        return side * (D + 1) - 1

    barrier = pltpu.get_barrier_semaphore()

    for k in range(1, n):
        pl.semaphore_signal(
            barrier, inc=1, device_id={"slab": lax.rem(slab + k, n)}, device_id_type=MESH
        )

    @pl.when(has_prev)
    def _():
        pl.semaphore_signal(barrier, inc=1, device_id={"segment": prev_seg}, device_id_type=MESH)

    @pl.when(has_next)
    def _():
        pl.semaphore_signal(barrier, inc=1, device_id={"segment": next_seg}, device_id_type=MESH)

    fetches = [
        pltpu.make_async_copy(src, dst, in_s.at[i])
        for i, (src, dst) in enumerate(
            [
                (bgrad_hbm, bgrad), (bout_hbm, bout), (fwd_hbm, fwd),
                (kern_hbm, kern), (nxt_hbm, nxt), (loss_hbm, loss),
            ]
        )
    ]
    for fetch in fetches:
        fetch.start()

    def lanes(at, size):
        return pl.ds(at if isinstance(at, int) else pl.multiple_of(at, W), size)

    def lane(q, hh):
        return ((q + 2) * (H + 2) + hh) * W

    zero = jnp.zeros((C, W), bf16)
    for t in range(2):
        for k in range(6):
            reach = 2 if t == 1 and k in (PH, PD) else 1
            for q in range(-reach, D + reach):
                for hh in (0, H + 1):
                    pad[t, k, :, pl.ds(lane(q, hh), W)] = zero

    for q, missing in ((-1, slab == 0), (D, slab == n - 1)):
        @pl.when(missing)
        def _():
            for t in range(2):
                for k in range(6):
                    pad[t, k, :, pl.ds(lane(q, 1), HW)] = jnp.zeros((C, HW), bf16)

    def load_stage(slot, ref, s):
        stage[slot] = ref[s].astype(f32)

    def staged(slot, r):
        return stage[slot, pl.ds(r, C, stride=DH), :]

    def prepare_weights():
        fetches[3].wait()
        wide = kern[...].astype(f32)
        kt[...] = jnp.concatenate([wide, jnp.zeros((LW - 2 * C, 27 * C), f32)], axis=0).T

        def tap(t):
            return kt[pl.ds(t, C, stride=27), :]

        for a in range(3):
            for c in range(3):
                block = jnp.concatenate([tap(9 * a + 3 * b + c) for b in range(3)], axis=0).T
                for f in range(2):
                    w[F + f, a, c * C : (c + 1) * C, :] = block[f * C : (f + 1) * C].astype(bf16)
                for f in range(2):
                    turned = jnp.concatenate(
                        [
                            tap(9 * (2 - a) + 3 * (2 - b) + 2 - c)[:, f * C : (f + 1) * C]
                            for b in range(3)
                        ],
                        axis=1,
                    )
                    w[FT + f, a, c * C : (c + 1) * C, :] = turned.astype(bf16)

    def load_pair(i, slot, ref):
        fetches[i].wait()
        for s in range(2):
            load_stage(slot + s, ref, s)

    def halo(t, k, side, slot, peer):
        if k == PU:
            src = made.at[t, R2, :, lanes((1 - side) * (D - 1) * HW, HW)]
            dst = rest.at[slot]
        else:
            src = pad.at[t, k, :, lanes(lane((1 - side) * (D - 1), 1), HW)]
            dst = pad.at[t, k, :, lanes(lane(near_q(side), 1), HW)]
        return pltpu.make_async_remote_copy(
            src_ref=src, dst_ref=dst, send_sem=halo_s.at[slot], recv_sem=halo_r.at[6 if t else k, slot],
            device_id={"slab": peer}, device_id_type=MESH,
        )

    def halo_start(t, k):
        over(toward, lambda side, slot, peer: halo(t, k, side, slot, peer).start())

    def halo_arrived(t, k):
        over(sides, lambda side, slot, peer: halo(t, k, side, slot, peer).wait_recv())

    def to_seg(k):
        return pltpu.make_async_remote_copy(
            src_ref=made.at[0, k], dst_ref=second.at[k],
            send_sem=seg_s.at[1 if k <= X2 else 0], recv_sem=seg_r.at[k],
            device_id={"segment": next_seg if k <= X2 else prev_seg}, device_id_type=MESH,
        )

    def edge_at(k, far, side, slot):
        return edge.at[k, slot, :, lanes((side if far else 1 - side) * HW, HW)]

    def edge_copy(src, k, far, target, which, side, slot, peer):
        plane = (1 - side) * (D - 2) + side if far else (1 - side) * (D - 1)
        return pltpu.make_async_remote_copy(
            src_ref=src.at[:, lanes(plane * HW, HW)], dst_ref=edge_at(k, far, side, slot),
            send_sem=edge_s.at[which, slot], recv_sem=edge_r.at[k // 2 + 4 if far else k - 1, slot],
            device_id={"segment": target, "slab": peer}, device_id_type=MESH,
        )

    def edge_start(src, k, far, target, which):
        over(toward, lambda *side: edge_copy(src, k, far, target, which, *side).start())

    def edge_arrived(k, far, *side):
        edge_copy(made.at[0, k], k, far, seg, 0, *side).wait_recv()

    def pass_on(k, side, slot, peer):
        if k == G1:
            src = pad.at[0, PE, :, lanes(lane(near_q(side), 1), HW)]
        else:
            src = rest.at[slot]
        return pltpu.make_async_remote_copy(
            src_ref=src, dst_ref=edge_at(k, False, side, slot),
            send_sem=pass_s.at[slot], recv_sem=edge_r.at[k - 1, slot],
            device_id={"segment": prev_seg}, device_id_type=MESH,
        )

    def drain(sem, src):
        pltpu.make_async_remote_copy(
            src_ref=src, dst_ref=src, send_sem=sem, recv_sem=sem,
            device_id={"slab": lax.rem(slab + 1, n)}, device_id_type=MESH,
        ).wait_send()

    def planes_of(count):
        return pad.at[0, 0, :, pl.ds(0, count * HW)]

    def out_prev(k):
        dst = backs.at[k - R1] if k < E1 else grads.at[k - E1]
        return pltpu.make_async_remote_copy(
            src_ref=nat.at[k], dst_ref=dst, send_sem=back_s.at[0], recv_sem=back_r.at[0],
            device_id={"segment": prev_seg}, device_id_type=MESH,
        )

    def own_out(k):
        return pltpu.make_async_copy(nat.at[k], fout.at[k], out_s.at[0])

    def last_act(k):
        return pltpu.make_async_copy(nat.at[k], backs.at[k], out_s.at[1])

    def last_grad(k):
        return pltpu.make_async_copy(loss.at[2 + k], grads.at[k], out_s.at[1])

    def put(t, k, r, value):
        d, h = divmod(r, H)
        put_at(t, k, d, h, value)

    def put_at(t, k, q, h, value):
        pad[t, k, :, lanes(lane(q, h + 1), W)] = value.astype(bf16)

    def tall(t, k, q):
        return jnp.concatenate([pad[t, k, :, lanes(lane(q, b), HW)] for b in range(3)], axis=0)

    def taps(t, k, m, p, which):
        total = None
        for a in which:
            part = jnp.dot(w[m, a], tall(t, k, p + a - 1), preferred_element_type=f32)
            total = part if total is None else total + part
        return total

    def inner(p):
        return [a for a in range(3) if 0 <= p + a - 1 < D]

    def conv_local(t, k, m, slot):
        for p in range(D):
            acc[slot, :, pl.ds(p * HW, HW)] = taps(t, k, m, p, inner(p))

    def rows_of(total):
        for h in range(H):
            y = total[:, h * W : (h + 1) * W]
            left = jnp.where(lane_no == 0, 0.0, pltpu.roll(y[:C], 1, 1))
            right = jnp.where(lane_no == W - 1, 0.0, pltpu.roll(y[2 * C :], W - 1, 1))
            yield h, y[C : 2 * C] + left + right

    def conv_finish(t, k, m, slot):
        def outer(side, at, peer):
            here = lanes(side * (D - 1) * HW, HW)
            acc[slot, :, here] += jnp.dot(
                w[m, 2 * side], tall(t, k, near_q(side)), preferred_element_type=f32
            )

        over(sides, outer)
        for p in range(D):
            for h, out in rows_of(acc[slot, :, pl.ds(p * HW, HW)]):
                yield p * H + h, out

    def conv_whole(t, k, m):
        for p in range(D):
            for h, out in rows_of(taps(t, k, m, p, range(3))):
                yield p * H + h, out

    def widen(j, r, v):
        at = pl.ds(r * W, W)
        g3[j, 0:C, at] = jnp.where(lane_no == W - 1, 0.0, pltpu.roll(v, W - 1, 1)).astype(bf16)
        g3[j, C : 2 * C, at] = v.astype(bf16)
        g3[j, 2 * C : 3 * C, at] = jnp.where(lane_no == 0, 0.0, pltpu.roll(v, 1, 1)).astype(bf16)

    def product(lhs, j, p):
        return lax.dot_general(
            lhs, g3[j, :, lanes(p * HW, HW)], (((1,), (1,)), ((), ())), preferred_element_type=f32
        )

    def wgrad_inner(t, k, j):
        parts = [None] * 3
        for p in range(D):
            which = inner(p)
            part = product(jnp.concatenate([tall(t, k, p + a - 1) for a in which], axis=0), j, p)
            for i, a in enumerate(which):
                block = part[i * 3 * C : (i + 1) * 3 * C]
                parts[a] = block if parts[a] is None else parts[a] + block
        for a in range(3):
            here = pl.ds(a * 3 * C, 3 * C)
            if t == 0:
                dsum[j, here] = parts[a]
            else:
                dsum[j, here] += parts[a]

    def wgrad_outer(t, k, j):
        def outer(side, slot, peer):
            at = side * 6 * C
            here = pl.ds(at if isinstance(at, int) else pl.multiple_of(at, 8), 3 * C)
            dsum[j, here] += product(tall(t, k, near_q(side)), j, side * (D - 1))

        over(sides, outer)

    def wgrad_share(j):
        total = dsum[j]
        total = jnp.concatenate([total, jnp.zeros((9 * C, LW - 3 * C), f32)], axis=1)
        for q in range(n):
            for ab in range(9):
                dpart[j, q, ab] = total[ab * C + q * cs : ab * C + (q + 1) * cs]
        for q in range(1, n):
            share(j, q).start()

    def share(j, q):
        target = lax.rem(slab + q, n)
        return pltpu.make_async_remote_copy(
            src_ref=dpart.at[j, target], dst_ref=dgot.at[j, q],
            send_sem=d_s.at[q - 1], recv_sem=d_r.at[j, q - 1],
            device_id={"slab": target}, device_id_type=MESH,
        )

    def keep(t, k, r, value):
        held = value.astype(bf16)
        made[t, k, :, pl.ds(r * W, W)] = held
        wide = held.astype(f32)
        if t == 1:
            stage[k, pl.ds(r, C, stride=DH), :] = wide
        return wide

    def hand_on(k):
        src = made.at[0, k]
        if k <= X2:
            @pl.when(has_next)
            def _():
                if k == Y2:
                    edge_start(src, X2, False, next_seg, 1)
                to_seg(k).start()

            @pl.when(is_last)
            def _():
                edge_start(src, O1 + k, False, seg, 2)
                if k == Y1:
                    edge_start(src, O1, True, seg, 2)
                second[O1 + k] = made[0, k]
        else:
            @pl.when(has_prev)
            def _():
                to_seg(k).start()
                if k in (O1, G2):
                    edge_start(src, k, False, prev_seg, 0)

    def hand_on_far():
        @pl.when(has_prev)
        def _():
            for k in (G2, O1):
                edge_start(made.at[0, k], k, True, prev_seg, 0)
            for k in (G1, O2):
                over(sides, lambda *side: pass_on(k, *side).start())

    def give_out(k):
        nat[k] = stage[k].astype(bf16)
        if k < R1:
            own_out(k).start()

            @pl.when(is_last)
            def _():
                last_act(k).start()
        else:
            @pl.when(has_prev)
            def _():
                out_prev(k).start()

    def arrived(k):
        @pl.when(has_prev if k <= X2 else has_next)
        def _():
            to_seg(k).wait_recv()

    load_pair(0, G1, bgrad)
    for r in range(DH):
        put(0, PD, r, staged(G2, r))
    peers = has_prev.astype(jnp.int32) + has_next.astype(jnp.int32) + n - 1
    pl.semaphore_wait(barrier, peers)
    halo_start(0, PD)

    @pl.when(has_prev)
    def _():
        pl.semaphore_signal(
            ready_s.at[1], inc=1, device_id={"segment": prev_seg}, device_id_type=MESH
        )

    @pl.when(has_next)
    def _():
        pl.semaphore_signal(
            ready_s.at[0], inc=1, device_id={"segment": next_seg}, device_id_type=MESH
        )

    load_pair(1, O1, bout)
    for r in range(DH):
        put(0, PH, r, silu(staged(O1, r)))
    halo_start(0, PH)
    load_pair(2, X1, fwd)
    for r in range(DH):
        put(0, PX, r, silu(staged(X2, r)))
    halo_start(0, PX)
    prepare_weights()
    conv_local(0, PD, GT, 0)
    conv_local(0, PH, G, 1)
    conv_local(0, PX, F, 2)
    for r in range(DH):
        widen(1, r, staged(G2, r))
    wgrad_inner(0, PH, 1)

    fetches[4].wait()
    fetches[5].wait()

    @pl.when(is_first)
    def _():
        for s in range(2):
            load_stage(6 + s, nxt, s)
            for r in range(DH):
                second[X1 + s, :, pl.ds(r * W, W)] = staged(6 + s, r).astype(bf16)
        edge_start(second.at[X2], X2, False, seg, 2)

    @pl.when(is_last)
    def _():
        for s in range(2):
            last_grad(s).start()
            load_stage(6 + s, loss, s)
            for r in range(DH):
                second[G1 + s, :, pl.ds(r * W, W)] = staged(6 + s, r).astype(bf16)
            edge_start(second.at[G1 + s], G1 + s, False, seg, 2)
        edge_start(second.at[G2], G2, True, seg, 2)

    @pl.when(has_prev)
    def _():
        pl.semaphore_wait(ready_s.at[0], 1)

    @pl.when(has_next)
    def _():
        pl.semaphore_wait(ready_s.at[1], 1)

    halo_arrived(0, PD)
    for r, out in conv_finish(0, PD, GT, 0):
        put(0, PE, r, keep(0, E1, r, staged(G1, r) + slope(staged(O1, r)) * out))
    halo_start(0, PE)
    hand_on(E1)
    conv_local(0, PE, FT, 0)
    for r in range(DH):
        widen(0, r, made[0, E1, :, pl.ds(r * W, W)].astype(f32))
    halo_arrived(0, PH)
    for r, out in conv_finish(0, PH, G, 1):
        put(0, PU, r, silu(keep(0, R2, r, staged(O2, r) - out)))
    halo_start(0, PU)
    hand_on(R2)
    conv_local(0, PU, F, 1)
    wgrad_outer(0, PH, 1)
    halo_arrived(0, PX)
    for r, out in conv_finish(0, PX, F, 2):
        put(0, PY, r, silu(keep(0, Y1, r, staged(X1, r) + out)))
    halo_start(0, PY)
    hand_on(Y1)
    conv_local(0, PY, G, 2)
    wgrad_inner(0, PU, 0)

    halo_arrived(0, PE)
    for r, out in conv_finish(0, PE, FT, 0):
        v = made[0, R2, :, pl.ds(r * W, W)].astype(f32)
        keep(0, E2, r, staged(G2, r) + slope(v) * out)
    hand_on(E2)
    halo_arrived(0, PU)

    def rest_in(side, slot, peer):
        for h in range(H):
            v = rest[slot, :, pl.ds(h * W, W)].astype(f32)
            put_at(0, PU, near_q(side), h, silu(v))

    over(sides, rest_in)
    for r, out in conv_finish(0, PU, F, 1):
        keep(0, R1, r, staged(O1, r) - out)
    hand_on(R1)
    halo_arrived(0, PY)
    for r, out in conv_finish(0, PY, G, 2):
        keep(0, Y2, r, staged(X2, r) + out)
    hand_on(Y2)
    hand_on_far()
    wgrad_outer(0, PU, 0)

    def got(k, r):
        return second[k, :, pl.ds(r * W, W)].astype(f32)

    def near(k, side, slot, h):
        return edge[k, slot, :, lanes((1 - side) * HW + h * W, W)].astype(f32)

    def forward():
        arrived(X2)
        for r in range(DH):
            put(1, PX, r, silu(got(X2, r)))
        conv_local(1, PX, F, 2)
        arrived(X1)

        def edges(side, slot, peer):
            edge_arrived(X2, False, side, slot, peer)
            for h in range(H):
                put_at(1, PX, near_q(side), h, silu(near(X2, side, slot, h)))

        over(sides, edges)
        for r, out in conv_finish(1, PX, F, 2):
            put(1, PY, r, silu(keep(1, Y1, r, got(X1, r) + out)))
        halo_start(1, PY)
        give_out(Y1)
        conv_local(1, PY, G, 2)

    odd = lax.rem(seg, 2) == 1
    pl.when(odd)(forward)

    arrived(G2)
    for d in range(D):
        pad[1, PD, :, pl.ds(lane(d, 1), HW)] = second[G2, :, pl.ds(d * HW, HW)]
    conv_local(1, PD, GT, 0)
    for r in range(DH):
        widen(1, r, got(G2, r))
    arrived(O1)
    for r in range(DH):
        put(1, PH, r, silu(got(O1, r)))
    conv_local(1, PH, G, 1)
    wgrad_inner(1, PH, 1)

    def edges_in(far, side, slot, peer):
        q = near_q(side) + (2 * side - 1 if far else 0)
        at = (side if far else 1 - side) * HW
        edge_arrived(G2, far, side, slot, peer)
        pad[1, PD, :, lanes(lane(q, 1), HW)] = edge[G2, slot, :, lanes(at, HW)]
        edge_arrived(O1, far, side, slot, peer)
        for h in range(H):
            put_at(1, PH, q, h, silu(edge[O1, slot, :, lanes(at + h * W, W)].astype(f32)))

    over(sides, functools.partial(edges_in, False))
    arrived(G1)
    for r, out in conv_finish(1, PD, GT, 0):
        put(1, PE, r, keep(1, E1, r, got(G1, r) + slope(got(O1, r)) * out))
    arrived(O2)
    for r, out in conv_finish(1, PH, G, 1):
        put(1, PU, r, silu(keep(1, R2, r, got(O2, r) - out)))
    wgrad_outer(1, PH, 1)
    wgrad_share(1)
    for r in range(DH):
        widen(0, r, made[1, E1, :, pl.ds(r * W, W)].astype(f32))
    wgrad_inner(1, PU, 0)

    def beyond(side, slot, peer):
        edges_in(True, side, slot, peer)
        edge_arrived(G1, False, side, slot, peer)
        edge_arrived(O2, False, side, slot, peer)
        q = near_q(side)
        turned, plain = taps(1, PD, GT, q, range(3)), taps(1, PH, G, q, range(3))
        for h, out in rows_of(turned):
            value = near(G1, side, slot, h) + slope(near(O1, side, slot, h)) * out
            put_at(1, PE, q, h, value)
        for h, out in rows_of(plain):
            value = (near(O2, side, slot, h) - out).astype(bf16).astype(f32)
            put_at(1, PU, q, h, silu(value))

    over(sides, beyond)
    wgrad_outer(1, PU, 0)
    wgrad_share(0)
    give_out(E1)
    give_out(R2)

    pl.when(jnp.logical_not(odd))(forward)

    for r, out in conv_whole(1, PE, FT):
        v = made[1, R2, :, pl.ds(r * W, W)].astype(f32)
        keep(1, E2, r, got(G2, r) + slope(v) * out)
    give_out(E2)
    for r, out in conv_whole(1, PU, F):
        keep(1, R1, r, got(O1, r) - out)
    give_out(R1)

    halo_arrived(1, PY)
    for r, out in conv_finish(1, PY, G, 2):
        keep(1, Y2, r, got(X2, r) + out)
    give_out(Y2)

    for j in (1, 0):
        for q in range(1, n):
            share(j, q).wait_recv()
        total = dpart[j, slab]
        for q in range(1, n):
            total += dgot[j, q]
        total *= scale
        for ab in range(9):
            for c in range(3):
                tap = total[ab] if c == 0 else pltpu.roll(total[ab], LW - c * C, 1)
                dt[j, pl.ds(3 * ab + c, cs, stride=27), :] = tap
        dw[j] = dt[j].T[:C]

    over(toward, lambda side, slot, peer: drain(halo_s.at[slot], planes_of(7)))
    for q in range(1, n):
        drain(d_s.at[q - 1], dpart.at[:, 0])
    pltpu.make_async_copy(nat.at[pl.ds(Y1, 2)], fout, out_s.at[0]).wait()

    @pl.when(is_first)
    def _():
        over(toward, lambda side, slot, peer: drain(edge_s.at[2, slot], planes_of(1)))

    @pl.when(is_last)
    def _():
        pltpu.make_async_copy(nat.at[pl.ds(0, 4)], nat.at[pl.ds(0, 4)], out_s.at[1]).wait()
        over(toward, lambda side, slot, peer: drain(edge_s.at[2, slot], planes_of(6)))

    @pl.when(has_next)
    def _():
        drain(seg_s.at[1], made.at[0, pl.ds(0, 2)])
        over(toward, lambda side, slot, peer: drain(edge_s.at[1, slot], planes_of(1)))
        drain(back_r.at[0], nat.at[pl.ds(R1, 4)])

    @pl.when(has_prev)
    def _():
        drain(seg_s.at[0], made.at[0, pl.ds(0, 4)])
        over(toward, lambda side, slot, peer: drain(edge_s.at[0, slot], planes_of(4)))
        over(sides, lambda side, slot, peer: drain(pass_s.at[slot], planes_of(2)))
        drain(back_s.at[0], nat.at[pl.ds(R1, 4)])


def write_out(*refs):
    srcs, dsts, sems = refs[:4], refs[4:8], refs[8]
    writes = [pltpu.make_async_copy(a, b, sems.at[i]) for i, (a, b) in enumerate(zip(srcs, dsts))]
    for write in writes:
        write.start()
    for write in writes:
        write.wait()


def local(segs, n, fwd_in, back_out, back_grad, batch_next, loss_grad, weights):
    _, _, C, D, H, W = fwd_in.shape
    rows = C * D * H
    cs = C // n
    ends = 1 if n == 2 else 2
    f32, bf16 = jnp.float32, jnp.bfloat16
    scale = float(D * n * H * W) ** (-0.5)
    vmem = pl.BlockSpec(memory_space=pltpu.VMEM)
    hbm = pl.BlockSpec(memory_space=pltpu.HBM)
    wide = pl.cdiv(3 * C, 128) * 128
    anywhere = pl.BlockSpec(memory_space=pl.ANY)
    pair = jax.ShapeDtypeStruct((2, rows, W), bf16)
    share = jax.ShapeDtypeStruct((2, C, 27 * cs), f32)
    dma = pltpu.SemaphoreType.DMA
    fout, backs, grads, dw = pl.pallas_call(
        functools.partial(kernel, (C, D, H, W, segs, n, scale)),
        out_shape=tuple(pltpu.VMEM(x.shape, x.dtype) for x in (pair, pair, pair, share)),
        in_specs=[hbm] * 6,
        out_specs=(vmem, vmem, vmem, vmem),
        scratch_shapes=[
            pltpu.VMEM((2, rows, W), bf16),
            pltpu.VMEM((2, rows, W), bf16),
            pltpu.VMEM((2, rows, W), bf16),
            pltpu.VMEM((2, rows, W), bf16),
            pltpu.VMEM((4, rows, W), bf16),
            pltpu.VMEM((2 * C, 27 * C), bf16),
            pltpu.VMEM((27 * C, wide), f32),
            pltpu.VMEM((4, 3, 3 * C, 3 * C), bf16),
            pltpu.VMEM((2, 27 * cs, wide), f32),
            pltpu.VMEM((2, 6, C, (D + 4) * (H + 2) * W), bf16),
            pltpu.VMEM((8, rows, W), f32),
            pltpu.VMEM((6, C, D * H * W), bf16),
            pltpu.VMEM((6, ends, C, 2 * H * W), bf16),
            pltpu.VMEM((ends, C, H * W), bf16),
            pltpu.VMEM((2, 6, C, D * H * W), bf16),
            pltpu.VMEM((6, rows, W), bf16),
            pltpu.VMEM((3, 3 * C, D * H * W), f32),
            pltpu.VMEM((2, 3 * C, D * H * W), bf16),
            pltpu.VMEM((2, 9 * C, 3 * C), f32),
            pltpu.VMEM((2, n, 9, cs, wide), f32),
            pltpu.VMEM((2, n, 9, cs, wide), f32),
            dma((ends,)),
            dma((7, ends)),
            dma((2,)),
            dma((6,)),
            dma((1,)),
            dma((1,)),
            dma((3, ends)),
            dma((7, ends)),
            dma((ends,)),
            dma((2,)),
            dma((n - 1,)),
            dma((2, n - 1)),
            dma((6,)),
            pltpu.SemaphoreType.REGULAR((2,)),
        ],
        compiler_params=pltpu.CompilerParams(
            collective_id=0, has_side_effects=True, vmem_limit_bytes=48 << 20
        ),
        name="petra",
    )(
        *[
            pltpu.with_memory_space_constraint(x, pltpu.HBM)
            for x in (
                fwd_in.reshape(2, rows, W),
                back_out.reshape(2, rows, W),
                back_grad.reshape(2, rows, W),
                batch_next.reshape(2, rows, W),
                loss_grad.reshape(4, rows, W),
                weights.reshape(2 * C, 27 * C),
            )
        ]
    )
    fout, backs, grads, dw = pl.pallas_call(
        write_out,
        out_shape=(pair, pair, pair, share),
        in_specs=[vmem] * 4,
        out_specs=(hbm,) * 4,
        scratch_shapes=[dma((4,))],
        compiler_params=pltpu.CompilerParams(vmem_limit_bytes=4 << 20),
        name="write_out",
    )(fout, backs, grads, dw)
    shape = fwd_in.shape
    return fout.reshape(shape), backs.reshape(shape), grads.reshape(shape), dw[None]


def solution(mesh):
    field = P("segment", None, None, "slab", None, None)
    return jax.shard_map(
        functools.partial(local, mesh.shape["segment"], mesh.shape["slab"]),
        mesh=mesh,
        in_specs=(
            field,
            field,
            field,
            P(None, None, "slab", None, None),
            P(None, None, None, "slab", None, None),
            P("segment", None, None, None),
        ),
        out_specs=(field, field, field, P("segment", None, None, "slab")),
        check_vma=False,
    )
```

```python
import functools

import jax
import jax.numpy as jnp
from jax import lax
from jax.experimental import pallas as pl
from jax.experimental.pallas import tpu as pltpu
from jax.sharding import PartitionSpec as P

MESH = pl.DeviceIdType.MESH
F, G, FT, GT = range(4)
X1, X2, O1, O2, G1, G2 = range(6)
Y1, Y2, R1, R2, E1, E2 = range(6)
PX, PH, PD, PY, PU, PE = range(6)


def sigmoid(v):
    return 1.0 / (1.0 + jnp.exp(-v))


def silu(v):
    return v / (1.0 + jnp.exp(-v))


def slope(v):
    sig = sigmoid(v)
    return sig * (1.0 + v * (1.0 - sig))


def kernel(
    dims, fwd_hbm, bout_hbm, bgrad_hbm, nxt_hbm, loss_hbm, kern_hbm, fout, backs, grads, dw,
    fwd, bout, bgrad, nxt, loss, kern, kt, w, dt, pad, stage, second, edge, rest, made, nat, acc,
    g3, dsum, dpart, dgot, halo_s, halo_r, seg_s, seg_r, back_s, back_r, edge_s, edge_r, pass_s,
    out_s, d_s, d_r, in_s, ready_s,
):
    C, D, H, W, segs, n, scale = dims
    DH, HW = D * H, H * W
    cs = C // n
    LW = pl.cdiv(3 * C, 128) * 128
    f32, bf16 = jnp.float32, jnp.bfloat16
    seg = lax.axis_index("segment")
    slab = lax.axis_index("slab")
    has_prev, has_next = seg > 0, seg < segs - 1
    is_first, is_last = seg == 0, seg == segs - 1
    odd, even = lax.rem(seg, 2) == 1, lax.rem(seg, 2) == 0
    relayed = jnp.logical_and(has_next, odd)
    whole = jnp.logical_and(has_next, even)
    prev_seg = lax.rem(seg + segs - 1, segs)
    next_seg = lax.rem(seg + 1, segs)
    lane_no = lax.broadcasted_iota(jnp.int32, (C, W), 1)

    if n == 2:
        sides = [(None, 1 - slab, 0, 1 - slab)]
        toward = [(None, slab, 0, 1 - slab)]
    else:
        below, above = lax.rem(slab + n - 1, n), lax.rem(slab + 1, n)
        sides = [(slab > 0, 0, 0, below), (slab < n - 1, 1, 1, above)]
        toward = [(slab < n - 1, 0, 0, above), (slab > 0, 1, 1, below)]

    def over(rows, act):
        for there, side, slot, peer in rows:
            if there is None:
                act(side, slot, peer)
            else:
                pl.when(there)(functools.partial(act, side, slot, peer))

    def near_q(side):
        return side * (D + 1) - 1

    barrier = pltpu.get_barrier_semaphore()

    for k in range(1, n):
        pl.semaphore_signal(
            barrier, inc=1, device_id={"slab": lax.rem(slab + k, n)}, device_id_type=MESH
        )

    @pl.when(has_prev)
    def _():
        pl.semaphore_signal(barrier, inc=1, device_id={"segment": prev_seg}, device_id_type=MESH)

    @pl.when(has_next)
    def _():
        pl.semaphore_signal(barrier, inc=1, device_id={"segment": next_seg}, device_id_type=MESH)

    fetches = [
        pltpu.make_async_copy(src, dst, in_s.at[i])
        for i, (src, dst) in enumerate(
            [
                (bgrad_hbm, bgrad), (bout_hbm, bout), (fwd_hbm, fwd),
                (kern_hbm, kern), (nxt_hbm, nxt), (loss_hbm, loss),
            ]
        )
    ]
    for fetch in fetches:
        fetch.start()

    def lanes(at, size):
        return pl.ds(at if isinstance(at, int) else pl.multiple_of(at, W), size)

    def lane(q, hh):
        return ((q + 2) * (H + 2) + hh) * W

    zero = jnp.zeros((C, W), bf16)
    for t in range(2):
        for k in range(6):
            reach = 2 if t == 1 and k in (PH, PD) else 1
            for q in range(-reach, D + reach):
                for hh in (0, H + 1):
                    pad[t, k, :, pl.ds(lane(q, hh), W)] = zero

    for q, missing in ((-1, slab == 0), (D, slab == n - 1)):
        @pl.when(missing)
        def _():
            for t in range(2):
                for k in range(6):
                    pad[t, k, :, pl.ds(lane(q, 1), HW)] = jnp.zeros((C, HW), bf16)

    def load_stage(slot, ref, s):
        stage[slot] = ref[s].astype(f32)

    def staged(slot, r):
        return stage[slot, pl.ds(r, C, stride=DH), :]

    def prepare_weights():
        fetches[3].wait()
        wide = kern[...].astype(f32)
        kt[...] = jnp.concatenate([wide, jnp.zeros((LW - 2 * C, 27 * C), f32)], axis=0).T

        def tap(t):
            return kt[pl.ds(t, C, stride=27), :]

        for a in range(3):
            for c in range(3):
                block = jnp.concatenate([tap(9 * a + 3 * b + c) for b in range(3)], axis=0).T
                for f in range(2):
                    w[F + f, a, c * C : (c + 1) * C, :] = block[f * C : (f + 1) * C].astype(bf16)
                for f in range(2):
                    turned = jnp.concatenate(
                        [
                            tap(9 * (2 - a) + 3 * (2 - b) + 2 - c)[:, f * C : (f + 1) * C]
                            for b in range(3)
                        ],
                        axis=1,
                    )
                    w[FT + f, a, c * C : (c + 1) * C, :] = turned.astype(bf16)

    def load_pair(i, slot, ref):
        fetches[i].wait()
        for s in range(2):
            load_stage(slot + s, ref, s)

    def halo(t, k, side, slot, peer):
        if k == PU:
            src = made.at[t, R2, :, lanes((1 - side) * (D - 1) * HW, HW)]
            dst = rest.at[slot]
        else:
            src = pad.at[t, k, :, lanes(lane((1 - side) * (D - 1), 1), HW)]
            dst = pad.at[t, k, :, lanes(lane(near_q(side), 1), HW)]
        return pltpu.make_async_remote_copy(
            src_ref=src, dst_ref=dst, send_sem=halo_s.at[slot], recv_sem=halo_r.at[6 if t else k, slot],
            device_id={"slab": peer}, device_id_type=MESH,
        )

    def halo_start(t, k):
        over(toward, lambda side, slot, peer: halo(t, k, side, slot, peer).start())

    def halo_arrived(t, k):
        over(sides, lambda side, slot, peer: halo(t, k, side, slot, peer).wait_recv())

    def to_seg(k):
        return pltpu.make_async_remote_copy(
            src_ref=made.at[0, k], dst_ref=second.at[k],
            send_sem=seg_s.at[1 if k <= X2 else 0], recv_sem=seg_r.at[k],
            device_id={"segment": next_seg if k <= X2 else prev_seg}, device_id_type=MESH,
        )

    def edge_at(k, far, side, slot):
        return edge.at[k, slot, :, lanes((side if far else 1 - side) * HW, HW)]

    def edge_copy(src, k, far, target, which, side, slot, peer):
        plane = (1 - side) * (D - 2) + side if far else (1 - side) * (D - 1)
        return pltpu.make_async_remote_copy(
            src_ref=src.at[:, lanes(plane * HW, HW)], dst_ref=edge_at(k, far, side, slot),
            send_sem=edge_s.at[which, slot], recv_sem=edge_r.at[k // 2 + 4 if far else k - 1, slot],
            device_id={"segment": target, "slab": peer}, device_id_type=MESH,
        )

    def edge_start(src, k, far, target, which):
        over(toward, lambda *side: edge_copy(src, k, far, target, which, *side).start())

    def edge_arrived(k, far, *side):
        edge_copy(made.at[0, k], k, far, seg, 0, *side).wait_recv()

    def pass_on(k, side, slot, peer):
        if k == G1:
            src = pad.at[0, PE, :, lanes(lane(near_q(side), 1), HW)]
        else:
            src = rest.at[slot]
        return pltpu.make_async_remote_copy(
            src_ref=src, dst_ref=edge_at(k, False, side, slot),
            send_sem=pass_s.at[slot], recv_sem=edge_r.at[k - 1, slot],
            device_id={"segment": prev_seg}, device_id_type=MESH,
        )

    def drain(sem, src):
        pltpu.make_async_remote_copy(
            src_ref=src, dst_ref=src, send_sem=sem, recv_sem=sem,
            device_id={"slab": lax.rem(slab + 1, n)}, device_id_type=MESH,
        ).wait_send()

    def planes_of(count):
        return pad.at[0, 0, :, pl.ds(0, count * HW)]

    def out_prev(k):
        dst = backs.at[k - R1] if k < E1 else grads.at[k - E1]
        return pltpu.make_async_remote_copy(
            src_ref=nat.at[k], dst_ref=dst, send_sem=back_s.at[0], recv_sem=back_r.at[0],
            device_id={"segment": prev_seg}, device_id_type=MESH,
        )

    def own_out(k):
        return pltpu.make_async_copy(nat.at[k], fout.at[k], out_s.at[0])

    def last_act(k):
        return pltpu.make_async_copy(nat.at[k], backs.at[k], out_s.at[1])

    def last_grad(k):
        return pltpu.make_async_copy(loss.at[2 + k], grads.at[k], out_s.at[1])

    def put(t, k, r, value):
        d, h = divmod(r, H)
        put_at(t, k, d, h, value)

    def put_at(t, k, q, h, value):
        pad[t, k, :, lanes(lane(q, h + 1), W)] = value.astype(bf16)

    def tall(t, k, q):
        return jnp.concatenate([pad[t, k, :, lanes(lane(q, b), HW)] for b in range(3)], axis=0)

    def taps(t, k, m, p, which):
        total = None
        for a in which:
            part = jnp.dot(w[m, a], tall(t, k, p + a - 1), preferred_element_type=f32)
            total = part if total is None else total + part
        return total

    def inner(p):
        return [a for a in range(3) if 0 <= p + a - 1 < D]

    def conv_local(t, k, m, slot):
        for p in range(D):
            acc[slot, :, pl.ds(p * HW, HW)] = taps(t, k, m, p, inner(p))

    def rows_of(total):
        for h in range(H):
            y = total[:, h * W : (h + 1) * W]
            left = jnp.where(lane_no == 0, 0.0, pltpu.roll(y[:C], 1, 1))
            right = jnp.where(lane_no == W - 1, 0.0, pltpu.roll(y[2 * C :], W - 1, 1))
            yield h, y[C : 2 * C] + left + right

    def conv_finish(t, k, m, slot, act, then=None):
        def outer(side):
            return jnp.dot(w[m, 2 * side], tall(t, k, near_q(side)), preferred_element_type=f32)

        def add(side, at, peer):
            acc[slot, :, lanes(side * (D - 1) * HW, HW)] += outer(side)

        if n > 2:
            over(sides, add)
        for i in range(D):
            p = (1 - slab) * (D - 1) + i * (2 * slab - 1) if n == 2 else i
            total = acc[slot, :, lanes(p * HW, HW)]
            if n == 2 and i == 0:
                total += outer(1 - slab)
            for h, out in rows_of(total):
                act(p * H + h, p, h, out)
            if then is not None and i == (0 if n == 2 else D - 1):
                then()

    def conv_whole(t, k, m):
        for p in range(D):
            for h, out in rows_of(taps(t, k, m, p, range(3))):
                yield p * H + h, out

    def widen(j, r, v):
        at = pl.ds(r * W, W)
        g3[j, 0:C, at] = jnp.where(lane_no == W - 1, 0.0, pltpu.roll(v, W - 1, 1)).astype(bf16)
        g3[j, C : 2 * C, at] = v.astype(bf16)
        g3[j, 2 * C : 3 * C, at] = jnp.where(lane_no == 0, 0.0, pltpu.roll(v, 1, 1)).astype(bf16)

    def product(lhs, j, p):
        return lax.dot_general(
            lhs, g3[j, :, lanes(p * HW, HW)], (((1,), (1,)), ((), ())), preferred_element_type=f32
        )

    def wgrad_inner(t, k, j):
        parts = [None] * 3
        for p in range(D):
            which = inner(p)
            part = product(jnp.concatenate([tall(t, k, p + a - 1) for a in which], axis=0), j, p)
            for i, a in enumerate(which):
                block = part[i * 3 * C : (i + 1) * 3 * C]
                parts[a] = block if parts[a] is None else parts[a] + block
        for a in range(3):
            here = pl.ds(a * 3 * C, 3 * C)
            if t == 0:
                dsum[j, here] = parts[a]
            else:
                dsum[j, here] += parts[a]

    def wgrad_whole(k, j):
        for p in range(D):
            lhs = jnp.concatenate([tall(1, k, p + a - 1) for a in range(3)], axis=0)
            part = product(lhs, j, p)
            total = part if p == 0 else total + part
        dsum[j] += total

    def wgrad_outer(t, k, j):
        def outer(side, slot, peer):
            at = side * 6 * C
            here = pl.ds(at if isinstance(at, int) else pl.multiple_of(at, 8), 3 * C)
            dsum[j, here] += product(tall(t, k, near_q(side)), j, side * (D - 1))

        over(sides, outer)

    def wgrad_share(j):
        for q in range(1, n):
            first = lax.rem(slab + q, n) * cs
            for ab in range(9):
                part = dsum[j, pl.ds(pl.multiple_of(ab * C + first, 8), cs)].astype(bf16)
                dpart[j, q - 1, ab] = jnp.concatenate(
                    [part, jnp.zeros((cs, LW - 3 * C), bf16)], axis=1
                )
            share(j, q).start()

    def share(j, q):
        target = lax.rem(slab + q, n)
        return pltpu.make_async_remote_copy(
            src_ref=dpart.at[j, q - 1], dst_ref=dgot.at[j, q - 1],
            send_sem=d_s.at[q - 1], recv_sem=d_r.at[j, q - 1],
            device_id={"slab": target}, device_id_type=MESH,
        )

    def keep(t, k, r, value):
        held = value.astype(bf16)
        made[t, k, :, lanes(r * W, W)] = held
        wide = held.astype(f32)
        if t == 1:
            stage[k, pl.ds(r, C, stride=DH), :] = wide
        return wide

    def hand_on(k):
        src = made.at[0, k]
        if k <= X2:
            @pl.when(has_next)
            def _():
                if k == Y2:
                    edge_start(src, X2, False, next_seg, 1)
                to_seg(k).start()

            @pl.when(is_last)
            def _():
                edge_start(src, O1 + k, False, seg, 2)
                if k == Y1:
                    edge_start(src, O1, True, seg, 2)
                second[O1 + k] = made[0, k]
        else:
            @pl.when(has_prev)
            def _():
                to_seg(k).start()
                if k == O1:
                    edge_start(src, O1, False, prev_seg, 0)
                    edge_start(made.at[0, G2], G2, False, prev_seg, 0)
                    pl.when(even)(functools.partial(edge_start, src, O1, True, prev_seg, 0))

    def hand_on_far():
        @pl.when(odd)
        def _():
            for k in (G2, O1):
                edge_start(made.at[0, k], k, True, prev_seg, 0)
            for k in (G1, O2):
                over(sides, lambda *side: pass_on(k, *side).start())

    def give_out(k):
        nat[k] = stage[k].astype(bf16)
        if k < R1:
            own_out(k).start()

            @pl.when(is_last)
            def _():
                last_act(k).start()
        else:
            @pl.when(has_prev)
            def _():
                out_prev(k).start()

    def arrived(k):
        there = has_prev if k <= X2 else whole if k in (G1, O2) else has_next

        @pl.when(there)
        def _():
            to_seg(k).wait_recv()

    load_pair(0, G1, bgrad)
    for r in range(DH):
        put(0, PD, r, staged(G2, r))
    peers = has_prev.astype(jnp.int32) + has_next.astype(jnp.int32) + n - 1
    pl.semaphore_wait(barrier, peers)
    halo_start(0, PD)

    @pl.when(has_prev)
    def _():
        pl.semaphore_signal(
            ready_s.at[1], inc=1, device_id={"segment": prev_seg}, device_id_type=MESH
        )

    @pl.when(has_next)
    def _():
        pl.semaphore_signal(
            ready_s.at[0], inc=1, device_id={"segment": next_seg}, device_id_type=MESH
        )

    load_pair(1, O1, bout)
    for r in range(DH):
        put(0, PH, r, silu(staged(O1, r)))
    halo_start(0, PH)
    load_pair(2, X1, fwd)
    for r in range(DH):
        put(0, PX, r, silu(staged(X2, r)))
    halo_start(0, PX)
    prepare_weights()
    conv_local(0, PD, GT, 0)
    conv_local(0, PH, G, 1)
    conv_local(0, PX, F, 2)
    for r in range(DH):
        widen(1, r, staged(G2, r))
    wgrad_inner(0, PH, 1)

    fetches[4].wait()
    fetches[5].wait()

    @pl.when(is_first)
    def _():
        for s in range(2):
            load_stage(6 + s, nxt, s)
            for r in range(DH):
                second[X1 + s, :, pl.ds(r * W, W)] = staged(6 + s, r).astype(bf16)
        edge_start(second.at[X2], X2, False, seg, 2)

    @pl.when(is_last)
    def _():
        for s in range(2):
            last_grad(s).start()
            load_stage(6 + s, loss, s)
            for r in range(DH):
                second[G1 + s, :, pl.ds(r * W, W)] = staged(6 + s, r).astype(bf16)
            edge_start(second.at[G1 + s], G1 + s, False, seg, 2)
        edge_start(second.at[G2], G2, True, seg, 2)

    @pl.when(has_prev)
    def _():
        pl.semaphore_wait(ready_s.at[0], 1)

    @pl.when(has_next)
    def _():
        pl.semaphore_wait(ready_s.at[1], 1)

    halo_arrived(0, PD)

    def act(r, p, h, out):
        put_at(0, PE, p, h, keep(0, E1, r, staged(G1, r) + slope(staged(O1, r)) * out))

    conv_finish(0, PD, GT, 0, act, functools.partial(halo_start, 0, PE))
    hand_on(E1)
    conv_local(0, PE, FT, 0)
    for r in range(DH):
        widen(0, r, made[0, E1, :, pl.ds(r * W, W)].astype(f32))
    halo_arrived(0, PH)

    def act(r, p, h, out):
        put_at(0, PU, p, h, silu(keep(0, R2, r, staged(O2, r) - out)))

    conv_finish(0, PH, G, 1, act, functools.partial(halo_start, 0, PU))
    hand_on(R2)
    conv_local(0, PU, F, 1)
    wgrad_outer(0, PH, 1)
    halo_arrived(0, PX)

    def act(r, p, h, out):
        put_at(0, PY, p, h, silu(keep(0, Y1, r, staged(X1, r) + out)))

    conv_finish(0, PX, F, 2, act, functools.partial(halo_start, 0, PY))
    hand_on(Y1)
    conv_local(0, PY, G, 2)
    wgrad_inner(0, PU, 0)

    halo_arrived(0, PE)

    def act(r, p, h, out):
        v = made[0, R2, :, lanes(r * W, W)].astype(f32)
        keep(0, E2, r, staged(G2, r) + slope(v) * out)

    conv_finish(0, PE, FT, 0, act)
    hand_on(E2)
    halo_arrived(0, PU)

    def rest_in(side, slot, peer):
        for h in range(H):
            v = rest[slot, :, pl.ds(h * W, W)].astype(f32)
            put_at(0, PU, near_q(side), h, silu(v))

    over(sides, rest_in)
    conv_finish(0, PU, F, 1, lambda r, p, h, out: keep(0, R1, r, staged(O1, r) - out))
    hand_on(R1)
    halo_arrived(0, PY)
    conv_finish(0, PY, G, 2, lambda r, p, h, out: keep(0, Y2, r, staged(X2, r) + out))
    hand_on(Y2)
    hand_on_far()
    wgrad_outer(0, PU, 0)

    def got(k, r):
        return second[k, :, lanes(r * W, W)].astype(f32)

    def near(k, side, slot, h):
        return edge[k, slot, :, lanes((1 - side) * HW + h * W, W)].astype(f32)

    @pl.when(relayed)
    def _():
        for k in (G1, O2):
            to_seg(k).wait_recv()
            edge_start(second.at[k], k, False, seg, 3)

    def forward_own():
        arrived(X2)
        for r in range(DH):
            put(1, PX, r, silu(got(X2, r)))
        conv_local(1, PX, F, 2)

    def forward():
        arrived(X1)

        def edges(side, slot, peer):
            edge_arrived(X2, False, side, slot, peer)
            for h in range(H):
                put_at(1, PX, near_q(side), h, silu(near(X2, side, slot, h)))

        over(sides, edges)

        def act(r, p, h, out):
            put_at(1, PY, p, h, silu(keep(1, Y1, r, got(X1, r) + out)))

        conv_finish(1, PX, F, 2, act, functools.partial(halo_start, 1, PY))
        give_out(Y1)
        conv_local(1, PY, G, 2)

    arrived(G2)

    @pl.when(relayed)
    def _():
        edge_start(second.at[G2], G2, True, seg, 3)

    pl.when(odd)(forward_own)
    for d in range(D):
        pad[1, PD, :, pl.ds(lane(d, 1), HW)] = second[G2, :, pl.ds(d * HW, HW)]
    conv_local(1, PD, GT, 0)
    arrived(O1)
    for r in range(DH):
        put(1, PH, r, silu(got(O1, r)))
    conv_local(1, PH, G, 1)
    for r in range(DH):
        widen(1, r, got(G2, r))
    wgrad_inner(1, PH, 1)
    pl.when(odd)(forward)

    def edges_in(far, side, slot, peer):
        q = near_q(side) + (2 * side - 1 if far else 0)
        at = (side if far else 1 - side) * HW
        edge_arrived(G2, far, side, slot, peer)
        pad[1, PD, :, lanes(lane(q, 1), HW)] = edge[G2, slot, :, lanes(at, HW)]
        edge_arrived(O1, far, side, slot, peer)
        for h in range(H):
            put_at(1, PH, q, h, silu(edge[O1, slot, :, lanes(at + h * W, W)].astype(f32)))

    over(sides, functools.partial(edges_in, False))
    arrived(G1)

    def act(r, p, h, out):
        put_at(1, PE, p, h, keep(1, E1, r, got(G1, r) + slope(got(O1, r)) * out))

    conv_finish(1, PD, GT, 0, act)
    arrived(O2)

    def act(r, p, h, out):
        put_at(1, PU, p, h, silu(keep(1, R2, r, got(O2, r) - out)))

    conv_finish(1, PH, G, 1, act)
    for r in range(DH):
        widen(0, r, made[1, E1, :, pl.ds(r * W, W)].astype(f32))

    def beyond(side, slot, peer):
        edges_in(True, side, slot, peer)
        edge_arrived(G1, False, side, slot, peer)
        edge_arrived(O2, False, side, slot, peer)
        q = near_q(side)
        turned, plain = taps(1, PD, GT, q, range(3)), taps(1, PH, G, q, range(3))
        for h, out in rows_of(turned):
            value = near(G1, side, slot, h) + slope(near(O1, side, slot, h)) * out
            put_at(1, PE, q, h, value)
        for h, out in rows_of(plain):
            value = (near(O2, side, slot, h) - out).astype(bf16).astype(f32)
            put_at(1, PU, q, h, silu(value))

    over(sides, beyond)
    wgrad_whole(PU, 0)
    wgrad_share(0)
    wgrad_outer(1, PH, 1)
    wgrad_share(1)
    give_out(E1)
    give_out(R2)


    for r, out in conv_whole(1, PE, FT):
        v = made[1, R2, :, pl.ds(r * W, W)].astype(f32)
        keep(1, E2, r, got(G2, r) + slope(v) * out)
    give_out(E2)
    for r, out in conv_whole(1, PU, F):
        keep(1, R1, r, got(O1, r) - out)
    give_out(R1)

    def gradients():
        for j in (0, 1):
            for q in range(1, n):
                share(j, q).wait_recv()
            for ab in range(9):
                own = dsum[j, pl.ds(pl.multiple_of(ab * C + slab * cs, 8), cs)]
                total = jnp.concatenate([own, jnp.zeros((cs, LW - 3 * C), f32)], axis=1)
                for q in range(1, n):
                    total += dgot[j, q - 1, ab].astype(f32)
                total *= scale
                for c in range(3):
                    tap = total if c == 0 else pltpu.roll(total, LW - c * C, 1)
                    dt[j, pl.ds(3 * ab + c, cs, stride=27), :] = tap
            dw[j] = dt[j].T[:C]

    @pl.when(even)
    def _():
        forward_own()
        forward()
        gradients()

    halo_arrived(1, PY)
    conv_finish(1, PY, G, 2, lambda r, p, h, out: keep(1, Y2, r, got(X2, r) + out))
    give_out(Y2)
    pl.when(odd)(gradients)

    over(toward, lambda side, slot, peer: drain(halo_s.at[slot], planes_of(7)))
    for q in range(1, n):
        drain(d_s.at[q - 1], dpart.at[:, 0])
    pltpu.make_async_copy(nat.at[pl.ds(Y1, 2)], fout, out_s.at[0]).wait()

    @pl.when(is_first)
    def _():
        over(toward, lambda side, slot, peer: drain(edge_s.at[2, slot], planes_of(1)))

    @pl.when(is_last)
    def _():
        pltpu.make_async_copy(nat.at[pl.ds(0, 4)], nat.at[pl.ds(0, 4)], out_s.at[1]).wait()
        over(toward, lambda side, slot, peer: drain(edge_s.at[2, slot], planes_of(6)))

    @pl.when(has_next)
    def _():
        drain(seg_s.at[1], made.at[0, pl.ds(0, 2)])
        over(toward, lambda side, slot, peer: drain(edge_s.at[1, slot], planes_of(1)))
        drain(back_r.at[0], nat.at[pl.ds(R1, 4)])

    @pl.when(has_prev)
    def _():
        drain(seg_s.at[0], made.at[0, pl.ds(0, 4)])
        drain(back_s.at[0], nat.at[pl.ds(R1, 4)])

        @pl.when(even)
        def _():
            over(toward, lambda side, slot, peer: drain(edge_s.at[0, slot], planes_of(3)))

    @pl.when(odd)
    def _():
        over(toward, lambda side, slot, peer: drain(edge_s.at[0, slot], planes_of(4)))
        over(sides, lambda side, slot, peer: drain(pass_s.at[slot], planes_of(2)))

    @pl.when(relayed)
    def _():
        over(toward, lambda side, slot, peer: drain(edge_s.at[3, slot], planes_of(3)))


def write_out(*refs):
    srcs, dsts, sems = refs[:4], refs[4:8], refs[8]
    writes = [pltpu.make_async_copy(a, b, sems.at[i]) for i, (a, b) in enumerate(zip(srcs, dsts))]
    for write in writes:
        write.start()
    for write in writes:
        write.wait()


def local(segs, n, fwd_in, back_out, back_grad, batch_next, loss_grad, weights):
    _, _, C, D, H, W = fwd_in.shape
    rows = C * D * H
    cs = C // n
    ends = 1 if n == 2 else 2
    f32, bf16 = jnp.float32, jnp.bfloat16
    scale = float(D * n * H * W) ** (-0.5)
    vmem = pl.BlockSpec(memory_space=pltpu.VMEM)
    hbm = pl.BlockSpec(memory_space=pltpu.HBM)
    wide = pl.cdiv(3 * C, 128) * 128
    anywhere = pl.BlockSpec(memory_space=pl.ANY)
    pair = jax.ShapeDtypeStruct((2, rows, W), bf16)
    share = jax.ShapeDtypeStruct((2, C, 27 * cs), f32)
    dma = pltpu.SemaphoreType.DMA
    fout, backs, grads, dw = pl.pallas_call(
        functools.partial(kernel, (C, D, H, W, segs, n, scale)),
        out_shape=tuple(pltpu.VMEM(x.shape, x.dtype) for x in (pair, pair, pair, share)),
        in_specs=[hbm] * 6,
        out_specs=(vmem, vmem, vmem, vmem),
        scratch_shapes=[
            pltpu.VMEM((2, rows, W), bf16),
            pltpu.VMEM((2, rows, W), bf16),
            pltpu.VMEM((2, rows, W), bf16),
            pltpu.VMEM((2, rows, W), bf16),
            pltpu.VMEM((4, rows, W), bf16),
            pltpu.VMEM((2 * C, 27 * C), bf16),
            pltpu.VMEM((27 * C, wide), f32),
            pltpu.VMEM((4, 3, 3 * C, 3 * C), bf16),
            pltpu.VMEM((2, 27 * cs, wide), f32),
            pltpu.VMEM((2, 6, C, (D + 4) * (H + 2) * W), bf16),
            pltpu.VMEM((8, rows, W), f32),
            pltpu.VMEM((6, C, D * H * W), bf16),
            pltpu.VMEM((6, ends, C, 2 * H * W), bf16),
            pltpu.VMEM((ends, C, H * W), bf16),
            pltpu.VMEM((2, 6, C, D * H * W), bf16),
            pltpu.VMEM((6, rows, W), bf16),
            pltpu.VMEM((3, 3 * C, D * H * W), f32),
            pltpu.VMEM((2, 3 * C, D * H * W), bf16),
            pltpu.VMEM((2, 9 * C, 3 * C), f32),
            pltpu.VMEM((2, n - 1, 9, cs, wide), bf16),
            pltpu.VMEM((2, n - 1, 9, cs, wide), bf16),
            dma((ends,)),
            dma((7, ends)),
            dma((2,)),
            dma((6,)),
            dma((1,)),
            dma((1,)),
            dma((4, ends)),
            dma((7, ends)),
            dma((ends,)),
            dma((2,)),
            dma((n - 1,)),
            dma((2, n - 1)),
            dma((6,)),
            pltpu.SemaphoreType.REGULAR((2,)),
        ],
        compiler_params=pltpu.CompilerParams(
            collective_id=0, has_side_effects=True, vmem_limit_bytes=48 << 20
        ),
        name="petra",
    )(
        *[
            pltpu.with_memory_space_constraint(x, pltpu.HBM)
            for x in (
                fwd_in.reshape(2, rows, W),
                back_out.reshape(2, rows, W),
                back_grad.reshape(2, rows, W),
                batch_next.reshape(2, rows, W),
                loss_grad.reshape(4, rows, W),
                weights.reshape(2 * C, 27 * C),
            )
        ]
    )
    fout, backs, grads, dw = pl.pallas_call(
        write_out,
        out_shape=(pair, pair, pair, share),
        in_specs=[vmem] * 4,
        out_specs=(hbm,) * 4,
        scratch_shapes=[dma((4,))],
        compiler_params=pltpu.CompilerParams(vmem_limit_bytes=4 << 20),
        name="write_out",
    )(fout, backs, grads, dw)
    shape = fwd_in.shape
    return fout.reshape(shape), backs.reshape(shape), grads.reshape(shape), dw[None]


def solution(mesh):
    field = P("segment", None, None, "slab", None, None)
    return jax.shard_map(
        functools.partial(local, mesh.shape["segment"], mesh.shape["slab"]),
        mesh=mesh,
        in_specs=(
            field,
            field,
            field,
            P(None, None, "slab", None, None),
            P(None, None, None, "slab", None, None),
            P("segment", None, None, None),
        ),
        out_specs=(field, field, field, P("segment", None, None, "slab")),
        check_vma=False,
    )
```

```python
import functools

import jax
import jax.numpy as jnp
from jax import lax
from jax.experimental import pallas as pl
from jax.experimental.pallas import tpu as pltpu
from jax.sharding import PartitionSpec as P

MESH = pl.DeviceIdType.MESH
F, G, FT, GT = range(4)
X1, X2, O1, O2, G1, G2 = range(6)
Y1, Y2, R1, R2, E1, E2 = range(6)
PX, PH, PD, PY, PU, PE = range(6)


def sigmoid(v):
    return 1.0 / (1.0 + jnp.exp(-v))


def silu(v):
    return v / (1.0 + jnp.exp(-v))


def slope(v):
    sig = sigmoid(v)
    return sig * (1.0 + v * (1.0 - sig))


def kernel(
    dims, fwd_hbm, bout_hbm, bgrad_hbm, nxt_hbm, loss_hbm, kern_hbm, fout, backs, grads, dw,
    fwd, bout, bgrad, nxt, loss, kern, kt, w, pairs, dt, pad, stage, second, edge, rest, made, nat, acc,
    g3, dsum, dpart, dgot, halo_s, halo_r, seg_s, seg_r, back_s, back_r, edge_s, edge_r, pass_s,
    out_s, d_s, d_r, in_s, ready_s,
):
    C, D, H, W, segs, n, scale = dims
    DH, HW = D * H, H * W
    cs = C // n
    LW = pl.cdiv(3 * C, 128) * 128
    f32, bf16 = jnp.float32, jnp.bfloat16
    seg = lax.axis_index("segment")
    slab = lax.axis_index("slab")
    has_prev, has_next = seg > 0, seg < segs - 1
    is_first, is_last = seg == 0, seg == segs - 1
    odd, even = lax.rem(seg, 2) == 1, lax.rem(seg, 2) == 0
    relayed = jnp.logical_and(has_next, odd)
    whole = jnp.logical_and(has_next, even)
    prev_seg = lax.rem(seg + segs - 1, segs)
    next_seg = lax.rem(seg + 1, segs)
    lane_no = lax.broadcasted_iota(jnp.int32, (C, W), 1)

    if n == 2:
        sides = [(None, 1 - slab, 0, 1 - slab)]
        toward = [(None, slab, 0, 1 - slab)]
    else:
        below, above = lax.rem(slab + n - 1, n), lax.rem(slab + 1, n)
        sides = [(slab > 0, 0, 0, below), (slab < n - 1, 1, 1, above)]
        toward = [(slab < n - 1, 0, 0, above), (slab > 0, 1, 1, below)]

    def over(rows, act):
        for there, side, slot, peer in rows:
            if there is None:
                act(side, slot, peer)
            else:
                pl.when(there)(functools.partial(act, side, slot, peer))

    def near_q(side):
        return side * (D + 1) - 1

    barrier = pltpu.get_barrier_semaphore()

    for k in range(1, n):
        pl.semaphore_signal(
            barrier, inc=1, device_id={"slab": lax.rem(slab + k, n)}, device_id_type=MESH
        )

    @pl.when(has_prev)
    def _():
        pl.semaphore_signal(barrier, inc=1, device_id={"segment": prev_seg}, device_id_type=MESH)

    @pl.when(has_next)
    def _():
        pl.semaphore_signal(barrier, inc=1, device_id={"segment": next_seg}, device_id_type=MESH)

    fetches = [
        pltpu.make_async_copy(src, dst, in_s.at[i])
        for i, (src, dst) in enumerate(
            [
                (bgrad_hbm, bgrad), (bout_hbm, bout), (fwd_hbm, fwd),
                (kern_hbm, kern), (nxt_hbm, nxt), (loss_hbm, loss),
            ]
        )
    ]
    for fetch in fetches:
        fetch.start()

    def lanes(at, size):
        return pl.ds(at if isinstance(at, int) else pl.multiple_of(at, W), size)

    def lane(q, hh):
        return ((q + 2) * (H + 2) + hh) * W

    zero = jnp.zeros((C, W), bf16)
    for t in range(2):
        for k in range(6):
            reach = 2 if t == 1 and k in (PH, PD) else 1
            for q in range(-reach, D + reach):
                for hh in (0, H + 1):
                    pad[t, k, :, pl.ds(lane(q, hh), W)] = zero

    for q, missing in ((-1, slab == 0), (D, slab == n - 1)):
        @pl.when(missing)
        def _():
            for t in range(2):
                for k in range(6):
                    pad[t, k, :, pl.ds(lane(q, 1), HW)] = jnp.zeros((C, HW), bf16)

    def load_stage(slot, ref, s):
        stage[slot] = ref[s].astype(f32)

    def staged(slot, r):
        return stage[slot, pl.ds(r, C, stride=DH), :]

    def prepare_weights():
        fetches[3].wait()
        wide = kern[...].astype(f32)
        kt[...] = jnp.concatenate([wide, jnp.zeros((LW - 2 * C, 27 * C), f32)], axis=0).T

        def tap(t):
            return kt[pl.ds(t, C, stride=27), :]

        def set_weights(m, a, c, block):
            here = pl.ds(c * C, C)
            w[m, a, here, :] = block
            if a < 2:
                pairs[m, a, here, 0 : 3 * C] = block
            if a > 0:
                pairs[m, a - 1, here, 3 * C : 6 * C] = block

        for a in range(3):
            for c in range(3):
                block = jnp.concatenate([tap(9 * a + 3 * b + c) for b in range(3)], axis=0).T
                for f in range(2):
                    set_weights(F + f, a, c, block[f * C : (f + 1) * C].astype(bf16))
                for f in range(2):
                    turned = jnp.concatenate(
                        [
                            tap(9 * (2 - a) + 3 * (2 - b) + 2 - c)[:, f * C : (f + 1) * C]
                            for b in range(3)
                        ],
                        axis=1,
                    )
                    set_weights(FT + f, a, c, turned.astype(bf16))

    def load_pair(i, slot, ref):
        fetches[i].wait()
        for s in range(2):
            load_stage(slot + s, ref, s)

    def halo(t, k, side, slot, peer):
        if k == PU:
            src = made.at[t, R2, :, lanes((1 - side) * (D - 1) * HW, HW)]
            dst = rest.at[slot]
        else:
            src = pad.at[t, k, :, lanes(lane((1 - side) * (D - 1), 1), HW)]
            dst = pad.at[t, k, :, lanes(lane(near_q(side), 1), HW)]
        return pltpu.make_async_remote_copy(
            src_ref=src, dst_ref=dst, send_sem=halo_s.at[slot], recv_sem=halo_r.at[6 if t else k, slot],
            device_id={"slab": peer}, device_id_type=MESH,
        )

    def halo_start(t, k):
        over(toward, lambda side, slot, peer: halo(t, k, side, slot, peer).start())

    def halo_arrived(t, k):
        over(sides, lambda side, slot, peer: halo(t, k, side, slot, peer).wait_recv())

    def to_seg(k):
        return pltpu.make_async_remote_copy(
            src_ref=made.at[0, k], dst_ref=second.at[k],
            send_sem=seg_s.at[1 if k <= X2 else 0], recv_sem=seg_r.at[k],
            device_id={"segment": next_seg if k <= X2 else prev_seg}, device_id_type=MESH,
        )

    def edge_at(k, far, side, slot):
        return edge.at[k, slot, :, lanes((side if far else 1 - side) * HW, HW)]

    def edge_copy(src, k, far, target, which, side, slot, peer):
        plane = (1 - side) * (D - 2) + side if far else (1 - side) * (D - 1)
        return pltpu.make_async_remote_copy(
            src_ref=src.at[:, lanes(plane * HW, HW)], dst_ref=edge_at(k, far, side, slot),
            send_sem=edge_s.at[which, slot], recv_sem=edge_r.at[k // 2 + 4 if far else k - 1, slot],
            device_id={"segment": target, "slab": peer}, device_id_type=MESH,
        )

    def edge_start(src, k, far, target, which):
        over(toward, lambda *side: edge_copy(src, k, far, target, which, *side).start())

    def edge_arrived(k, far, *side):
        edge_copy(made.at[0, k], k, far, seg, 0, *side).wait_recv()

    def pass_on(k, side, slot, peer):
        if k == G1:
            src = pad.at[0, PE, :, lanes(lane(near_q(side), 1), HW)]
        else:
            src = rest.at[slot]
        return pltpu.make_async_remote_copy(
            src_ref=src, dst_ref=edge_at(k, False, side, slot),
            send_sem=pass_s.at[slot], recv_sem=edge_r.at[k - 1, slot],
            device_id={"segment": prev_seg}, device_id_type=MESH,
        )

    def drain(sem, src):
        pltpu.make_async_remote_copy(
            src_ref=src, dst_ref=src, send_sem=sem, recv_sem=sem,
            device_id={"slab": lax.rem(slab + 1, n)}, device_id_type=MESH,
        ).wait_send()

    def planes_of(count):
        return pad.at[0, 0, :, pl.ds(0, count * HW)]

    def out_prev(k):
        dst = backs.at[k - R1] if k < E1 else grads.at[k - E1]
        return pltpu.make_async_remote_copy(
            src_ref=nat.at[k], dst_ref=dst, send_sem=back_s.at[0], recv_sem=back_r.at[0],
            device_id={"segment": prev_seg}, device_id_type=MESH,
        )

    def own_out(k):
        return pltpu.make_async_copy(nat.at[k], fout.at[k], out_s.at[0])

    def last_act(k):
        return pltpu.make_async_copy(nat.at[k], backs.at[k], out_s.at[1])

    def last_grad(k):
        return pltpu.make_async_copy(loss.at[2 + k], grads.at[k], out_s.at[1])

    def put(t, k, r, value):
        d, h = divmod(r, H)
        put_at(t, k, d, h, value)

    def put_at(t, k, q, h, value):
        pad[t, k, :, lanes(lane(q, h + 1), W)] = value.astype(bf16)

    def tall(t, k, q):
        return jnp.concatenate([pad[t, k, :, lanes(lane(q, b), HW)] for b in range(3)], axis=0)

    def taps(t, k, m, p, which):
        total, which = None, list(which)
        while which:
            a = which.pop(0)
            lhs, rhs = w[m, a], tall(t, k, p + a - 1)
            if which:
                which.pop(0)
                lhs = pairs[m, a]
                rhs = jnp.concatenate([rhs, tall(t, k, p + a)], axis=0)
            part = jnp.dot(lhs, rhs, preferred_element_type=f32)
            total = part if total is None else total + part
        return total

    def inner(p):
        return [a for a in range(3) if 0 <= p + a - 1 < D]

    def conv_local(t, k, m, slot):
        for p in range(D):
            acc[slot, :, pl.ds(p * HW, HW)] = taps(t, k, m, p, inner(p))

    def rows_of(total):
        for h in range(H):
            y = total[:, h * W : (h + 1) * W]
            left = jnp.where(lane_no == 0, 0.0, pltpu.roll(y[:C], 1, 1))
            right = jnp.where(lane_no == W - 1, 0.0, pltpu.roll(y[2 * C :], W - 1, 1))
            yield h, y[C : 2 * C] + left + right

    def conv_finish(t, k, m, slot, act, then=None):
        def outer(side):
            return jnp.dot(w[m, 2 * side], tall(t, k, near_q(side)), preferred_element_type=f32)

        def add(side, at, peer):
            acc[slot, :, lanes(side * (D - 1) * HW, HW)] += outer(side)

        if n > 2:
            over(sides, add)
        for i in range(D):
            p = (1 - slab) * (D - 1) + i * (2 * slab - 1) if n == 2 else i
            total = acc[slot, :, lanes(p * HW, HW)]
            if n == 2 and i == 0:
                total += outer(1 - slab)
            for h, out in rows_of(total):
                act(p * H + h, p, h, out)
            if then is not None and i == (0 if n == 2 else D - 1):
                then()

    def conv_whole(t, k, m):
        for p in range(D):
            for h, out in rows_of(taps(t, k, m, p, range(3))):
                yield p * H + h, out

    def widen(j, r, v):
        at = pl.ds(r * W, W)
        g3[j, 0:C, at] = jnp.where(lane_no == W - 1, 0.0, pltpu.roll(v, W - 1, 1)).astype(bf16)
        g3[j, C : 2 * C, at] = v.astype(bf16)
        g3[j, 2 * C : 3 * C, at] = jnp.where(lane_no == 0, 0.0, pltpu.roll(v, 1, 1)).astype(bf16)

    def product(lhs, j, p):
        return lax.dot_general(
            lhs, g3[j, :, lanes(p * HW, HW)], (((1,), (1,)), ((), ())), preferred_element_type=f32
        )

    def wgrad_inner(t, k, j):
        parts = [None] * 3
        for p in range(D):
            which = inner(p)
            part = product(jnp.concatenate([tall(t, k, p + a - 1) for a in which], axis=0), j, p)
            for i, a in enumerate(which):
                block = part[i * 3 * C : (i + 1) * 3 * C]
                parts[a] = block if parts[a] is None else parts[a] + block
        for a in range(3):
            here = pl.ds(a * 3 * C, 3 * C)
            if t == 0:
                dsum[j, here] = parts[a]
            else:
                dsum[j, here] += parts[a]

    def wgrad_whole(k, j):
        for p in range(D):
            lhs = jnp.concatenate([tall(1, k, p + a - 1) for a in range(3)], axis=0)
            part = product(lhs, j, p)
            total = part if p == 0 else total + part
        dsum[j] += total

    def wgrad_outer(t, k, j):
        def outer(side, slot, peer):
            at = side * 6 * C
            here = pl.ds(at if isinstance(at, int) else pl.multiple_of(at, 8), 3 * C)
            dsum[j, here] += product(tall(t, k, near_q(side)), j, side * (D - 1))

        over(sides, outer)

    def wgrad_share(j):
        for q in range(1, n):
            first = lax.rem(slab + q, n) * cs
            for ab in range(9):
                part = dsum[j, pl.ds(pl.multiple_of(ab * C + first, 8), cs)].astype(bf16)
                dpart[j, q - 1, ab] = jnp.concatenate(
                    [part, jnp.zeros((cs, LW - 3 * C), bf16)], axis=1
                )
            share(j, q).start()

    def share(j, q):
        target = lax.rem(slab + q, n)
        return pltpu.make_async_remote_copy(
            src_ref=dpart.at[j, q - 1], dst_ref=dgot.at[j, q - 1],
            send_sem=d_s.at[q - 1], recv_sem=d_r.at[j, q - 1],
            device_id={"slab": target}, device_id_type=MESH,
        )

    def keep(t, k, r, value):
        held = value.astype(bf16)
        made[t, k, :, lanes(r * W, W)] = held
        wide = held.astype(f32)
        if t == 1:
            stage[k, pl.ds(r, C, stride=DH), :] = wide
        return wide

    def straight(first, side):
        return jnp.logical_and(lax.rem(seg, 4) == first, side == 1)

    def far_direct(side, slot, peer):
        @pl.when(straight(2, side))
        def _():
            for k in (O1, G2):
                edge_copy(made.at[0, k], k, True, prev_seg, 0, side, slot, peer).start()

    def far_relay(k):
        def act(side, slot, peer):
            @pl.when(jnp.logical_not(straight(1, side)))
            def _():
                edge_copy(second.at[k], k, True, seg, 3, side, slot, peer).start()

        @pl.when(relayed)
        def _():
            over(toward, act)

    def hand_on(k):
        src = made.at[0, k]
        if k <= X2:
            @pl.when(has_next)
            def _():
                if k == Y2:
                    edge_start(src, X2, False, next_seg, 1)
                to_seg(k).start()

            @pl.when(is_last)
            def _():
                edge_start(src, O1 + k, False, seg, 2)
                if k == Y1:
                    edge_start(src, O1, True, seg, 2)
                second[O1 + k] = made[0, k]
        else:
            @pl.when(has_prev)
            def _():
                to_seg(k).start()
                if k == O1:
                    edge_start(src, O1, False, prev_seg, 0)
                    edge_start(made.at[0, G2], G2, False, prev_seg, 0)
                    over(toward, far_direct)

    def hand_on_far():
        @pl.when(odd)
        def _():
            for k in (G2, O1):
                edge_start(made.at[0, k], k, True, prev_seg, 0)
            for k in (G1, O2):
                over(sides, lambda *side: pass_on(k, *side).start())

    def give_out(k):
        nat[k] = stage[k].astype(bf16)
        if k < R1:
            own_out(k).start()

            @pl.when(is_last)
            def _():
                last_act(k).start()
        else:
            @pl.when(has_prev)
            def _():
                out_prev(k).start()

    def arrived(k):
        there = has_prev if k <= X2 else whole if k in (G1, O2) else has_next

        @pl.when(there)
        def _():
            to_seg(k).wait_recv()

    load_pair(0, G1, bgrad)
    for r in range(DH):
        put(0, PD, r, staged(G2, r))
    peers = has_prev.astype(jnp.int32) + has_next.astype(jnp.int32) + n - 1
    pl.semaphore_wait(barrier, peers)
    halo_start(0, PD)

    @pl.when(has_prev)
    def _():
        pl.semaphore_signal(
            ready_s.at[1], inc=1, device_id={"segment": prev_seg}, device_id_type=MESH
        )

    @pl.when(has_next)
    def _():
        pl.semaphore_signal(
            ready_s.at[0], inc=1, device_id={"segment": next_seg}, device_id_type=MESH
        )

    load_pair(1, O1, bout)
    for r in range(DH):
        put(0, PH, r, silu(staged(O1, r)))
    halo_start(0, PH)
    load_pair(2, X1, fwd)
    for r in range(DH):
        put(0, PX, r, silu(staged(X2, r)))
    halo_start(0, PX)
    prepare_weights()
    conv_local(0, PD, GT, 0)
    conv_local(0, PH, G, 1)
    conv_local(0, PX, F, 2)
    for r in range(DH):
        widen(1, r, staged(G2, r))
    wgrad_inner(0, PH, 1)

    fetches[4].wait()
    fetches[5].wait()

    @pl.when(is_first)
    def _():
        for s in range(2):
            load_stage(6 + s, nxt, s)
            for r in range(DH):
                second[X1 + s, :, pl.ds(r * W, W)] = staged(6 + s, r).astype(bf16)
        edge_start(second.at[X2], X2, False, seg, 2)

    @pl.when(is_last)
    def _():
        for s in range(2):
            last_grad(s).start()
            load_stage(6 + s, loss, s)
            for r in range(DH):
                second[G1 + s, :, pl.ds(r * W, W)] = staged(6 + s, r).astype(bf16)
            edge_start(second.at[G1 + s], G1 + s, False, seg, 2)
        edge_start(second.at[G2], G2, True, seg, 2)

    @pl.when(has_prev)
    def _():
        pl.semaphore_wait(ready_s.at[0], 1)

    @pl.when(has_next)
    def _():
        pl.semaphore_wait(ready_s.at[1], 1)

    halo_arrived(0, PD)

    def act(r, p, h, out):
        put_at(0, PE, p, h, keep(0, E1, r, staged(G1, r) + slope(staged(O1, r)) * out))

    conv_finish(0, PD, GT, 0, act, functools.partial(halo_start, 0, PE))
    hand_on(E1)
    halo_arrived(0, PH)

    def act(r, p, h, out):
        put_at(0, PU, p, h, silu(keep(0, R2, r, staged(O2, r) - out)))

    conv_finish(0, PH, G, 1, act, functools.partial(halo_start, 0, PU))
    hand_on(R2)
    conv_local(0, PU, F, 1)
    wgrad_outer(0, PH, 1)
    halo_arrived(0, PX)

    def act(r, p, h, out):
        put_at(0, PY, p, h, silu(keep(0, Y1, r, staged(X1, r) + out)))

    conv_finish(0, PX, F, 2, act, functools.partial(halo_start, 0, PY))
    hand_on(Y1)
    conv_local(0, PE, FT, 0)
    for r in range(DH):
        widen(0, r, made[0, E1, :, pl.ds(r * W, W)].astype(f32))
    conv_local(0, PY, G, 2)
    wgrad_inner(0, PU, 0)

    halo_arrived(0, PE)

    def act(r, p, h, out):
        v = made[0, R2, :, lanes(r * W, W)].astype(f32)
        keep(0, E2, r, staged(G2, r) + slope(v) * out)

    conv_finish(0, PE, FT, 0, act)
    hand_on(E2)
    halo_arrived(0, PU)

    def rest_in(side, slot, peer):
        for h in range(H):
            v = rest[slot, :, pl.ds(h * W, W)].astype(f32)
            put_at(0, PU, near_q(side), h, silu(v))

    over(sides, rest_in)
    conv_finish(0, PU, F, 1, lambda r, p, h, out: keep(0, R1, r, staged(O1, r) - out))
    hand_on(R1)
    halo_arrived(0, PY)
    conv_finish(0, PY, G, 2, lambda r, p, h, out: keep(0, Y2, r, staged(X2, r) + out))
    hand_on(Y2)
    hand_on_far()
    wgrad_outer(0, PU, 0)

    def got(k, r):
        return second[k, :, lanes(r * W, W)].astype(f32)

    def near(k, side, slot, h):
        return edge[k, slot, :, lanes((1 - side) * HW + h * W, W)].astype(f32)

    @pl.when(relayed)
    def _():
        for k in (G1, O2):
            to_seg(k).wait_recv()
            edge_start(second.at[k], k, False, seg, 3)

    def forward_own():
        arrived(X2)
        for r in range(DH):
            put(1, PX, r, silu(got(X2, r)))
        conv_local(1, PX, F, 2)

    def forward():
        arrived(X1)

        def edges(side, slot, peer):
            edge_arrived(X2, False, side, slot, peer)
            for h in range(H):
                put_at(1, PX, near_q(side), h, silu(near(X2, side, slot, h)))

        over(sides, edges)

        def act(r, p, h, out):
            put_at(1, PY, p, h, silu(keep(1, Y1, r, got(X1, r) + out)))

        conv_finish(1, PX, F, 2, act, functools.partial(halo_start, 1, PY))
        give_out(Y1)
        conv_local(1, PY, G, 2)

    arrived(G2)
    far_relay(G2)

    pl.when(odd)(forward_own)
    for d in range(D):
        pad[1, PD, :, pl.ds(lane(d, 1), HW)] = second[G2, :, pl.ds(d * HW, HW)]
    conv_local(1, PD, GT, 0)
    arrived(O1)
    far_relay(O1)

    for r in range(DH):
        put(1, PH, r, silu(got(O1, r)))
    conv_local(1, PH, G, 1)
    for r in range(DH):
        widen(1, r, got(G2, r))
    wgrad_inner(1, PH, 1)
    pl.when(odd)(forward)

    def edge_q(far, side):
        return near_q(side) + (2 * side - 1 if far else 0), (side if far else 1 - side) * HW

    def grad_in(far, side, slot, peer):
        q, at = edge_q(far, side)
        edge_arrived(G2, far, side, slot, peer)
        pad[1, PD, :, lanes(lane(q, 1), HW)] = edge[G2, slot, :, lanes(at, HW)]

    def act_in(far, side, slot, peer):
        q, at = edge_q(far, side)
        edge_arrived(O1, far, side, slot, peer)
        for h in range(H):
            put_at(1, PH, q, h, silu(edge[O1, slot, :, lanes(at + h * W, W)].astype(f32)))

    over(sides, functools.partial(grad_in, False))
    over(sides, functools.partial(act_in, False))
    arrived(G1)

    def act(r, p, h, out):
        put_at(1, PE, p, h, keep(1, E1, r, got(G1, r) + slope(got(O1, r)) * out))

    conv_finish(1, PD, GT, 0, act)
    arrived(O2)

    def act(r, p, h, out):
        put_at(1, PU, p, h, silu(keep(1, R2, r, got(O2, r) - out)))

    conv_finish(1, PH, G, 1, act)

    def give_first():
        give_out(E1)
        give_out(R2)

    pl.when(even)(give_first)
    wgrad_outer(1, PH, 1)
    wgrad_share(1)

    def beyond_act(side, slot, peer):
        act_in(True, side, slot, peer)
        edge_arrived(O2, False, side, slot, peer)
        q = near_q(side)
        for h, out in rows_of(taps(1, PH, G, q, range(3))):
            value = (near(O2, side, slot, h) - out).astype(bf16).astype(f32)
            put_at(1, PU, q, h, silu(value))

    over(sides, beyond_act)
    for r in range(DH):
        widen(0, r, made[1, E1, :, pl.ds(r * W, W)].astype(f32))
    wgrad_whole(PU, 0)
    wgrad_share(0)

    def beyond_grad(side, slot, peer):
        grad_in(True, side, slot, peer)
        edge_arrived(G1, False, side, slot, peer)
        q = near_q(side)
        for h, out in rows_of(taps(1, PD, GT, q, range(3))):
            value = near(G1, side, slot, h) + slope(near(O1, side, slot, h)) * out
            put_at(1, PE, q, h, value)

    over(sides, beyond_grad)
    pl.when(odd)(give_first)


    for r, out in conv_whole(1, PE, FT):
        v = made[1, R2, :, pl.ds(r * W, W)].astype(f32)
        keep(1, E2, r, got(G2, r) + slope(v) * out)
    give_out(E2)
    for r, out in conv_whole(1, PU, F):
        keep(1, R1, r, got(O1, r) - out)
    give_out(R1)

    def gradients():
        for j in (1, 0):
            for q in range(1, n):
                share(j, q).wait_recv()
            for ab in range(9):
                own = dsum[j, pl.ds(pl.multiple_of(ab * C + slab * cs, 8), cs)]
                total = jnp.concatenate([own, jnp.zeros((cs, LW - 3 * C), f32)], axis=1)
                for q in range(1, n):
                    total += dgot[j, q - 1, ab].astype(f32)
                total *= scale
                for c in range(3):
                    tap = total if c == 0 else pltpu.roll(total, LW - c * C, 1)
                    dt[j, pl.ds(3 * ab + c, cs, stride=27), :] = tap
            dw[j] = dt[j].T[:C]

    @pl.when(even)
    def _():
        forward_own()
        forward()
        gradients()

    halo_arrived(1, PY)
    conv_finish(1, PY, G, 2, lambda r, p, h, out: keep(1, Y2, r, got(X2, r) + out))
    give_out(Y2)
    pl.when(odd)(gradients)

    def drain_edges(which, first, fewer, more):
        def act(side, slot, peer):
            direct = straight(first, side)
            sem = edge_s.at[which, slot]
            pl.when(direct)(lambda: drain(sem, planes_of(more)))
            pl.when(jnp.logical_not(direct))(lambda: drain(sem, planes_of(fewer)))

        over(toward, act)

    over(toward, lambda side, slot, peer: drain(halo_s.at[slot], planes_of(7)))
    for q in range(1, n):
        drain(d_s.at[q - 1], dpart.at[:, 0])
    pltpu.make_async_copy(nat.at[pl.ds(Y1, 2)], fout, out_s.at[0]).wait()

    @pl.when(is_first)
    def _():
        over(toward, lambda side, slot, peer: drain(edge_s.at[2, slot], planes_of(1)))

    @pl.when(is_last)
    def _():
        pltpu.make_async_copy(nat.at[pl.ds(0, 4)], nat.at[pl.ds(0, 4)], out_s.at[1]).wait()
        over(toward, lambda side, slot, peer: drain(edge_s.at[2, slot], planes_of(6)))

    @pl.when(has_next)
    def _():
        drain(seg_s.at[1], made.at[0, pl.ds(0, 2)])
        over(toward, lambda side, slot, peer: drain(edge_s.at[1, slot], planes_of(1)))
        drain(back_r.at[0], nat.at[pl.ds(R1, 4)])

    @pl.when(has_prev)
    def _():
        drain(seg_s.at[0], made.at[0, pl.ds(0, 4)])
        drain(back_s.at[0], nat.at[pl.ds(R1, 4)])

        @pl.when(even)
        def _():
            drain_edges(0, 2, 2, 4)

    @pl.when(odd)
    def _():
        over(toward, lambda side, slot, peer: drain(edge_s.at[0, slot], planes_of(4)))
        over(sides, lambda side, slot, peer: drain(pass_s.at[slot], planes_of(2)))

    @pl.when(relayed)
    def _():
        drain_edges(3, 1, 4, 2)


def write_out(*refs):
    srcs, dsts, sems = refs[:4], refs[4:8], refs[8]
    writes = [pltpu.make_async_copy(a, b, sems.at[i]) for i, (a, b) in enumerate(zip(srcs, dsts))]
    for write in writes:
        write.start()
    for write in writes:
        write.wait()


def local(segs, n, fwd_in, back_out, back_grad, batch_next, loss_grad, weights):
    _, _, C, D, H, W = fwd_in.shape
    rows = C * D * H
    cs = C // n
    ends = 1 if n == 2 else 2
    f32, bf16 = jnp.float32, jnp.bfloat16
    scale = float(D * n * H * W) ** (-0.5)
    vmem = pl.BlockSpec(memory_space=pltpu.VMEM)
    hbm = pl.BlockSpec(memory_space=pltpu.HBM)
    wide = pl.cdiv(3 * C, 128) * 128
    anywhere = pl.BlockSpec(memory_space=pl.ANY)
    pair = jax.ShapeDtypeStruct((2, rows, W), bf16)
    share = jax.ShapeDtypeStruct((2, C, 27 * cs), f32)
    dma = pltpu.SemaphoreType.DMA
    fout, backs, grads, dw = pl.pallas_call(
        functools.partial(kernel, (C, D, H, W, segs, n, scale)),
        out_shape=tuple(pltpu.VMEM(x.shape, x.dtype) for x in (pair, pair, pair, share)),
        in_specs=[hbm] * 6,
        out_specs=(vmem, vmem, vmem, vmem),
        scratch_shapes=[
            pltpu.VMEM((2, rows, W), bf16),
            pltpu.VMEM((2, rows, W), bf16),
            pltpu.VMEM((2, rows, W), bf16),
            pltpu.VMEM((2, rows, W), bf16),
            pltpu.VMEM((4, rows, W), bf16),
            pltpu.VMEM((2 * C, 27 * C), bf16),
            pltpu.VMEM((27 * C, wide), f32),
            pltpu.VMEM((4, 3, 3 * C, 3 * C), bf16),
            pltpu.VMEM((4, 2, 3 * C, 6 * C), bf16),
            pltpu.VMEM((2, 27 * cs, wide), f32),
            pltpu.VMEM((2, 6, C, (D + 4) * (H + 2) * W), bf16),
            pltpu.VMEM((8, rows, W), f32),
            pltpu.VMEM((6, C, D * H * W), bf16),
            pltpu.VMEM((6, ends, C, 2 * H * W), bf16),
            pltpu.VMEM((ends, C, H * W), bf16),
            pltpu.VMEM((2, 6, C, D * H * W), bf16),
            pltpu.VMEM((6, rows, W), bf16),
            pltpu.VMEM((3, 3 * C, D * H * W), f32),
            pltpu.VMEM((2, 3 * C, D * H * W), bf16),
            pltpu.VMEM((2, 9 * C, 3 * C), f32),
            pltpu.VMEM((2, n - 1, 9, cs, wide), bf16),
            pltpu.VMEM((2, n - 1, 9, cs, wide), bf16),
            dma((ends,)),
            dma((7, ends)),
            dma((2,)),
            dma((6,)),
            dma((1,)),
            dma((1,)),
            dma((4, ends)),
            dma((7, ends)),
            dma((ends,)),
            dma((2,)),
            dma((n - 1,)),
            dma((2, n - 1)),
            dma((6,)),
            pltpu.SemaphoreType.REGULAR((2,)),
        ],
        compiler_params=pltpu.CompilerParams(
            collective_id=0, has_side_effects=True, vmem_limit_bytes=48 << 20
        ),
        name="petra",
    )(
        *[
            pltpu.with_memory_space_constraint(x, pltpu.HBM)
            for x in (
                fwd_in.reshape(2, rows, W),
                back_out.reshape(2, rows, W),
                back_grad.reshape(2, rows, W),
                batch_next.reshape(2, rows, W),
                loss_grad.reshape(4, rows, W),
                weights.reshape(2 * C, 27 * C),
            )
        ]
    )
    fout, backs, grads, dw = pl.pallas_call(
        write_out,
        out_shape=(pair, pair, pair, share),
        in_specs=[vmem] * 4,
        out_specs=(hbm,) * 4,
        scratch_shapes=[dma((4,))],
        compiler_params=pltpu.CompilerParams(vmem_limit_bytes=4 << 20),
        name="write_out",
    )(fout, backs, grads, dw)
    shape = fwd_in.shape
    return fout.reshape(shape), backs.reshape(shape), grads.reshape(shape), dw[None]


def solution(mesh):
    field = P("segment", None, None, "slab", None, None)
    return jax.shard_map(
        functools.partial(local, mesh.shape["segment"], mesh.shape["slab"]),
        mesh=mesh,
        in_specs=(
            field,
            field,
            field,
            P(None, None, "slab", None, None),
            P(None, None, None, "slab", None, None),
            P("segment", None, None, None),
        ),
        out_specs=(field, field, field, P("segment", None, None, "slab")),
        check_vma=False,
    )
```

```python
import functools

import jax
import jax.numpy as jnp
from jax import lax
from jax.experimental import pallas as pl
from jax.experimental.pallas import tpu as pltpu
from jax.sharding import PartitionSpec as P

MESH = pl.DeviceIdType.MESH
F, G, FT, GT = range(4)
X1, X2, O1, O2, G1, G2 = range(6)
Y1, Y2, R1, R2, E1, E2 = range(6)
PX, PH, PD, PY, PU, PE = range(6)


def sigmoid(v):
    return 1.0 / (1.0 + jnp.exp(-v))


def silu(v):
    return v / (1.0 + jnp.exp(-v))


def slope(v):
    sig = sigmoid(v)
    return sig * (1.0 + v * (1.0 - sig))


def kernel(
    dims, fwd_hbm, bout_hbm, bgrad_hbm, nxt_hbm, loss_hbm, kern_hbm, fout, backs, grads, dw,
    fwd, bout, bgrad, nxt, loss, kern, kt, w, pairs, dt, pad, stage, second, edge, rest, made, nat, acc,
    g3, dsum, dpart, dgot, halo_s, halo_r, seg_s, seg_r, back_s, back_r, edge_s, edge_r, pass_s,
    out_s, d_s, d_r, in_s, ready_s,
):
    C, D, H, W, segs, n, scale = dims
    DH, HW = D * H, H * W
    cs = C // n
    LW = pl.cdiv(3 * C, 128) * 128
    f32, bf16 = jnp.float32, jnp.bfloat16
    seg = lax.axis_index("segment")
    slab = lax.axis_index("slab")
    has_prev, has_next = seg > 0, seg < segs - 1
    is_first, is_last = seg == 0, seg == segs - 1
    odd, even = lax.rem(seg, 2) == 1, lax.rem(seg, 2) == 0
    relayed = jnp.logical_and(has_next, odd)
    whole = jnp.logical_and(has_next, even)
    prev_seg = lax.rem(seg + segs - 1, segs)
    next_seg = lax.rem(seg + 1, segs)
    lane_no = lax.broadcasted_iota(jnp.int32, (C, W), 1)

    if n == 2:
        sides = [(None, 1 - slab, 0, 1 - slab)]
        toward = [(None, slab, 0, 1 - slab)]
    else:
        below, above = lax.rem(slab + n - 1, n), lax.rem(slab + 1, n)
        sides = [(slab > 0, 0, 0, below), (slab < n - 1, 1, 1, above)]
        toward = [(slab < n - 1, 0, 0, above), (slab > 0, 1, 1, below)]

    def over(rows, act):
        for there, side, slot, peer in rows:
            if there is None:
                act(side, slot, peer)
            else:
                pl.when(there)(functools.partial(act, side, slot, peer))

    def near_q(side):
        return side * (D + 1) - 1

    barrier = pltpu.get_barrier_semaphore()

    for k in range(1, n):
        pl.semaphore_signal(
            barrier, inc=1, device_id={"slab": lax.rem(slab + k, n)}, device_id_type=MESH
        )

    @pl.when(has_prev)
    def _():
        pl.semaphore_signal(barrier, inc=1, device_id={"segment": prev_seg}, device_id_type=MESH)

    @pl.when(has_next)
    def _():
        pl.semaphore_signal(barrier, inc=1, device_id={"segment": next_seg}, device_id_type=MESH)

    fetches = [
        pltpu.make_async_copy(src, dst, in_s.at[i])
        for i, (src, dst) in enumerate(
            [
                (bgrad_hbm, bgrad), (bout_hbm, bout), (fwd_hbm, fwd),
                (kern_hbm, kern), (nxt_hbm, nxt), (loss_hbm, loss),
            ]
        )
    ]
    for fetch in fetches:
        fetch.start()

    def lanes(at, size):
        return pl.ds(at if isinstance(at, int) else pl.multiple_of(at, W), size)

    def lane(q, hh):
        return ((q + 2) * (H + 2) + hh) * W

    zero = jnp.zeros((C, W), bf16)
    for t in range(2):
        for k in range(6):
            reach = 2 if t == 1 and k in (PH, PD) else 1
            for q in range(-reach, D + reach):
                for hh in (0, H + 1):
                    pad[t, k, :, pl.ds(lane(q, hh), W)] = zero

    for q, missing in ((-1, slab == 0), (D, slab == n - 1)):
        @pl.when(missing)
        def _():
            for t in range(2):
                for k in range(6):
                    pad[t, k, :, pl.ds(lane(q, 1), HW)] = jnp.zeros((C, HW), bf16)

    def load_stage(slot, ref, s):
        stage[slot] = ref[s].astype(f32)

    def staged(slot, r):
        return stage[slot, pl.ds(r, C, stride=DH), :]

    def prepare_weights():
        fetches[3].wait()
        wide = kern[...].astype(f32)
        kt[...] = jnp.concatenate([wide, jnp.zeros((LW - 2 * C, 27 * C), f32)], axis=0).T

        def tap(t):
            return kt[pl.ds(t, C, stride=27), :]

        def set_weights(m, a, c, block):
            here = pl.ds(c * C, C)
            w[m, a, here, :] = block
            if a < 2:
                pairs[m, a, here, 0 : 3 * C] = block
            if a > 0:
                pairs[m, a - 1, here, 3 * C : 6 * C] = block

        for a in range(3):
            for c in range(3):
                block = jnp.concatenate([tap(9 * a + 3 * b + c) for b in range(3)], axis=0).T
                for f in range(2):
                    set_weights(F + f, a, c, block[f * C : (f + 1) * C].astype(bf16))
                for f in range(2):
                    turned = jnp.concatenate(
                        [
                            tap(9 * (2 - a) + 3 * (2 - b) + 2 - c)[:, f * C : (f + 1) * C]
                            for b in range(3)
                        ],
                        axis=1,
                    )
                    set_weights(FT + f, a, c, turned.astype(bf16))

    def load_pair(i, slot, ref):
        fetches[i].wait()
        for s in range(2):
            load_stage(slot + s, ref, s)

    def halo(t, k, side, slot, peer):
        if k == PU:
            src = made.at[t, R2, :, lanes((1 - side) * (D - 1) * HW, HW)]
            dst = rest.at[slot]
        else:
            src = pad.at[t, k, :, lanes(lane((1 - side) * (D - 1), 1), HW)]
            dst = pad.at[t, k, :, lanes(lane(near_q(side), 1), HW)]
        return pltpu.make_async_remote_copy(
            src_ref=src, dst_ref=dst, send_sem=halo_s.at[slot], recv_sem=halo_r.at[6 if t else k, slot],
            device_id={"slab": peer}, device_id_type=MESH,
        )

    def halo_start(t, k):
        over(toward, lambda side, slot, peer: halo(t, k, side, slot, peer).start())

    def halo_arrived(t, k):
        over(sides, lambda side, slot, peer: halo(t, k, side, slot, peer).wait_recv())

    def to_seg(k):
        return pltpu.make_async_remote_copy(
            src_ref=made.at[0, k], dst_ref=second.at[k],
            send_sem=seg_s.at[1 if k <= X2 else 0], recv_sem=seg_r.at[k],
            device_id={"segment": next_seg if k <= X2 else prev_seg}, device_id_type=MESH,
        )

    def edge_at(k, far, side, slot):
        return edge.at[k, slot, :, lanes((side if far else 1 - side) * HW, HW)]

    def edge_copy(src, k, far, target, which, side, slot, peer):
        plane = (1 - side) * (D - 2) + side if far else (1 - side) * (D - 1)
        return pltpu.make_async_remote_copy(
            src_ref=src.at[:, lanes(plane * HW, HW)], dst_ref=edge_at(k, far, side, slot),
            send_sem=edge_s.at[which, slot], recv_sem=edge_r.at[k // 2 + 4 if far else k - 1, slot],
            device_id={"segment": target, "slab": peer}, device_id_type=MESH,
        )

    def edge_start(src, k, far, target, which):
        over(toward, lambda *side: edge_copy(src, k, far, target, which, *side).start())

    def edge_arrived(k, far, *side):
        edge_copy(made.at[0, k], k, far, seg, 0, *side).wait_recv()

    def pass_on(k, side, slot, peer):
        if k == G1:
            src = pad.at[0, PE, :, lanes(lane(near_q(side), 1), HW)]
        else:
            src = rest.at[slot]
        return pltpu.make_async_remote_copy(
            src_ref=src, dst_ref=edge_at(k, False, side, slot),
            send_sem=pass_s.at[slot], recv_sem=edge_r.at[k - 1, slot],
            device_id={"segment": prev_seg}, device_id_type=MESH,
        )

    def drain(sem, src):
        pltpu.make_async_remote_copy(
            src_ref=src, dst_ref=src, send_sem=sem, recv_sem=sem,
            device_id={"slab": lax.rem(slab + 1, n)}, device_id_type=MESH,
        ).wait_send()

    def planes_of(count):
        return pad.at[0, 0, :, pl.ds(0, count * HW)]

    def out_prev(k):
        dst = backs.at[k - R1] if k < E1 else grads.at[k - E1]
        return pltpu.make_async_remote_copy(
            src_ref=nat.at[k], dst_ref=dst, send_sem=back_s.at[0], recv_sem=back_r.at[0],
            device_id={"segment": prev_seg}, device_id_type=MESH,
        )

    def own_out(k):
        return pltpu.make_async_copy(nat.at[k], fout.at[k], out_s.at[0])

    def last_act(k):
        return pltpu.make_async_copy(nat.at[k], backs.at[k], out_s.at[1])

    def last_grad(k):
        return pltpu.make_async_copy(loss.at[2 + k], grads.at[k], out_s.at[1])

    def put(t, k, r, value):
        d, h = divmod(r, H)
        put_at(t, k, d, h, value)

    def put_at(t, k, q, h, value):
        pad[t, k, :, lanes(lane(q, h + 1), W)] = value.astype(bf16)

    def tall(t, k, q):
        return jnp.concatenate([pad[t, k, :, lanes(lane(q, b), HW)] for b in range(3)], axis=0)

    def taps(t, k, m, p, which):
        total, which = None, list(which)
        while which:
            a = which.pop(0)
            lhs, rhs = w[m, a], tall(t, k, p + a - 1)
            if which:
                which.pop(0)
                lhs = pairs[m, a]
                rhs = jnp.concatenate([rhs, tall(t, k, p + a)], axis=0)
            part = jnp.dot(lhs, rhs, preferred_element_type=f32)
            total = part if total is None else total + part
        return total

    def inner(p):
        return [a for a in range(3) if 0 <= p + a - 1 < D]

    def conv_local(t, k, m, slot):
        for p in range(D):
            acc[slot, :, pl.ds(p * HW, HW)] = taps(t, k, m, p, inner(p))

    def rows_of(total):
        for h in range(H):
            y = total[:, h * W : (h + 1) * W]
            left = jnp.where(lane_no == 0, 0.0, pltpu.roll(y[:C], 1, 1))
            right = jnp.where(lane_no == W - 1, 0.0, pltpu.roll(y[2 * C :], W - 1, 1))
            yield h, y[C : 2 * C] + left + right

    def conv_finish(t, k, m, slot, act, then=None):
        def outer(side):
            return jnp.dot(w[m, 2 * side], tall(t, k, near_q(side)), preferred_element_type=f32)

        def add(side, at, peer):
            acc[slot, :, lanes(side * (D - 1) * HW, HW)] += outer(side)

        if n > 2:
            over(sides, add)
        for i in range(D):
            p = (1 - slab) * (D - 1) + i * (2 * slab - 1) if n == 2 else i
            total = acc[slot, :, lanes(p * HW, HW)]
            if n == 2 and i == 0:
                total += outer(1 - slab)
            for h, out in rows_of(total):
                act(p * H + h, p, h, out)
            if then is not None and i == (0 if n == 2 else D - 1):
                then()

    def conv_whole(t, k, m):
        for p in range(D):
            for h, out in rows_of(taps(t, k, m, p, range(3))):
                yield p * H + h, out

    def widen(j, r, v):
        at = pl.ds(r * W, W)
        g3[j, 0:C, at] = jnp.where(lane_no == W - 1, 0.0, pltpu.roll(v, W - 1, 1)).astype(bf16)
        g3[j, C : 2 * C, at] = v.astype(bf16)
        g3[j, 2 * C : 3 * C, at] = jnp.where(lane_no == 0, 0.0, pltpu.roll(v, 1, 1)).astype(bf16)

    def product(lhs, j, p):
        return lax.dot_general(
            lhs, g3[j, :, lanes(p * HW, HW)], (((1,), (1,)), ((), ())), preferred_element_type=f32
        )

    def wgrad_inner(t, k, j):
        parts = [None] * 3
        for p in range(D):
            which = inner(p)
            part = product(jnp.concatenate([tall(t, k, p + a - 1) for a in which], axis=0), j, p)
            for i, a in enumerate(which):
                block = part[i * 3 * C : (i + 1) * 3 * C]
                parts[a] = block if parts[a] is None else parts[a] + block
        for a in range(3):
            here = pl.ds(a * 3 * C, 3 * C)
            if t == 0:
                dsum[j, here] = parts[a]
            else:
                dsum[j, here] += parts[a]

    def wgrad_whole(k, j):
        for p in range(D):
            lhs = jnp.concatenate([tall(1, k, p + a - 1) for a in range(3)], axis=0)
            part = product(lhs, j, p)
            total = part if p == 0 else total + part
        dsum[j] += total

    def wgrad_outer(t, k, j):
        def outer(side, slot, peer):
            at = side * 6 * C
            here = pl.ds(at if isinstance(at, int) else pl.multiple_of(at, 8), 3 * C)
            dsum[j, here] += product(tall(t, k, near_q(side)), j, side * (D - 1))

        over(sides, outer)

    def wgrad_share(j):
        for q in range(1, n):
            first = lax.rem(slab + q, n) * cs
            for ab in range(9):
                part = dsum[j, pl.ds(pl.multiple_of(ab * C + first, 8), cs)].astype(bf16)
                dpart[j, q - 1, ab] = jnp.concatenate(
                    [part, jnp.zeros((cs, LW - 3 * C), bf16)], axis=1
                )
            share(j, q).start()

    def share(j, q):
        target = lax.rem(slab + q, n)
        return pltpu.make_async_remote_copy(
            src_ref=dpart.at[j, q - 1], dst_ref=dgot.at[j, q - 1],
            send_sem=d_s.at[q - 1], recv_sem=d_r.at[j, q - 1],
            device_id={"slab": target}, device_id_type=MESH,
        )

    def keep(t, k, r, value):
        held = value.astype(bf16)
        made[t, k, :, lanes(r * W, W)] = held
        wide = held.astype(f32)
        if t == 1:
            stage[k, pl.ds(r, C, stride=DH), :] = wide
        return wide

    def straight(first, side):
        return lax.rem(seg, 4) == first

    def far_direct(side, slot, peer):
        @pl.when(straight(2, side))
        def _():
            for k in (O1, G2):
                edge_copy(made.at[0, k], k, True, prev_seg, 0, side, slot, peer).start()

    def far_relay(k):
        def act(side, slot, peer):
            @pl.when(jnp.logical_not(straight(1, side)))
            def _():
                edge_copy(second.at[k], k, True, seg, 3, side, slot, peer).start()

        @pl.when(relayed)
        def _():
            over(toward, act)

    def hand_on(k):
        src = made.at[0, k]
        if k <= X2:
            @pl.when(has_next)
            def _():
                if k == Y2:
                    edge_start(src, X2, False, next_seg, 1)
                to_seg(k).start()

            @pl.when(is_last)
            def _():
                edge_start(src, O1 + k, False, seg, 2)
                if k == Y1:
                    edge_start(src, O1, True, seg, 2)
                second[O1 + k] = made[0, k]
        else:
            @pl.when(has_prev)
            def _():
                to_seg(k).start()
                if k == O1:
                    edge_start(src, O1, False, prev_seg, 0)
                    edge_start(made.at[0, G2], G2, False, prev_seg, 0)
                    over(toward, far_direct)

    def hand_on_far():
        @pl.when(odd)
        def _():
            for k in (G2, O1):
                edge_start(made.at[0, k], k, True, prev_seg, 0)
            for k in (G1, O2):
                over(sides, lambda *side: pass_on(k, *side).start())

    def give_out(k):
        nat[k] = stage[k].astype(bf16)
        if k < R1:
            own_out(k).start()

            @pl.when(is_last)
            def _():
                last_act(k).start()
        else:
            @pl.when(has_prev)
            def _():
                out_prev(k).start()

    def arrived(k):
        there = has_prev if k <= X2 else whole if k in (G1, O2) else has_next

        @pl.when(there)
        def _():
            to_seg(k).wait_recv()

    load_pair(0, G1, bgrad)
    for r in range(DH):
        put(0, PD, r, staged(G2, r))
    peers = has_prev.astype(jnp.int32) + has_next.astype(jnp.int32) + n - 1
    pl.semaphore_wait(barrier, peers)
    halo_start(0, PD)

    @pl.when(has_prev)
    def _():
        pl.semaphore_signal(
            ready_s.at[1], inc=1, device_id={"segment": prev_seg}, device_id_type=MESH
        )

    @pl.when(has_next)
    def _():
        pl.semaphore_signal(
            ready_s.at[0], inc=1, device_id={"segment": next_seg}, device_id_type=MESH
        )

    load_pair(1, O1, bout)
    for r in range(DH):
        put(0, PH, r, silu(staged(O1, r)))
    halo_start(0, PH)
    load_pair(2, X1, fwd)
    for r in range(DH):
        put(0, PX, r, silu(staged(X2, r)))
    halo_start(0, PX)
    prepare_weights()
    conv_local(0, PD, GT, 0)
    conv_local(0, PH, G, 1)
    conv_local(0, PX, F, 2)
    for r in range(DH):
        widen(1, r, staged(G2, r))
    wgrad_inner(0, PH, 1)

    fetches[4].wait()
    fetches[5].wait()

    @pl.when(is_first)
    def _():
        for s in range(2):
            load_stage(6 + s, nxt, s)
            for r in range(DH):
                second[X1 + s, :, pl.ds(r * W, W)] = staged(6 + s, r).astype(bf16)
        edge_start(second.at[X2], X2, False, seg, 2)

    @pl.when(is_last)
    def _():
        for s in range(2):
            last_grad(s).start()
            load_stage(6 + s, loss, s)
            for r in range(DH):
                second[G1 + s, :, pl.ds(r * W, W)] = staged(6 + s, r).astype(bf16)
            edge_start(second.at[G1 + s], G1 + s, False, seg, 2)
        edge_start(second.at[G2], G2, True, seg, 2)

    @pl.when(has_prev)
    def _():
        pl.semaphore_wait(ready_s.at[0], 1)

    @pl.when(has_next)
    def _():
        pl.semaphore_wait(ready_s.at[1], 1)

    halo_arrived(0, PD)

    def act(r, p, h, out):
        put_at(0, PE, p, h, keep(0, E1, r, staged(G1, r) + slope(staged(O1, r)) * out))

    conv_finish(0, PD, GT, 0, act, functools.partial(halo_start, 0, PE))
    hand_on(E1)
    halo_arrived(0, PH)

    def act(r, p, h, out):
        put_at(0, PU, p, h, silu(keep(0, R2, r, staged(O2, r) - out)))

    conv_finish(0, PH, G, 1, act, functools.partial(halo_start, 0, PU))
    hand_on(R2)
    conv_local(0, PU, F, 1)
    wgrad_outer(0, PH, 1)
    halo_arrived(0, PX)

    def act(r, p, h, out):
        put_at(0, PY, p, h, silu(keep(0, Y1, r, staged(X1, r) + out)))

    conv_finish(0, PX, F, 2, act, functools.partial(halo_start, 0, PY))
    hand_on(Y1)
    conv_local(0, PE, FT, 0)
    for r in range(DH):
        widen(0, r, made[0, E1, :, pl.ds(r * W, W)].astype(f32))
    conv_local(0, PY, G, 2)
    wgrad_inner(0, PU, 0)

    halo_arrived(0, PE)

    def act(r, p, h, out):
        v = made[0, R2, :, lanes(r * W, W)].astype(f32)
        keep(0, E2, r, staged(G2, r) + slope(v) * out)

    conv_finish(0, PE, FT, 0, act)
    hand_on(E2)
    halo_arrived(0, PU)

    def rest_in(side, slot, peer):
        for h in range(H):
            v = rest[slot, :, pl.ds(h * W, W)].astype(f32)
            put_at(0, PU, near_q(side), h, silu(v))

    over(sides, rest_in)
    conv_finish(0, PU, F, 1, lambda r, p, h, out: keep(0, R1, r, staged(O1, r) - out))
    hand_on(R1)
    halo_arrived(0, PY)
    conv_finish(0, PY, G, 2, lambda r, p, h, out: keep(0, Y2, r, staged(X2, r) + out))
    hand_on(Y2)
    hand_on_far()
    wgrad_outer(0, PU, 0)

    def got(k, r):
        return second[k, :, lanes(r * W, W)].astype(f32)

    def near(k, side, slot, h):
        return edge[k, slot, :, lanes((1 - side) * HW + h * W, W)].astype(f32)

    @pl.when(relayed)
    def _():
        for k in (G1, O2):
            to_seg(k).wait_recv()
            edge_start(second.at[k], k, False, seg, 3)

    def forward_own():
        arrived(X2)
        for r in range(DH):
            put(1, PX, r, silu(got(X2, r)))
        conv_local(1, PX, F, 2)

    def forward():
        arrived(X1)

        def edges(side, slot, peer):
            edge_arrived(X2, False, side, slot, peer)
            for h in range(H):
                put_at(1, PX, near_q(side), h, silu(near(X2, side, slot, h)))

        over(sides, edges)

        def act(r, p, h, out):
            put_at(1, PY, p, h, silu(keep(1, Y1, r, got(X1, r) + out)))

        conv_finish(1, PX, F, 2, act, functools.partial(halo_start, 1, PY))
        give_out(Y1)
        conv_local(1, PY, G, 2)

    arrived(G2)
    far_relay(G2)

    pl.when(odd)(forward_own)
    for d in range(D):
        pad[1, PD, :, pl.ds(lane(d, 1), HW)] = second[G2, :, pl.ds(d * HW, HW)]
    conv_local(1, PD, GT, 0)
    arrived(O1)
    far_relay(O1)

    for r in range(DH):
        put(1, PH, r, silu(got(O1, r)))
    conv_local(1, PH, G, 1)
    for r in range(DH):
        widen(1, r, got(G2, r))
    wgrad_inner(1, PH, 1)
    pl.when(odd)(forward)

    def edge_q(far, side):
        return near_q(side) + (2 * side - 1 if far else 0), (side if far else 1 - side) * HW

    def grad_in(far, side, slot, peer):
        q, at = edge_q(far, side)
        edge_arrived(G2, far, side, slot, peer)
        pad[1, PD, :, lanes(lane(q, 1), HW)] = edge[G2, slot, :, lanes(at, HW)]

    def act_in(far, side, slot, peer):
        q, at = edge_q(far, side)
        edge_arrived(O1, far, side, slot, peer)
        for h in range(H):
            put_at(1, PH, q, h, silu(edge[O1, slot, :, lanes(at + h * W, W)].astype(f32)))

    over(sides, functools.partial(act_in, False))
    arrived(O2)

    def act(r, p, h, out):
        put_at(1, PU, p, h, silu(keep(1, R2, r, got(O2, r) - out)))

    conv_finish(1, PH, G, 1, act)
    over(sides, functools.partial(grad_in, False))
    arrived(G1)

    def act(r, p, h, out):
        put_at(1, PE, p, h, keep(1, E1, r, got(G1, r) + slope(got(O1, r)) * out))

    conv_finish(1, PD, GT, 0, act)

    def give_first():
        give_out(E1)
        give_out(R2)

    pl.when(even)(give_first)
    wgrad_outer(1, PH, 1)
    wgrad_share(1)

    def beyond_act(side, slot, peer):
        act_in(True, side, slot, peer)
        edge_arrived(O2, False, side, slot, peer)
        q = near_q(side)
        for h, out in rows_of(taps(1, PH, G, q, range(3))):
            value = (near(O2, side, slot, h) - out).astype(bf16).astype(f32)
            put_at(1, PU, q, h, silu(value))

    over(sides, beyond_act)
    for r in range(DH):
        widen(0, r, made[1, E1, :, pl.ds(r * W, W)].astype(f32))
    wgrad_whole(PU, 0)
    wgrad_share(0)

    def beyond_grad(side, slot, peer):
        grad_in(True, side, slot, peer)
        edge_arrived(G1, False, side, slot, peer)
        q = near_q(side)
        for h, out in rows_of(taps(1, PD, GT, q, range(3))):
            value = near(G1, side, slot, h) + slope(near(O1, side, slot, h)) * out
            put_at(1, PE, q, h, value)

    over(sides, beyond_grad)
    pl.when(odd)(give_first)


    for r, out in conv_whole(1, PE, FT):
        v = made[1, R2, :, pl.ds(r * W, W)].astype(f32)
        keep(1, E2, r, got(G2, r) + slope(v) * out)
    give_out(E2)
    for r, out in conv_whole(1, PU, F):
        keep(1, R1, r, got(O1, r) - out)
    give_out(R1)

    def gradients():
        for j in (1, 0):
            for q in range(1, n):
                share(j, q).wait_recv()
            for ab in range(9):
                own = dsum[j, pl.ds(pl.multiple_of(ab * C + slab * cs, 8), cs)]
                total = jnp.concatenate([own, jnp.zeros((cs, LW - 3 * C), f32)], axis=1)
                for q in range(1, n):
                    total += dgot[j, q - 1, ab].astype(f32)
                total *= scale
                for c in range(3):
                    tap = total if c == 0 else pltpu.roll(total, LW - c * C, 1)
                    dt[j, pl.ds(3 * ab + c, cs, stride=27), :] = tap
            dw[j] = dt[j].T[:C]

    @pl.when(even)
    def _():
        forward_own()
        forward()
        gradients()

    halo_arrived(1, PY)
    conv_finish(1, PY, G, 2, lambda r, p, h, out: keep(1, Y2, r, got(X2, r) + out))
    give_out(Y2)
    pl.when(odd)(gradients)

    def drain_edges(which, first, fewer, more):
        def act(side, slot, peer):
            direct = straight(first, side)
            sem = edge_s.at[which, slot]
            pl.when(direct)(lambda: drain(sem, planes_of(more)))
            pl.when(jnp.logical_not(direct))(lambda: drain(sem, planes_of(fewer)))

        over(toward, act)

    over(toward, lambda side, slot, peer: drain(halo_s.at[slot], planes_of(7)))
    for q in range(1, n):
        drain(d_s.at[q - 1], dpart.at[:, 0])
    pltpu.make_async_copy(nat.at[pl.ds(Y1, 2)], fout, out_s.at[0]).wait()

    @pl.when(is_first)
    def _():
        over(toward, lambda side, slot, peer: drain(edge_s.at[2, slot], planes_of(1)))

    @pl.when(is_last)
    def _():
        pltpu.make_async_copy(nat.at[pl.ds(0, 4)], nat.at[pl.ds(0, 4)], out_s.at[1]).wait()
        over(toward, lambda side, slot, peer: drain(edge_s.at[2, slot], planes_of(6)))

    @pl.when(has_next)
    def _():
        drain(seg_s.at[1], made.at[0, pl.ds(0, 2)])
        over(toward, lambda side, slot, peer: drain(edge_s.at[1, slot], planes_of(1)))
        drain(back_r.at[0], nat.at[pl.ds(R1, 4)])

    @pl.when(has_prev)
    def _():
        drain(seg_s.at[0], made.at[0, pl.ds(0, 4)])
        drain(back_s.at[0], nat.at[pl.ds(R1, 4)])

        @pl.when(even)
        def _():
            drain_edges(0, 2, 2, 4)

    @pl.when(odd)
    def _():
        over(toward, lambda side, slot, peer: drain(edge_s.at[0, slot], planes_of(4)))
        over(sides, lambda side, slot, peer: drain(pass_s.at[slot], planes_of(2)))

    @pl.when(relayed)
    def _():
        drain_edges(3, 1, 4, 2)


def write_out(*refs):
    srcs, dsts, sems = refs[:4], refs[4:8], refs[8]
    writes = [pltpu.make_async_copy(a, b, sems.at[i]) for i, (a, b) in enumerate(zip(srcs, dsts))]
    for write in writes:
        write.start()
    for write in writes:
        write.wait()


def local(segs, n, fwd_in, back_out, back_grad, batch_next, loss_grad, weights):
    _, _, C, D, H, W = fwd_in.shape
    rows = C * D * H
    cs = C // n
    ends = 1 if n == 2 else 2
    f32, bf16 = jnp.float32, jnp.bfloat16
    scale = float(D * n * H * W) ** (-0.5)
    vmem = pl.BlockSpec(memory_space=pltpu.VMEM)
    hbm = pl.BlockSpec(memory_space=pltpu.HBM)
    wide = pl.cdiv(3 * C, 128) * 128
    anywhere = pl.BlockSpec(memory_space=pl.ANY)
    pair = jax.ShapeDtypeStruct((2, rows, W), bf16)
    share = jax.ShapeDtypeStruct((2, C, 27 * cs), f32)
    dma = pltpu.SemaphoreType.DMA
    fout, backs, grads, dw = pl.pallas_call(
        functools.partial(kernel, (C, D, H, W, segs, n, scale)),
        out_shape=tuple(pltpu.VMEM(x.shape, x.dtype) for x in (pair, pair, pair, share)),
        in_specs=[hbm] * 6,
        out_specs=(vmem, vmem, vmem, vmem),
        scratch_shapes=[
            pltpu.VMEM((2, rows, W), bf16),
            pltpu.VMEM((2, rows, W), bf16),
            pltpu.VMEM((2, rows, W), bf16),
            pltpu.VMEM((2, rows, W), bf16),
            pltpu.VMEM((4, rows, W), bf16),
            pltpu.VMEM((2 * C, 27 * C), bf16),
            pltpu.VMEM((27 * C, wide), f32),
            pltpu.VMEM((4, 3, 3 * C, 3 * C), bf16),
            pltpu.VMEM((4, 2, 3 * C, 6 * C), bf16),
            pltpu.VMEM((2, 27 * cs, wide), f32),
            pltpu.VMEM((2, 6, C, (D + 4) * (H + 2) * W), bf16),
            pltpu.VMEM((8, rows, W), f32),
            pltpu.VMEM((6, C, D * H * W), bf16),
            pltpu.VMEM((6, ends, C, 2 * H * W), bf16),
            pltpu.VMEM((ends, C, H * W), bf16),
            pltpu.VMEM((2, 6, C, D * H * W), bf16),
            pltpu.VMEM((6, rows, W), bf16),
            pltpu.VMEM((3, 3 * C, D * H * W), f32),
            pltpu.VMEM((2, 3 * C, D * H * W), bf16),
            pltpu.VMEM((2, 9 * C, 3 * C), f32),
            pltpu.VMEM((2, n - 1, 9, cs, wide), bf16),
            pltpu.VMEM((2, n - 1, 9, cs, wide), bf16),
            dma((ends,)),
            dma((7, ends)),
            dma((2,)),
            dma((6,)),
            dma((1,)),
            dma((1,)),
            dma((4, ends)),
            dma((7, ends)),
            dma((ends,)),
            dma((2,)),
            dma((n - 1,)),
            dma((2, n - 1)),
            dma((6,)),
            pltpu.SemaphoreType.REGULAR((2,)),
        ],
        compiler_params=pltpu.CompilerParams(
            collective_id=0, has_side_effects=True, vmem_limit_bytes=48 << 20
        ),
        name="petra",
    )(
        *[
            pltpu.with_memory_space_constraint(x, pltpu.HBM)
            for x in (
                fwd_in.reshape(2, rows, W),
                back_out.reshape(2, rows, W),
                back_grad.reshape(2, rows, W),
                batch_next.reshape(2, rows, W),
                loss_grad.reshape(4, rows, W),
                weights.reshape(2 * C, 27 * C),
            )
        ]
    )
    fout, backs, grads, dw = pl.pallas_call(
        write_out,
        out_shape=(pair, pair, pair, share),
        in_specs=[vmem] * 4,
        out_specs=(hbm,) * 4,
        scratch_shapes=[dma((4,))],
        compiler_params=pltpu.CompilerParams(vmem_limit_bytes=4 << 20),
        name="write_out",
    )(fout, backs, grads, dw)
    shape = fwd_in.shape
    return fout.reshape(shape), backs.reshape(shape), grads.reshape(shape), dw[None]


def solution(mesh):
    field = P("segment", None, None, "slab", None, None)
    return jax.shard_map(
        functools.partial(local, mesh.shape["segment"], mesh.shape["slab"]),
        mesh=mesh,
        in_specs=(
            field,
            field,
            field,
            P(None, None, "slab", None, None),
            P(None, None, None, "slab", None, None),
            P("segment", None, None, None),
        ),
        out_specs=(field, field, field, P("segment", None, None, "slab")),
        check_vma=False,
    )
```

```python
import functools

import jax
import jax.numpy as jnp
from jax import lax
from jax.experimental import pallas as pl
from jax.experimental.pallas import tpu as pltpu
from jax.sharding import PartitionSpec as P

MESH = pl.DeviceIdType.MESH
F, G, FT, GT = range(4)
X1, X2, O1, O2, G1, G2 = range(6)
Y1, Y2, R1, R2, E1, E2 = range(6)
PX, PH, PD, PY, PU, PE = range(6)


def sigmoid(v):
    return 1.0 / (1.0 + jnp.exp(-v))


def silu(v):
    return v / (1.0 + jnp.exp(-v))


def slope(v):
    sig = sigmoid(v)
    return sig * (1.0 + v * (1.0 - sig))


def kernel(
    dims, fwd_hbm, bout_hbm, bgrad_hbm, nxt_hbm, loss_hbm, kern_hbm, fout, backs, grads, dw,
    fwd, bout, bgrad, nxt, loss, kern, kt, w, pairs, dt, pad, stage, second, edge, rest, made, nat, acc,
    g3, dsum, dpart, dgot, halo_s, halo_r, seg_s, seg_r, back_s, back_r, edge_s, edge_r, pass_s,
    out_s, d_s, d_r, in_s, ready_s,
):
    C, D, H, W, segs, n, scale = dims
    DH, HW = D * H, H * W
    cs = C // n
    LW = pl.cdiv(3 * C, 128) * 128
    f32, bf16 = jnp.float32, jnp.bfloat16
    seg = lax.axis_index("segment")
    slab = lax.axis_index("slab")
    has_prev, has_next = seg > 0, seg < segs - 1
    is_first, is_last = seg == 0, seg == segs - 1
    odd, even = lax.rem(seg, 2) == 1, lax.rem(seg, 2) == 0
    relayed = jnp.logical_and(has_next, odd)
    whole = jnp.logical_and(has_next, even)
    prev_seg = lax.rem(seg + segs - 1, segs)
    next_seg = lax.rem(seg + 1, segs)
    lane_no = lax.broadcasted_iota(jnp.int32, (C, W), 1)

    if n == 2:
        sides = [(None, 1 - slab, 0, 1 - slab)]
        toward = [(None, slab, 0, 1 - slab)]
    else:
        below, above = lax.rem(slab + n - 1, n), lax.rem(slab + 1, n)
        sides = [(slab > 0, 0, 0, below), (slab < n - 1, 1, 1, above)]
        toward = [(slab < n - 1, 0, 0, above), (slab > 0, 1, 1, below)]

    def over(rows, act):
        for there, side, slot, peer in rows:
            if there is None:
                act(side, slot, peer)
            else:
                pl.when(there)(functools.partial(act, side, slot, peer))

    def near_q(side):
        return side * (D + 1) - 1

    barrier = pltpu.get_barrier_semaphore()

    for k in range(1, n):
        pl.semaphore_signal(
            barrier, inc=1, device_id={"slab": lax.rem(slab + k, n)}, device_id_type=MESH
        )

    @pl.when(has_prev)
    def _():
        pl.semaphore_signal(barrier, inc=1, device_id={"segment": prev_seg}, device_id_type=MESH)

    @pl.when(has_next)
    def _():
        pl.semaphore_signal(barrier, inc=1, device_id={"segment": next_seg}, device_id_type=MESH)

    fetches = [
        pltpu.make_async_copy(src, dst, in_s.at[i])
        for i, (src, dst) in enumerate(
            [
                (bgrad_hbm, bgrad), (bout_hbm, bout), (fwd_hbm, fwd),
                (kern_hbm, kern), (nxt_hbm, nxt), (loss_hbm, loss),
            ]
        )
    ]
    for fetch in fetches:
        fetch.start()

    def lanes(at, size):
        return pl.ds(at if isinstance(at, int) else pl.multiple_of(at, W), size)

    def lane(q, hh):
        return ((q + 2) * (H + 2) + hh) * W

    zero = jnp.zeros((C, W), bf16)
    for t in range(2):
        for k in range(6):
            reach = 2 if t == 1 and k in (PH, PD) else 1
            for q in range(-reach, D + reach):
                for hh in (0, H + 1):
                    pad[t, k, :, pl.ds(lane(q, hh), W)] = zero

    for q, missing in ((-1, slab == 0), (D, slab == n - 1)):
        @pl.when(missing)
        def _():
            for t in range(2):
                for k in range(6):
                    pad[t, k, :, pl.ds(lane(q, 1), HW)] = jnp.zeros((C, HW), bf16)

    def load_stage(slot, ref, s):
        stage[slot] = ref[s].astype(f32)

    def staged(slot, r):
        return stage[slot, pl.ds(r, C, stride=DH), :]

    def prepare_weights():
        fetches[3].wait()
        wide = kern[...].astype(f32)
        kt[...] = jnp.concatenate([wide, jnp.zeros((LW - 2 * C, 27 * C), f32)], axis=0).T

        def tap(t):
            return kt[pl.ds(t, C, stride=27), :]

        def set_weights(m, a, c, block):
            here = pl.ds(c * C, C)
            w[m, a, here, :] = block
            if a < 2:
                pairs[m, a, here, 0 : 3 * C] = block
            if a > 0:
                pairs[m, a - 1, here, 3 * C : 6 * C] = block

        for a in range(3):
            for c in range(3):
                block = jnp.concatenate([tap(9 * a + 3 * b + c) for b in range(3)], axis=0).T
                for f in range(2):
                    set_weights(F + f, a, c, block[f * C : (f + 1) * C].astype(bf16))
                for f in range(2):
                    turned = jnp.concatenate(
                        [
                            tap(9 * (2 - a) + 3 * (2 - b) + 2 - c)[:, f * C : (f + 1) * C]
                            for b in range(3)
                        ],
                        axis=1,
                    )
                    set_weights(FT + f, a, c, turned.astype(bf16))

    def load_pair(i, slot, ref):
        fetches[i].wait()
        for s in range(2):
            load_stage(slot + s, ref, s)

    def halo(t, k, side, slot, peer):
        if k == PU:
            src = made.at[t, R2, :, lanes((1 - side) * (D - 1) * HW, HW)]
            dst = rest.at[slot]
        else:
            src = pad.at[t, k, :, lanes(lane((1 - side) * (D - 1), 1), HW)]
            dst = pad.at[t, k, :, lanes(lane(near_q(side), 1), HW)]
        return pltpu.make_async_remote_copy(
            src_ref=src, dst_ref=dst, send_sem=halo_s.at[slot], recv_sem=halo_r.at[6 if t else k, slot],
            device_id={"slab": peer}, device_id_type=MESH,
        )

    def halo_start(t, k):
        over(toward, lambda side, slot, peer: halo(t, k, side, slot, peer).start())

    def halo_arrived(t, k):
        over(sides, lambda side, slot, peer: halo(t, k, side, slot, peer).wait_recv())

    def to_seg(k):
        return pltpu.make_async_remote_copy(
            src_ref=made.at[0, k], dst_ref=second.at[k],
            send_sem=seg_s.at[1 if k <= X2 else 0], recv_sem=seg_r.at[k],
            device_id={"segment": next_seg if k <= X2 else prev_seg}, device_id_type=MESH,
        )

    def edge_at(k, far, side, slot):
        return edge.at[k, slot, :, lanes((side if far else 1 - side) * HW, HW)]

    def edge_copy(src, k, far, target, which, side, slot, peer):
        plane = (1 - side) * (D - 2) + side if far else (1 - side) * (D - 1)
        return pltpu.make_async_remote_copy(
            src_ref=src.at[:, lanes(plane * HW, HW)], dst_ref=edge_at(k, far, side, slot),
            send_sem=edge_s.at[which, slot], recv_sem=edge_r.at[k // 2 + 4 if far else k - 1, slot],
            device_id={"segment": target, "slab": peer}, device_id_type=MESH,
        )

    def edge_start(src, k, far, target, which):
        over(toward, lambda *side: edge_copy(src, k, far, target, which, *side).start())

    def edge_arrived(k, far, *side):
        edge_copy(made.at[0, k], k, far, seg, 0, *side).wait_recv()

    def pass_on(k, side, slot, peer):
        if k == G1:
            src = pad.at[0, PE, :, lanes(lane(near_q(side), 1), HW)]
        else:
            src = rest.at[slot]
        return pltpu.make_async_remote_copy(
            src_ref=src, dst_ref=edge_at(k, False, side, slot),
            send_sem=pass_s.at[slot], recv_sem=edge_r.at[k - 1, slot],
            device_id={"segment": prev_seg}, device_id_type=MESH,
        )

    def drain(sem, src):
        pltpu.make_async_remote_copy(
            src_ref=src, dst_ref=src, send_sem=sem, recv_sem=sem,
            device_id={"slab": lax.rem(slab + 1, n)}, device_id_type=MESH,
        ).wait_send()

    def planes_of(count):
        return pad.at[0, 0, :, pl.ds(0, count * HW)]

    def out_prev(k):
        dst = backs.at[k - R1] if k < E1 else grads.at[k - E1]
        return pltpu.make_async_remote_copy(
            src_ref=nat.at[k], dst_ref=dst, send_sem=back_s.at[0], recv_sem=back_r.at[0],
            device_id={"segment": prev_seg}, device_id_type=MESH,
        )

    def own_out(k):
        return pltpu.make_async_copy(nat.at[k], fout.at[k], out_s.at[0])

    def last_act(k):
        return pltpu.make_async_copy(nat.at[k], backs.at[k], out_s.at[1])

    def last_grad(k):
        return pltpu.make_async_copy(loss.at[2 + k], grads.at[k], out_s.at[1])

    def put(t, k, r, value):
        d, h = divmod(r, H)
        put_at(t, k, d, h, value)

    def put_at(t, k, q, h, value):
        pad[t, k, :, lanes(lane(q, h + 1), W)] = value.astype(bf16)

    def tall(t, k, q):
        return jnp.concatenate([pad[t, k, :, lanes(lane(q, b), HW)] for b in range(3)], axis=0)

    def taps(t, k, m, p, which):
        total, which = None, list(which)
        while which:
            a = which.pop(0)
            lhs, rhs = w[m, a], tall(t, k, p + a - 1)
            if which:
                which.pop(0)
                lhs = pairs[m, a]
                rhs = jnp.concatenate([rhs, tall(t, k, p + a)], axis=0)
            part = jnp.dot(lhs, rhs, preferred_element_type=f32)
            total = part if total is None else total + part
        return total

    def inner(p):
        return [a for a in range(3) if 0 <= p + a - 1 < D]

    def conv_local(t, k, m, slot):
        for p in range(D):
            acc[slot, :, pl.ds(p * HW, HW)] = taps(t, k, m, p, inner(p))

    def rows_of(total):
        for h in range(H):
            y = total[:, h * W : (h + 1) * W]
            left = jnp.where(lane_no == 0, 0.0, pltpu.roll(y[:C], 1, 1))
            right = jnp.where(lane_no == W - 1, 0.0, pltpu.roll(y[2 * C :], W - 1, 1))
            yield h, y[C : 2 * C] + left + right

    def conv_finish(t, k, m, slot, act, then=None):
        def outer(side):
            return jnp.dot(w[m, 2 * side], tall(t, k, near_q(side)), preferred_element_type=f32)

        def add(side, at, peer):
            acc[slot, :, lanes(side * (D - 1) * HW, HW)] += outer(side)

        if n > 2:
            over(sides, add)
        for i in range(D):
            p = (1 - slab) * (D - 1) + i * (2 * slab - 1) if n == 2 else i
            total = acc[slot, :, lanes(p * HW, HW)]
            if n == 2 and i == 0:
                total += outer(1 - slab)
            for h, out in rows_of(total):
                act(p * H + h, p, h, out)
            if then is not None and i == (0 if n == 2 else D - 1):
                then()

    def conv_whole(t, k, m):
        for p in range(D):
            for h, out in rows_of(taps(t, k, m, p, range(3))):
                yield p * H + h, out

    def widen(j, r, v):
        at = pl.ds(r * W, W)
        g3[j, 0:C, at] = jnp.where(lane_no == W - 1, 0.0, pltpu.roll(v, W - 1, 1)).astype(bf16)
        g3[j, C : 2 * C, at] = v.astype(bf16)
        g3[j, 2 * C : 3 * C, at] = jnp.where(lane_no == 0, 0.0, pltpu.roll(v, 1, 1)).astype(bf16)

    def product(lhs, j, p):
        return lax.dot_general(
            lhs, g3[j, :, lanes(p * HW, HW)], (((1,), (1,)), ((), ())), preferred_element_type=f32
        )

    def wgrad_inner(t, k, j):
        parts = [None] * 3
        for p in range(D):
            which = inner(p)
            part = product(jnp.concatenate([tall(t, k, p + a - 1) for a in which], axis=0), j, p)
            for i, a in enumerate(which):
                block = part[i * 3 * C : (i + 1) * 3 * C]
                parts[a] = block if parts[a] is None else parts[a] + block
        for a in range(3):
            here = pl.ds(a * 3 * C, 3 * C)
            if t == 0:
                dsum[j, here] = parts[a]
            else:
                dsum[j, here] += parts[a]

    def wgrad_whole(k, j):
        for p in range(D):
            lhs = jnp.concatenate([tall(1, k, p + a - 1) for a in range(3)], axis=0)
            part = product(lhs, j, p)
            total = part if p == 0 else total + part
        dsum[j] += total

    def wgrad_outer(t, k, j):
        def outer(side, slot, peer):
            at = side * 6 * C
            here = pl.ds(at if isinstance(at, int) else pl.multiple_of(at, 8), 3 * C)
            dsum[j, here] += product(tall(t, k, near_q(side)), j, side * (D - 1))

        over(sides, outer)

    def wgrad_share(j):
        for q in range(1, n):
            first = lax.rem(slab + q, n) * cs
            for ab in range(9):
                part = dsum[j, pl.ds(pl.multiple_of(ab * C + first, 8), cs)].astype(bf16)
                dpart[j, q - 1, ab] = jnp.concatenate(
                    [part, jnp.zeros((cs, LW - 3 * C), bf16)], axis=1
                )
            share(j, q).start()

    def share(j, q):
        target = lax.rem(slab + q, n)
        return pltpu.make_async_remote_copy(
            src_ref=dpart.at[j, q - 1], dst_ref=dgot.at[j, q - 1],
            send_sem=d_s.at[q - 1], recv_sem=d_r.at[j, q - 1],
            device_id={"slab": target}, device_id_type=MESH,
        )

    def keep(t, k, r, value):
        held = value.astype(bf16)
        made[t, k, :, lanes(r * W, W)] = held
        wide = held.astype(f32)
        if t == 1:
            stage[k, pl.ds(r, C, stride=DH), :] = wide
        return wide

    def straight(first, side):
        return lax.rem(seg, 4) == first

    def far_direct(side, slot, peer):
        @pl.when(straight(2, side))
        def _():
            for k in (O1, G2):
                edge_copy(made.at[0, k], k, True, prev_seg, 0, side, slot, peer).start()

    def far_relay(k):
        def act(side, slot, peer):
            @pl.when(jnp.logical_not(straight(1, side)))
            def _():
                edge_copy(second.at[k], k, True, seg, 3, side, slot, peer).start()

        @pl.when(relayed)
        def _():
            over(toward, act)

    def hand_on(k):
        src = made.at[0, k]
        if k <= X2:
            @pl.when(has_next)
            def _():
                if k == Y2:
                    edge_start(src, X2, False, next_seg, 1)
                to_seg(k).start()

            @pl.when(is_last)
            def _():
                edge_start(src, O1 + k, False, seg, 2)
                if k == Y1:
                    edge_start(src, O1, True, seg, 2)
                second[O1 + k] = made[0, k]
        else:
            @pl.when(has_prev)
            def _():
                to_seg(k).start()
                if k == O1:
                    edge_start(src, O1, False, prev_seg, 0)
                    edge_start(made.at[0, G2], G2, False, prev_seg, 0)
                    over(toward, far_direct)

    def hand_on_far():
        @pl.when(odd)
        def _():
            for k in (G2, O1):
                edge_start(made.at[0, k], k, True, prev_seg, 0)
            for k in (G1, O2):
                over(sides, lambda *side: pass_on(k, *side).start())

    def give_out(k):
        nat[k] = stage[k].astype(bf16)
        if k < R1:
            own_out(k).start()

            @pl.when(is_last)
            def _():
                last_act(k).start()
        else:
            @pl.when(has_prev)
            def _():
                out_prev(k).start()

    def arrived(k):
        there = has_prev if k <= X2 else whole if k in (G1, O2) else has_next

        @pl.when(there)
        def _():
            to_seg(k).wait_recv()

    load_pair(0, G1, bgrad)
    for r in range(DH):
        put(0, PD, r, staged(G2, r))
    peers = has_prev.astype(jnp.int32) + has_next.astype(jnp.int32) + n - 1
    pl.semaphore_wait(barrier, peers)
    halo_start(0, PD)

    @pl.when(has_prev)
    def _():
        pl.semaphore_signal(
            ready_s.at[1], inc=1, device_id={"segment": prev_seg}, device_id_type=MESH
        )

    @pl.when(has_next)
    def _():
        pl.semaphore_signal(
            ready_s.at[0], inc=1, device_id={"segment": next_seg}, device_id_type=MESH
        )

    load_pair(1, O1, bout)
    for r in range(DH):
        put(0, PH, r, silu(staged(O1, r)))
    halo_start(0, PH)
    load_pair(2, X1, fwd)
    for r in range(DH):
        put(0, PX, r, silu(staged(X2, r)))
    halo_start(0, PX)
    prepare_weights()
    conv_local(0, PD, GT, 0)
    conv_local(0, PH, G, 1)
    conv_local(0, PX, F, 2)
    for r in range(DH):
        widen(1, r, staged(G2, r))
    wgrad_inner(0, PH, 1)

    fetches[4].wait()
    fetches[5].wait()

    @pl.when(is_first)
    def _():
        for s in range(2):
            load_stage(6 + s, nxt, s)
            for r in range(DH):
                second[X1 + s, :, pl.ds(r * W, W)] = staged(6 + s, r).astype(bf16)
        edge_start(second.at[X2], X2, False, seg, 2)

    @pl.when(is_last)
    def _():
        for s in range(2):
            last_grad(s).start()
            load_stage(6 + s, loss, s)
            for r in range(DH):
                second[G1 + s, :, pl.ds(r * W, W)] = staged(6 + s, r).astype(bf16)
            edge_start(second.at[G1 + s], G1 + s, False, seg, 2)
        edge_start(second.at[G2], G2, True, seg, 2)

    @pl.when(has_prev)
    def _():
        pl.semaphore_wait(ready_s.at[0], 1)

    @pl.when(has_next)
    def _():
        pl.semaphore_wait(ready_s.at[1], 1)

    halo_arrived(0, PD)

    def act(r, p, h, out):
        put_at(0, PE, p, h, keep(0, E1, r, staged(G1, r) + slope(staged(O1, r)) * out))

    conv_finish(0, PD, GT, 0, act, functools.partial(halo_start, 0, PE))
    hand_on(E1)
    halo_arrived(0, PH)

    def act(r, p, h, out):
        put_at(0, PU, p, h, silu(keep(0, R2, r, staged(O2, r) - out)))

    conv_finish(0, PH, G, 1, act, functools.partial(halo_start, 0, PU))
    hand_on(R2)
    conv_local(0, PU, F, 1)
    wgrad_outer(0, PH, 1)
    halo_arrived(0, PX)

    def act(r, p, h, out):
        put_at(0, PY, p, h, silu(keep(0, Y1, r, staged(X1, r) + out)))

    conv_finish(0, PX, F, 2, act, functools.partial(halo_start, 0, PY))
    hand_on(Y1)
    conv_local(0, PE, FT, 0)
    for r in range(DH):
        widen(0, r, made[0, E1, :, pl.ds(r * W, W)].astype(f32))
    conv_local(0, PY, G, 2)
    wgrad_inner(0, PU, 0)

    halo_arrived(0, PE)

    def act(r, p, h, out):
        v = made[0, R2, :, lanes(r * W, W)].astype(f32)
        keep(0, E2, r, staged(G2, r) + slope(v) * out)

    conv_finish(0, PE, FT, 0, act)
    hand_on(E2)
    halo_arrived(0, PU)

    def rest_in(side, slot, peer):
        for h in range(H):
            v = rest[slot, :, pl.ds(h * W, W)].astype(f32)
            put_at(0, PU, near_q(side), h, silu(v))

    over(sides, rest_in)
    conv_finish(0, PU, F, 1, lambda r, p, h, out: keep(0, R1, r, staged(O1, r) - out))
    hand_on(R1)
    halo_arrived(0, PY)
    conv_finish(0, PY, G, 2, lambda r, p, h, out: keep(0, Y2, r, staged(X2, r) + out))
    hand_on(Y2)
    hand_on_far()
    wgrad_outer(0, PU, 0)

    def got(k, r):
        return second[k, :, lanes(r * W, W)].astype(f32)

    def near(k, side, slot, h):
        return edge[k, slot, :, lanes((1 - side) * HW + h * W, W)].astype(f32)

    @pl.when(relayed)
    def _():
        for k in (G1, O2):
            to_seg(k).wait_recv()
            edge_start(second.at[k], k, False, seg, 3)

    def forward_own():
        arrived(X2)
        for r in range(DH):
            put(1, PX, r, silu(got(X2, r)))
        conv_local(1, PX, F, 2)

    def forward():
        arrived(X1)

        def edges(side, slot, peer):
            edge_arrived(X2, False, side, slot, peer)
            for h in range(H):
                put_at(1, PX, near_q(side), h, silu(near(X2, side, slot, h)))

        over(sides, edges)

        def act(r, p, h, out):
            put_at(1, PY, p, h, silu(keep(1, Y1, r, got(X1, r) + out)))

        conv_finish(1, PX, F, 2, act, functools.partial(halo_start, 1, PY))
        give_out(Y1)
        conv_local(1, PY, G, 2)

    arrived(G2)
    far_relay(G2)

    pl.when(odd)(forward_own)
    for d in range(D):
        pad[1, PD, :, pl.ds(lane(d, 1), HW)] = second[G2, :, pl.ds(d * HW, HW)]
    conv_local(1, PD, GT, 0)
    arrived(O1)
    far_relay(O1)

    for r in range(DH):
        put(1, PH, r, silu(got(O1, r)))
    conv_local(1, PH, G, 1)
    for r in range(DH):
        widen(1, r, got(G2, r))
    pl.when(odd)(forward)

    def edge_q(far, side):
        return near_q(side) + (2 * side - 1 if far else 0), (side if far else 1 - side) * HW

    def grad_in(far, side, slot, peer):
        q, at = edge_q(far, side)
        edge_arrived(G2, far, side, slot, peer)
        pad[1, PD, :, lanes(lane(q, 1), HW)] = edge[G2, slot, :, lanes(at, HW)]

    def act_in(far, side, slot, peer):
        q, at = edge_q(far, side)
        edge_arrived(O1, far, side, slot, peer)
        for h in range(H):
            put_at(1, PH, q, h, silu(edge[O1, slot, :, lanes(at + h * W, W)].astype(f32)))

    over(sides, functools.partial(act_in, False))
    arrived(O2)

    def act(r, p, h, out):
        put_at(1, PU, p, h, silu(keep(1, R2, r, got(O2, r) - out)))

    conv_finish(1, PH, G, 1, act)
    over(sides, functools.partial(grad_in, False))
    arrived(G1)

    def act(r, p, h, out):
        put_at(1, PE, p, h, keep(1, E1, r, got(G1, r) + slope(got(O1, r)) * out))

    conv_finish(1, PD, GT, 0, act)

    def give_first():
        give_out(E1)
        give_out(R2)

    pl.when(even)(give_first)
    wgrad_whole(PH, 1)
    wgrad_share(1)

    def beyond_act(side, slot, peer):
        act_in(True, side, slot, peer)
        edge_arrived(O2, False, side, slot, peer)
        q = near_q(side)
        for h, out in rows_of(taps(1, PH, G, q, range(3))):
            value = (near(O2, side, slot, h) - out).astype(bf16).astype(f32)
            put_at(1, PU, q, h, silu(value))

    over(sides, beyond_act)
    for r in range(DH):
        widen(0, r, made[1, E1, :, pl.ds(r * W, W)].astype(f32))
    wgrad_whole(PU, 0)
    wgrad_share(0)

    def beyond_grad(side, slot, peer):
        grad_in(True, side, slot, peer)
        edge_arrived(G1, False, side, slot, peer)
        q = near_q(side)
        for h, out in rows_of(taps(1, PD, GT, q, range(3))):
            value = near(G1, side, slot, h) + slope(near(O1, side, slot, h)) * out
            put_at(1, PE, q, h, value)

    over(sides, beyond_grad)
    pl.when(odd)(give_first)


    for r, out in conv_whole(1, PE, FT):
        v = made[1, R2, :, pl.ds(r * W, W)].astype(f32)
        keep(1, E2, r, got(G2, r) + slope(v) * out)
    give_out(E2)
    for r, out in conv_whole(1, PU, F):
        keep(1, R1, r, got(O1, r) - out)
    give_out(R1)

    def gradients():
        for j in (1, 0):
            for q in range(1, n):
                share(j, q).wait_recv()
            for ab in range(9):
                own = dsum[j, pl.ds(pl.multiple_of(ab * C + slab * cs, 8), cs)]
                total = jnp.concatenate([own, jnp.zeros((cs, LW - 3 * C), f32)], axis=1)
                for q in range(1, n):
                    total += dgot[j, q - 1, ab].astype(f32)
                total *= scale
                for c in range(3):
                    tap = total if c == 0 else pltpu.roll(total, LW - c * C, 1)
                    dt[j, pl.ds(3 * ab + c, cs, stride=27), :] = tap
            dw[j] = dt[j].T[:C]

    @pl.when(even)
    def _():
        forward_own()
        forward()
        gradients()

    halo_arrived(1, PY)
    conv_finish(1, PY, G, 2, lambda r, p, h, out: keep(1, Y2, r, got(X2, r) + out))
    give_out(Y2)
    pl.when(odd)(gradients)

    def drain_edges(which, first, fewer, more):
        def act(side, slot, peer):
            direct = straight(first, side)
            sem = edge_s.at[which, slot]
            pl.when(direct)(lambda: drain(sem, planes_of(more)))
            pl.when(jnp.logical_not(direct))(lambda: drain(sem, planes_of(fewer)))

        over(toward, act)

    over(toward, lambda side, slot, peer: drain(halo_s.at[slot], planes_of(7)))
    for q in range(1, n):
        drain(d_s.at[q - 1], dpart.at[:, 0])
    pltpu.make_async_copy(nat.at[pl.ds(Y1, 2)], fout, out_s.at[0]).wait()

    @pl.when(is_first)
    def _():
        over(toward, lambda side, slot, peer: drain(edge_s.at[2, slot], planes_of(1)))

    @pl.when(is_last)
    def _():
        pltpu.make_async_copy(nat.at[pl.ds(0, 4)], nat.at[pl.ds(0, 4)], out_s.at[1]).wait()
        over(toward, lambda side, slot, peer: drain(edge_s.at[2, slot], planes_of(6)))

    @pl.when(has_next)
    def _():
        drain(seg_s.at[1], made.at[0, pl.ds(0, 2)])
        over(toward, lambda side, slot, peer: drain(edge_s.at[1, slot], planes_of(1)))
        drain(back_r.at[0], nat.at[pl.ds(R1, 4)])

    @pl.when(has_prev)
    def _():
        drain(seg_s.at[0], made.at[0, pl.ds(0, 4)])
        drain(back_s.at[0], nat.at[pl.ds(R1, 4)])

        @pl.when(even)
        def _():
            drain_edges(0, 2, 2, 4)

    @pl.when(odd)
    def _():
        over(toward, lambda side, slot, peer: drain(edge_s.at[0, slot], planes_of(4)))
        over(sides, lambda side, slot, peer: drain(pass_s.at[slot], planes_of(2)))

    @pl.when(relayed)
    def _():
        drain_edges(3, 1, 4, 2)


def write_out(*refs):
    srcs, dsts, sems = refs[:4], refs[4:8], refs[8]
    writes = [pltpu.make_async_copy(a, b, sems.at[i]) for i, (a, b) in enumerate(zip(srcs, dsts))]
    for write in writes:
        write.start()
    for write in writes:
        write.wait()


def local(segs, n, fwd_in, back_out, back_grad, batch_next, loss_grad, weights):
    _, _, C, D, H, W = fwd_in.shape
    rows = C * D * H
    cs = C // n
    ends = 1 if n == 2 else 2
    f32, bf16 = jnp.float32, jnp.bfloat16
    scale = float(D * n * H * W) ** (-0.5)
    vmem = pl.BlockSpec(memory_space=pltpu.VMEM)
    hbm = pl.BlockSpec(memory_space=pltpu.HBM)
    wide = pl.cdiv(3 * C, 128) * 128
    anywhere = pl.BlockSpec(memory_space=pl.ANY)
    pair = jax.ShapeDtypeStruct((2, rows, W), bf16)
    share = jax.ShapeDtypeStruct((2, C, 27 * cs), f32)
    dma = pltpu.SemaphoreType.DMA
    fout, backs, grads, dw = pl.pallas_call(
        functools.partial(kernel, (C, D, H, W, segs, n, scale)),
        out_shape=tuple(pltpu.VMEM(x.shape, x.dtype) for x in (pair, pair, pair, share)),
        in_specs=[hbm] * 6,
        out_specs=(vmem, vmem, vmem, vmem),
        scratch_shapes=[
            pltpu.VMEM((2, rows, W), bf16),
            pltpu.VMEM((2, rows, W), bf16),
            pltpu.VMEM((2, rows, W), bf16),
            pltpu.VMEM((2, rows, W), bf16),
            pltpu.VMEM((4, rows, W), bf16),
            pltpu.VMEM((2 * C, 27 * C), bf16),
            pltpu.VMEM((27 * C, wide), f32),
            pltpu.VMEM((4, 3, 3 * C, 3 * C), bf16),
            pltpu.VMEM((4, 2, 3 * C, 6 * C), bf16),
            pltpu.VMEM((2, 27 * cs, wide), f32),
            pltpu.VMEM((2, 6, C, (D + 4) * (H + 2) * W), bf16),
            pltpu.VMEM((8, rows, W), f32),
            pltpu.VMEM((6, C, D * H * W), bf16),
            pltpu.VMEM((6, ends, C, 2 * H * W), bf16),
            pltpu.VMEM((ends, C, H * W), bf16),
            pltpu.VMEM((2, 6, C, D * H * W), bf16),
            pltpu.VMEM((6, rows, W), bf16),
            pltpu.VMEM((3, 3 * C, D * H * W), f32),
            pltpu.VMEM((2, 3 * C, D * H * W), bf16),
            pltpu.VMEM((2, 9 * C, 3 * C), f32),
            pltpu.VMEM((2, n - 1, 9, cs, wide), bf16),
            pltpu.VMEM((2, n - 1, 9, cs, wide), bf16),
            dma((ends,)),
            dma((7, ends)),
            dma((2,)),
            dma((6,)),
            dma((1,)),
            dma((1,)),
            dma((4, ends)),
            dma((7, ends)),
            dma((ends,)),
            dma((2,)),
            dma((n - 1,)),
            dma((2, n - 1)),
            dma((6,)),
            pltpu.SemaphoreType.REGULAR((2,)),
        ],
        compiler_params=pltpu.CompilerParams(
            collective_id=0, has_side_effects=True, vmem_limit_bytes=48 << 20
        ),
        name="petra",
    )(
        *[
            pltpu.with_memory_space_constraint(x, pltpu.HBM)
            for x in (
                fwd_in.reshape(2, rows, W),
                back_out.reshape(2, rows, W),
                back_grad.reshape(2, rows, W),
                batch_next.reshape(2, rows, W),
                loss_grad.reshape(4, rows, W),
                weights.reshape(2 * C, 27 * C),
            )
        ]
    )
    fout, backs, grads, dw = pl.pallas_call(
        write_out,
        out_shape=(pair, pair, pair, share),
        in_specs=[vmem] * 4,
        out_specs=(hbm,) * 4,
        scratch_shapes=[dma((4,))],
        compiler_params=pltpu.CompilerParams(vmem_limit_bytes=4 << 20),
        name="write_out",
    )(fout, backs, grads, dw)
    shape = fwd_in.shape
    return fout.reshape(shape), backs.reshape(shape), grads.reshape(shape), dw[None]


def solution(mesh):
    field = P("segment", None, None, "slab", None, None)
    return jax.shard_map(
        functools.partial(local, mesh.shape["segment"], mesh.shape["slab"]),
        mesh=mesh,
        in_specs=(
            field,
            field,
            field,
            P(None, None, "slab", None, None),
            P(None, None, None, "slab", None, None),
            P("segment", None, None, None),
        ),
        out_specs=(field, field, field, P("segment", None, None, "slab")),
        check_vma=False,
    )
```

```python
import functools

import jax
import jax.numpy as jnp
from jax import lax
from jax.experimental import pallas as pl
from jax.experimental.pallas import tpu as pltpu
from jax.sharding import PartitionSpec as P

MESH = pl.DeviceIdType.MESH
F, G, FT, GT = range(4)
X1, X2, O1, O2, G1, G2 = range(6)
Y1, Y2, R1, R2, E1, E2 = range(6)
PX, PH, PD, PY, PU, PE = range(6)


def sigmoid(v):
    return 1.0 / (1.0 + jnp.exp(-v))


def silu(v):
    return v / (1.0 + jnp.exp(-v))


def slope(v):
    sig = sigmoid(v)
    return sig * (1.0 + v * (1.0 - sig))


def kernel(
    dims, fwd_hbm, bout_hbm, bgrad_hbm, nxt_hbm, loss_hbm, kern_hbm, fout, backs, grads, dw,
    fwd, bout, bgrad, nxt, loss, kern, kt, w, pairs, dt, pad, stage, second, edge, rest, made, nat, acc,
    g3, dsum, dpart, dgot, halo_s, halo_r, seg_s, seg_r, back_s, back_r, edge_s, edge_r, pass_s,
    out_s, d_s, d_r, in_s, ready_s,
):
    C, D, H, W, segs, n, scale = dims
    DH, HW = D * H, H * W
    cs = C // n
    LW = pl.cdiv(3 * C, 128) * 128
    f32, bf16 = jnp.float32, jnp.bfloat16
    seg = lax.axis_index("segment")
    slab = lax.axis_index("slab")
    has_prev, has_next = seg > 0, seg < segs - 1
    is_first, is_last = seg == 0, seg == segs - 1
    odd, even = lax.rem(seg, 2) == 1, lax.rem(seg, 2) == 0
    relayed = jnp.logical_and(has_next, odd)
    whole = jnp.logical_and(has_next, even)
    prev_seg = lax.rem(seg + segs - 1, segs)
    next_seg = lax.rem(seg + 1, segs)
    lane_no = lax.broadcasted_iota(jnp.int32, (C, W), 1)

    if n == 2:
        sides = [(None, 1 - slab, 0, 1 - slab)]
        toward = [(None, slab, 0, 1 - slab)]
    else:
        below, above = lax.rem(slab + n - 1, n), lax.rem(slab + 1, n)
        sides = [(slab > 0, 0, 0, below), (slab < n - 1, 1, 1, above)]
        toward = [(slab < n - 1, 0, 0, above), (slab > 0, 1, 1, below)]

    def over(rows, act):
        for there, side, slot, peer in rows:
            if there is None:
                act(side, slot, peer)
            else:
                pl.when(there)(functools.partial(act, side, slot, peer))

    def near_q(side):
        return side * (D + 1) - 1

    barrier = pltpu.get_barrier_semaphore()

    for k in range(1, n):
        pl.semaphore_signal(
            barrier, inc=1, device_id={"slab": lax.rem(slab + k, n)}, device_id_type=MESH
        )

    @pl.when(has_prev)
    def _():
        pl.semaphore_signal(barrier, inc=1, device_id={"segment": prev_seg}, device_id_type=MESH)

    @pl.when(has_next)
    def _():
        pl.semaphore_signal(barrier, inc=1, device_id={"segment": next_seg}, device_id_type=MESH)

    fetches = [
        pltpu.make_async_copy(src, dst, in_s.at[i])
        for i, (src, dst) in enumerate(
            [
                (bgrad_hbm, bgrad), (bout_hbm, bout), (fwd_hbm, fwd),
                (kern_hbm, kern), (nxt_hbm, nxt), (loss_hbm, loss),
            ]
        )
    ]
    for fetch in fetches:
        fetch.start()

    def lanes(at, size):
        return pl.ds(at if isinstance(at, int) else pl.multiple_of(at, W), size)

    def lane(q, hh):
        return ((q + 2) * (H + 2) + hh) * W

    zero = jnp.zeros((C, W), bf16)
    for t in range(2):
        for k in range(6):
            reach = 2 if t == 1 and k in (PH, PD) else 1
            for q in range(-reach, D + reach):
                for hh in (0, H + 1):
                    pad[t, k, :, pl.ds(lane(q, hh), W)] = zero

    for q, missing in ((-1, slab == 0), (D, slab == n - 1)):
        @pl.when(missing)
        def _():
            for t in range(2):
                for k in range(6):
                    pad[t, k, :, pl.ds(lane(q, 1), HW)] = jnp.zeros((C, HW), bf16)

    def load_stage(slot, ref, s):
        stage[slot] = ref[s].astype(f32)

    def staged(slot, r):
        return stage[slot, pl.ds(r, C, stride=DH), :]

    def prepare_weights():
        fetches[3].wait()
        wide = kern[...].astype(f32)
        kt[...] = jnp.concatenate([wide, jnp.zeros((LW - 2 * C, 27 * C), f32)], axis=0).T

        def tap(t):
            return kt[pl.ds(t, C, stride=27), :]

        def set_weights(m, a, c, block):
            here = pl.ds(c * C, C)
            w[m, a, here, :] = block
            if a < 2:
                pairs[m, a, here, 0 : 3 * C] = block
            if a > 0:
                pairs[m, a - 1, here, 3 * C : 6 * C] = block

        for a in range(3):
            for c in range(3):
                block = jnp.concatenate([tap(9 * a + 3 * b + c) for b in range(3)], axis=0).T
                for f in range(2):
                    set_weights(F + f, a, c, block[f * C : (f + 1) * C].astype(bf16))
                for f in range(2):
                    turned = jnp.concatenate(
                        [
                            tap(9 * (2 - a) + 3 * (2 - b) + 2 - c)[:, f * C : (f + 1) * C]
                            for b in range(3)
                        ],
                        axis=1,
                    )
                    set_weights(FT + f, a, c, turned.astype(bf16))

    def load_pair(i, slot, ref):
        fetches[i].wait()
        for s in range(2):
            load_stage(slot + s, ref, s)

    def halo(t, k, side, slot, peer):
        if k == PU:
            src = made.at[t, R2, :, lanes((1 - side) * (D - 1) * HW, HW)]
            dst = rest.at[slot]
        else:
            src = pad.at[t, k, :, lanes(lane((1 - side) * (D - 1), 1), HW)]
            dst = pad.at[t, k, :, lanes(lane(near_q(side), 1), HW)]
        return pltpu.make_async_remote_copy(
            src_ref=src, dst_ref=dst, send_sem=halo_s.at[slot], recv_sem=halo_r.at[6 if t else k, slot],
            device_id={"slab": peer}, device_id_type=MESH,
        )

    def halo_start(t, k):
        over(toward, lambda side, slot, peer: halo(t, k, side, slot, peer).start())

    def halo_arrived(t, k):
        over(sides, lambda side, slot, peer: halo(t, k, side, slot, peer).wait_recv())

    def to_seg(k):
        return pltpu.make_async_remote_copy(
            src_ref=made.at[0, k], dst_ref=second.at[k],
            send_sem=seg_s.at[1 if k <= X2 else 0], recv_sem=seg_r.at[k],
            device_id={"segment": next_seg if k <= X2 else prev_seg}, device_id_type=MESH,
        )

    def edge_at(k, far, side, slot):
        return edge.at[k, slot, :, lanes((side if far else 1 - side) * HW, HW)]

    def edge_copy(src, k, far, target, which, side, slot, peer):
        plane = (1 - side) * (D - 2) + side if far else (1 - side) * (D - 1)
        return pltpu.make_async_remote_copy(
            src_ref=src.at[:, lanes(plane * HW, HW)], dst_ref=edge_at(k, far, side, slot),
            send_sem=edge_s.at[which, slot], recv_sem=edge_r.at[k // 2 + 4 if far else k - 1, slot],
            device_id={"segment": target, "slab": peer}, device_id_type=MESH,
        )

    def edge_start(src, k, far, target, which):
        over(toward, lambda *side: edge_copy(src, k, far, target, which, *side).start())

    def edge_arrived(k, far, *side):
        edge_copy(made.at[0, k], k, far, seg, 0, *side).wait_recv()

    def pass_on(k, side, slot, peer):
        if k == G1:
            src = pad.at[0, PE, :, lanes(lane(near_q(side), 1), HW)]
        else:
            src = rest.at[slot]
        return pltpu.make_async_remote_copy(
            src_ref=src, dst_ref=edge_at(k, False, side, slot),
            send_sem=pass_s.at[slot], recv_sem=edge_r.at[k - 1, slot],
            device_id={"segment": prev_seg}, device_id_type=MESH,
        )

    def drain(sem, src):
        pltpu.make_async_remote_copy(
            src_ref=src, dst_ref=src, send_sem=sem, recv_sem=sem,
            device_id={"slab": lax.rem(slab + 1, n)}, device_id_type=MESH,
        ).wait_send()

    def planes_of(count):
        return pad.at[0, 0, :, pl.ds(0, count * HW)]

    def out_prev(k):
        dst = backs.at[k - R1] if k < E1 else grads.at[k - E1]
        return pltpu.make_async_remote_copy(
            src_ref=nat.at[k], dst_ref=dst, send_sem=back_s.at[0], recv_sem=back_r.at[0],
            device_id={"segment": prev_seg}, device_id_type=MESH,
        )

    def own_out(k):
        return pltpu.make_async_copy(nat.at[k], fout.at[k], out_s.at[0])

    def last_act(k):
        return pltpu.make_async_copy(nat.at[k], backs.at[k], out_s.at[1])

    def last_grad(k):
        return pltpu.make_async_copy(loss.at[2 + k], grads.at[k], out_s.at[1])

    def put(t, k, r, value):
        d, h = divmod(r, H)
        put_at(t, k, d, h, value)

    def put_at(t, k, q, h, value):
        pad[t, k, :, lanes(lane(q, h + 1), W)] = value.astype(bf16)

    def tall(t, k, q):
        return jnp.concatenate([pad[t, k, :, lanes(lane(q, b), HW)] for b in range(3)], axis=0)

    def taps(t, k, m, p, which):
        total, which = None, list(which)
        while which:
            a = which.pop(0)
            lhs, rhs = w[m, a], tall(t, k, p + a - 1)
            if which:
                which.pop(0)
                lhs = pairs[m, a]
                rhs = jnp.concatenate([rhs, tall(t, k, p + a)], axis=0)
            part = jnp.dot(lhs, rhs, preferred_element_type=f32)
            total = part if total is None else total + part
        return total

    def inner(p):
        return [a for a in range(3) if 0 <= p + a - 1 < D]

    def conv_local(t, k, m, slot):
        for p in range(D):
            acc[slot, :, pl.ds(p * HW, HW)] = taps(t, k, m, p, inner(p))

    def rows_of(total):
        for h in range(H):
            y = total[:, h * W : (h + 1) * W]
            left = jnp.where(lane_no == 0, 0.0, pltpu.roll(y[:C], 1, 1))
            right = jnp.where(lane_no == W - 1, 0.0, pltpu.roll(y[2 * C :], W - 1, 1))
            yield h, y[C : 2 * C] + left + right

    def conv_finish(t, k, m, slot, act, then=None):
        def outer(side):
            return jnp.dot(w[m, 2 * side], tall(t, k, near_q(side)), preferred_element_type=f32)

        def add(side, at, peer):
            acc[slot, :, lanes(side * (D - 1) * HW, HW)] += outer(side)

        if n > 2:
            over(sides, add)
        for i in range(D):
            p = (1 - slab) * (D - 1) + i * (2 * slab - 1) if n == 2 else i
            total = acc[slot, :, lanes(p * HW, HW)]
            if n == 2 and i == 0:
                total += outer(1 - slab)
            for h, out in rows_of(total):
                act(p * H + h, p, h, out)
            if then is not None and i == (0 if n == 2 else D - 1):
                then()

    def conv_whole(t, k, m):
        for p in range(D):
            for h, out in rows_of(taps(t, k, m, p, range(3))):
                yield p * H + h, out

    def widen(j, r, v):
        at = pl.ds(r * W, W)
        g3[j, 0:C, at] = jnp.where(lane_no == W - 1, 0.0, pltpu.roll(v, W - 1, 1)).astype(bf16)
        g3[j, C : 2 * C, at] = v.astype(bf16)
        g3[j, 2 * C : 3 * C, at] = jnp.where(lane_no == 0, 0.0, pltpu.roll(v, 1, 1)).astype(bf16)

    def product(lhs, j, p):
        return lax.dot_general(
            lhs, g3[j, :, lanes(p * HW, HW)], (((1,), (1,)), ((), ())), preferred_element_type=f32
        )

    def wgrad_inner(t, k, j):
        parts = [None] * 3
        for p in range(D):
            which = inner(p)
            part = product(jnp.concatenate([tall(t, k, p + a - 1) for a in which], axis=0), j, p)
            for i, a in enumerate(which):
                block = part[i * 3 * C : (i + 1) * 3 * C]
                parts[a] = block if parts[a] is None else parts[a] + block
        for a in range(3):
            here = pl.ds(a * 3 * C, 3 * C)
            if t == 0:
                dsum[j, here] = parts[a]
            else:
                dsum[j, here] += parts[a]

    def wgrad_whole(k, j):
        for p in range(D):
            lhs = jnp.concatenate([tall(1, k, p + a - 1) for a in range(3)], axis=0)
            part = product(lhs, j, p)
            total = part if p == 0 else total + part
        dsum[j] += total

    def wgrad_outer(t, k, j):
        def outer(side, slot, peer):
            at = side * 6 * C
            here = pl.ds(at if isinstance(at, int) else pl.multiple_of(at, 8), 3 * C)
            dsum[j, here] += product(tall(t, k, near_q(side)), j, side * (D - 1))

        over(sides, outer)

    def wgrad_share(j):
        for q in range(1, n):
            first = lax.rem(slab + q, n) * cs
            for ab in range(9):
                part = dsum[j, pl.ds(pl.multiple_of(ab * C + first, 8), cs)].astype(bf16)
                dpart[j, q - 1, ab] = jnp.concatenate(
                    [part, jnp.zeros((cs, LW - 3 * C), bf16)], axis=1
                )
            share(j, q).start()

    def share(j, q):
        target = lax.rem(slab + q, n)
        return pltpu.make_async_remote_copy(
            src_ref=dpart.at[j, q - 1], dst_ref=dgot.at[j, q - 1],
            send_sem=d_s.at[q - 1], recv_sem=d_r.at[j, q - 1],
            device_id={"slab": target}, device_id_type=MESH,
        )

    def keep(t, k, r, value):
        held = value.astype(bf16)
        made[t, k, :, lanes(r * W, W)] = held
        wide = held.astype(f32)
        if t == 1:
            stage[k, pl.ds(r, C, stride=DH), :] = wide
        return wide

    def straight(first, side):
        return lax.rem(seg, 4) == first

    def far_direct(side, slot, peer):
        @pl.when(straight(2, side))
        def _():
            for k in (O1, G2):
                edge_copy(made.at[0, k], k, True, prev_seg, 0, side, slot, peer).start()

    def far_relay(k):
        def act(side, slot, peer):
            @pl.when(jnp.logical_not(straight(1, side)))
            def _():
                edge_copy(second.at[k], k, True, seg, 3, side, slot, peer).start()

        @pl.when(relayed)
        def _():
            over(toward, act)

    def hand_on(k):
        src = made.at[0, k]
        if k <= X2:
            @pl.when(has_next)
            def _():
                if k == Y2:
                    edge_start(src, X2, False, next_seg, 1)
                to_seg(k).start()

            @pl.when(is_last)
            def _():
                edge_start(src, O1 + k, False, seg, 2)
                if k == Y1:
                    edge_start(src, O1, True, seg, 2)
                second[O1 + k] = made[0, k]
        else:
            @pl.when(has_prev)
            def _():
                to_seg(k).start()
                if k == O1:
                    edge_start(src, O1, False, prev_seg, 0)
                    edge_start(made.at[0, G2], G2, False, prev_seg, 0)
                    over(toward, far_direct)

    def hand_on_far():
        @pl.when(odd)
        def _():
            for k in (G2, O1):
                edge_start(made.at[0, k], k, True, prev_seg, 0)
            for k in (G1, O2):
                over(sides, lambda *side: pass_on(k, *side).start())

    def give_out(k):
        nat[k] = stage[k].astype(bf16)
        if k < R1:
            own_out(k).start()

            @pl.when(is_last)
            def _():
                last_act(k).start()
        else:
            @pl.when(has_prev)
            def _():
                out_prev(k).start()

    def arrived(k):
        there = has_prev if k <= X2 else whole if k in (G1, O2) else has_next

        @pl.when(there)
        def _():
            to_seg(k).wait_recv()

    load_pair(0, G1, bgrad)
    for r in range(DH):
        put(0, PD, r, staged(G2, r))
    peers = has_prev.astype(jnp.int32) + has_next.astype(jnp.int32) + n - 1
    pl.semaphore_wait(barrier, peers)
    halo_start(0, PD)

    @pl.when(has_prev)
    def _():
        pl.semaphore_signal(
            ready_s.at[1], inc=1, device_id={"segment": prev_seg}, device_id_type=MESH
        )

    @pl.when(has_next)
    def _():
        pl.semaphore_signal(
            ready_s.at[0], inc=1, device_id={"segment": next_seg}, device_id_type=MESH
        )

    load_pair(1, O1, bout)
    for r in range(DH):
        put(0, PH, r, silu(staged(O1, r)))
    halo_start(0, PH)
    load_pair(2, X1, fwd)
    for r in range(DH):
        put(0, PX, r, silu(staged(X2, r)))
    halo_start(0, PX)
    prepare_weights()
    conv_local(0, PD, GT, 0)
    conv_local(0, PH, G, 1)
    conv_local(0, PX, F, 2)
    for r in range(DH):
        widen(1, r, staged(G2, r))
    wgrad_inner(0, PH, 1)

    fetches[4].wait()
    fetches[5].wait()

    @pl.when(is_first)
    def _():
        for s in range(2):
            load_stage(6 + s, nxt, s)
            for r in range(DH):
                second[X1 + s, :, pl.ds(r * W, W)] = staged(6 + s, r).astype(bf16)
        edge_start(second.at[X2], X2, False, seg, 2)

    @pl.when(is_last)
    def _():
        for s in range(2):
            last_grad(s).start()
            load_stage(6 + s, loss, s)
            for r in range(DH):
                second[G1 + s, :, pl.ds(r * W, W)] = staged(6 + s, r).astype(bf16)
            edge_start(second.at[G1 + s], G1 + s, False, seg, 2)
        edge_start(second.at[G2], G2, True, seg, 2)

    @pl.when(has_prev)
    def _():
        pl.semaphore_wait(ready_s.at[0], 1)

    @pl.when(has_next)
    def _():
        pl.semaphore_wait(ready_s.at[1], 1)

    halo_arrived(0, PD)

    def act(r, p, h, out):
        put_at(0, PE, p, h, keep(0, E1, r, staged(G1, r) + slope(staged(O1, r)) * out))

    conv_finish(0, PD, GT, 0, act, functools.partial(halo_start, 0, PE))
    hand_on(E1)
    halo_arrived(0, PH)

    def act(r, p, h, out):
        put_at(0, PU, p, h, silu(keep(0, R2, r, staged(O2, r) - out)))

    conv_finish(0, PH, G, 1, act, functools.partial(halo_start, 0, PU))
    hand_on(R2)
    conv_local(0, PU, F, 1)
    wgrad_outer(0, PH, 1)
    halo_arrived(0, PX)

    def act(r, p, h, out):
        put_at(0, PY, p, h, silu(keep(0, Y1, r, staged(X1, r) + out)))

    conv_finish(0, PX, F, 2, act, functools.partial(halo_start, 0, PY))
    hand_on(Y1)
    conv_local(0, PE, FT, 0)
    for r in range(DH):
        widen(0, r, made[0, E1, :, pl.ds(r * W, W)].astype(f32))
    conv_local(0, PY, G, 2)
    wgrad_inner(0, PU, 0)

    halo_arrived(0, PE)

    def act(r, p, h, out):
        v = made[0, R2, :, lanes(r * W, W)].astype(f32)
        keep(0, E2, r, staged(G2, r) + slope(v) * out)

    conv_finish(0, PE, FT, 0, act)
    hand_on(E2)
    halo_arrived(0, PU)

    def rest_in(side, slot, peer):
        for h in range(H):
            v = rest[slot, :, pl.ds(h * W, W)].astype(f32)
            put_at(0, PU, near_q(side), h, silu(v))

    over(sides, rest_in)
    conv_finish(0, PU, F, 1, lambda r, p, h, out: keep(0, R1, r, staged(O1, r) - out))
    hand_on(R1)
    halo_arrived(0, PY)
    conv_finish(0, PY, G, 2, lambda r, p, h, out: keep(0, Y2, r, staged(X2, r) + out))
    hand_on(Y2)
    hand_on_far()
    wgrad_outer(0, PU, 0)

    def got(k, r):
        return second[k, :, lanes(r * W, W)].astype(f32)

    def near(k, side, slot, h):
        return edge[k, slot, :, lanes((1 - side) * HW + h * W, W)].astype(f32)

    @pl.when(relayed)
    def _():
        for k in (G1, O2):
            to_seg(k).wait_recv()
            edge_start(second.at[k], k, False, seg, 3)

    def forward_own():
        arrived(X2)
        for r in range(DH):
            put(1, PX, r, silu(got(X2, r)))
        conv_local(1, PX, F, 2)

    def forward():
        arrived(X1)

        def edges(side, slot, peer):
            edge_arrived(X2, False, side, slot, peer)
            for h in range(H):
                put_at(1, PX, near_q(side), h, silu(near(X2, side, slot, h)))

        over(sides, edges)

        def act(r, p, h, out):
            put_at(1, PY, p, h, silu(keep(1, Y1, r, got(X1, r) + out)))

        conv_finish(1, PX, F, 2, act, functools.partial(halo_start, 1, PY))

    def forward_rest():
        give_out(Y1)
        conv_local(1, PY, G, 2)

    arrived(G2)
    far_relay(G2)

    pl.when(odd)(forward_own)
    for d in range(D):
        pad[1, PD, :, pl.ds(lane(d, 1), HW)] = second[G2, :, pl.ds(d * HW, HW)]
    conv_local(1, PD, GT, 0)
    arrived(O1)
    far_relay(O1)

    for r in range(DH):
        put(1, PH, r, silu(got(O1, r)))
    conv_local(1, PH, G, 1)
    for r in range(DH):
        widen(1, r, got(G2, r))
    pl.when(odd)(forward)

    def edge_q(far, side):
        return near_q(side) + (2 * side - 1 if far else 0), (side if far else 1 - side) * HW

    def grad_in(far, side, slot, peer):
        q, at = edge_q(far, side)
        edge_arrived(G2, far, side, slot, peer)
        pad[1, PD, :, lanes(lane(q, 1), HW)] = edge[G2, slot, :, lanes(at, HW)]

    def act_in(far, side, slot, peer):
        q, at = edge_q(far, side)
        edge_arrived(O1, far, side, slot, peer)
        for h in range(H):
            put_at(1, PH, q, h, silu(edge[O1, slot, :, lanes(at + h * W, W)].astype(f32)))

    over(sides, functools.partial(act_in, False))
    arrived(O2)

    def act(r, p, h, out):
        put_at(1, PU, p, h, silu(keep(1, R2, r, got(O2, r) - out)))

    conv_finish(1, PH, G, 1, act)
    over(sides, functools.partial(grad_in, False))
    arrived(G1)

    def act(r, p, h, out):
        put_at(1, PE, p, h, keep(1, E1, r, got(G1, r) + slope(got(O1, r)) * out))

    conv_finish(1, PD, GT, 0, act)

    def give_first():
        give_out(E1)
        give_out(R2)

    pl.when(even)(give_first)
    wgrad_whole(PH, 1)
    wgrad_share(1)

    def beyond_act(side, slot, peer):
        act_in(True, side, slot, peer)
        edge_arrived(O2, False, side, slot, peer)
        q = near_q(side)
        for h, out in rows_of(taps(1, PH, G, q, range(3))):
            value = (near(O2, side, slot, h) - out).astype(bf16).astype(f32)
            put_at(1, PU, q, h, silu(value))

    over(sides, beyond_act)
    for r in range(DH):
        widen(0, r, made[1, E1, :, pl.ds(r * W, W)].astype(f32))
    wgrad_whole(PU, 0)
    wgrad_share(0)

    def beyond_grad(side, slot, peer):
        grad_in(True, side, slot, peer)
        edge_arrived(G1, False, side, slot, peer)
        q = near_q(side)
        for h, out in rows_of(taps(1, PD, GT, q, range(3))):
            value = near(G1, side, slot, h) + slope(near(O1, side, slot, h)) * out
            put_at(1, PE, q, h, value)

    over(sides, beyond_grad)

    @pl.when(odd)
    def _():
        give_first()
        forward_rest()


    for r, out in conv_whole(1, PE, FT):
        v = made[1, R2, :, pl.ds(r * W, W)].astype(f32)
        keep(1, E2, r, got(G2, r) + slope(v) * out)
    give_out(E2)
    for r, out in conv_whole(1, PU, F):
        keep(1, R1, r, got(O1, r) - out)
    give_out(R1)

    def gradients():
        for j in (1, 0):
            for q in range(1, n):
                share(j, q).wait_recv()
            for ab in range(9):
                own = dsum[j, pl.ds(pl.multiple_of(ab * C + slab * cs, 8), cs)]
                total = jnp.concatenate([own, jnp.zeros((cs, LW - 3 * C), f32)], axis=1)
                for q in range(1, n):
                    total += dgot[j, q - 1, ab].astype(f32)
                total *= scale
                for c in range(3):
                    tap = total if c == 0 else pltpu.roll(total, LW - c * C, 1)
                    dt[j, pl.ds(3 * ab + c, cs, stride=27), :] = tap
            dw[j] = dt[j].T[:C]

    @pl.when(even)
    def _():
        forward_own()
        forward()
        forward_rest()
        gradients()

    halo_arrived(1, PY)
    conv_finish(1, PY, G, 2, lambda r, p, h, out: keep(1, Y2, r, got(X2, r) + out))
    give_out(Y2)
    pl.when(odd)(gradients)

    def drain_edges(which, first, fewer, more):
        def act(side, slot, peer):
            direct = straight(first, side)
            sem = edge_s.at[which, slot]
            pl.when(direct)(lambda: drain(sem, planes_of(more)))
            pl.when(jnp.logical_not(direct))(lambda: drain(sem, planes_of(fewer)))

        over(toward, act)

    over(toward, lambda side, slot, peer: drain(halo_s.at[slot], planes_of(7)))
    for q in range(1, n):
        drain(d_s.at[q - 1], dpart.at[:, 0])
    pltpu.make_async_copy(nat.at[pl.ds(Y1, 2)], fout, out_s.at[0]).wait()

    @pl.when(is_first)
    def _():
        over(toward, lambda side, slot, peer: drain(edge_s.at[2, slot], planes_of(1)))

    @pl.when(is_last)
    def _():
        pltpu.make_async_copy(nat.at[pl.ds(0, 4)], nat.at[pl.ds(0, 4)], out_s.at[1]).wait()
        over(toward, lambda side, slot, peer: drain(edge_s.at[2, slot], planes_of(6)))

    @pl.when(has_next)
    def _():
        drain(seg_s.at[1], made.at[0, pl.ds(0, 2)])
        over(toward, lambda side, slot, peer: drain(edge_s.at[1, slot], planes_of(1)))
        drain(back_r.at[0], nat.at[pl.ds(R1, 4)])

    @pl.when(has_prev)
    def _():
        drain(seg_s.at[0], made.at[0, pl.ds(0, 4)])
        drain(back_s.at[0], nat.at[pl.ds(R1, 4)])

        @pl.when(even)
        def _():
            drain_edges(0, 2, 2, 4)

    @pl.when(odd)
    def _():
        over(toward, lambda side, slot, peer: drain(edge_s.at[0, slot], planes_of(4)))
        over(sides, lambda side, slot, peer: drain(pass_s.at[slot], planes_of(2)))

    @pl.when(relayed)
    def _():
        drain_edges(3, 1, 4, 2)


def write_out(*refs):
    srcs, dsts, sems = refs[:4], refs[4:8], refs[8]
    writes = [pltpu.make_async_copy(a, b, sems.at[i]) for i, (a, b) in enumerate(zip(srcs, dsts))]
    for write in writes:
        write.start()
    for write in writes:
        write.wait()


def local(segs, n, fwd_in, back_out, back_grad, batch_next, loss_grad, weights):
    _, _, C, D, H, W = fwd_in.shape
    rows = C * D * H
    cs = C // n
    ends = 1 if n == 2 else 2
    f32, bf16 = jnp.float32, jnp.bfloat16
    scale = float(D * n * H * W) ** (-0.5)
    vmem = pl.BlockSpec(memory_space=pltpu.VMEM)
    hbm = pl.BlockSpec(memory_space=pltpu.HBM)
    wide = pl.cdiv(3 * C, 128) * 128
    anywhere = pl.BlockSpec(memory_space=pl.ANY)
    pair = jax.ShapeDtypeStruct((2, rows, W), bf16)
    share = jax.ShapeDtypeStruct((2, C, 27 * cs), f32)
    dma = pltpu.SemaphoreType.DMA
    fout, backs, grads, dw = pl.pallas_call(
        functools.partial(kernel, (C, D, H, W, segs, n, scale)),
        out_shape=tuple(pltpu.VMEM(x.shape, x.dtype) for x in (pair, pair, pair, share)),
        in_specs=[hbm] * 6,
        out_specs=(vmem, vmem, vmem, vmem),
        scratch_shapes=[
            pltpu.VMEM((2, rows, W), bf16),
            pltpu.VMEM((2, rows, W), bf16),
            pltpu.VMEM((2, rows, W), bf16),
            pltpu.VMEM((2, rows, W), bf16),
            pltpu.VMEM((4, rows, W), bf16),
            pltpu.VMEM((2 * C, 27 * C), bf16),
            pltpu.VMEM((27 * C, wide), f32),
            pltpu.VMEM((4, 3, 3 * C, 3 * C), bf16),
            pltpu.VMEM((4, 2, 3 * C, 6 * C), bf16),
            pltpu.VMEM((2, 27 * cs, wide), f32),
            pltpu.VMEM((2, 6, C, (D + 4) * (H + 2) * W), bf16),
            pltpu.VMEM((8, rows, W), f32),
            pltpu.VMEM((6, C, D * H * W), bf16),
            pltpu.VMEM((6, ends, C, 2 * H * W), bf16),
            pltpu.VMEM((ends, C, H * W), bf16),
            pltpu.VMEM((2, 6, C, D * H * W), bf16),
            pltpu.VMEM((6, rows, W), bf16),
            pltpu.VMEM((3, 3 * C, D * H * W), f32),
            pltpu.VMEM((2, 3 * C, D * H * W), bf16),
            pltpu.VMEM((2, 9 * C, 3 * C), f32),
            pltpu.VMEM((2, n - 1, 9, cs, wide), bf16),
            pltpu.VMEM((2, n - 1, 9, cs, wide), bf16),
            dma((ends,)),
            dma((7, ends)),
            dma((2,)),
            dma((6,)),
            dma((1,)),
            dma((1,)),
            dma((4, ends)),
            dma((7, ends)),
            dma((ends,)),
            dma((2,)),
            dma((n - 1,)),
            dma((2, n - 1)),
            dma((6,)),
            pltpu.SemaphoreType.REGULAR((2,)),
        ],
        compiler_params=pltpu.CompilerParams(
            collective_id=0, has_side_effects=True, vmem_limit_bytes=48 << 20
        ),
        name="petra",
    )(
        *[
            pltpu.with_memory_space_constraint(x, pltpu.HBM)
            for x in (
                fwd_in.reshape(2, rows, W),
                back_out.reshape(2, rows, W),
                back_grad.reshape(2, rows, W),
                batch_next.reshape(2, rows, W),
                loss_grad.reshape(4, rows, W),
                weights.reshape(2 * C, 27 * C),
            )
        ]
    )
    fout, backs, grads, dw = pl.pallas_call(
        write_out,
        out_shape=(pair, pair, pair, share),
        in_specs=[vmem] * 4,
        out_specs=(hbm,) * 4,
        scratch_shapes=[dma((4,))],
        compiler_params=pltpu.CompilerParams(vmem_limit_bytes=4 << 20),
        name="write_out",
    )(fout, backs, grads, dw)
    shape = fwd_in.shape
    return fout.reshape(shape), backs.reshape(shape), grads.reshape(shape), dw[None]


def solution(mesh):
    field = P("segment", None, None, "slab", None, None)
    return jax.shard_map(
        functools.partial(local, mesh.shape["segment"], mesh.shape["slab"]),
        mesh=mesh,
        in_specs=(
            field,
            field,
            field,
            P(None, None, "slab", None, None),
            P(None, None, None, "slab", None, None),
            P("segment", None, None, None),
        ),
        out_specs=(field, field, field, P("segment", None, None, "slab")),
        check_vma=False,
    )
```

```python
import functools

import jax
import jax.numpy as jnp
from jax import lax
from jax.experimental import pallas as pl
from jax.experimental.pallas import tpu as pltpu
from jax.sharding import PartitionSpec as P

MESH = pl.DeviceIdType.MESH
F, G, FT, GT = range(4)
X1, X2, O1, O2, G1, G2 = range(6)
Y1, Y2, R1, R2, E1, E2 = range(6)
PX, PH, PD, PY, PU, PE = range(6)


def sigmoid(v):
    return 1.0 / (1.0 + jnp.exp(-v))


def silu(v):
    return v / (1.0 + jnp.exp(-v))


def slope(v):
    sig = sigmoid(v)
    return sig * (1.0 + v * (1.0 - sig))


def kernel(
    dims, fwd_hbm, bout_hbm, bgrad_hbm, nxt_hbm, loss_hbm, kern_hbm, fout, backs, grads, dw,
    fwd, bout, bgrad, nxt, loss, kern, kt, w, pairs, dt, pad, stage, second, edge, rest, made, nat, acc,
    g3, dsum, dpart, dgot, halo_s, halo_r, seg_s, seg_r, back_s, back_r, edge_s, edge_r, pass_s,
    out_s, d_s, d_r, in_s, ready_s,
):
    C, D, H, W, segs, n, scale = dims
    DH, HW = D * H, H * W
    cs = C // n
    LW = pl.cdiv(3 * C, 128) * 128
    f32, bf16 = jnp.float32, jnp.bfloat16
    seg = lax.axis_index("segment")
    slab = lax.axis_index("slab")
    has_prev, has_next = seg > 0, seg < segs - 1
    is_first, is_last = seg == 0, seg == segs - 1
    odd, even = lax.rem(seg, 2) == 1, lax.rem(seg, 2) == 0
    relayed = jnp.logical_and(has_next, odd)
    whole = jnp.logical_and(has_next, even)
    prev_seg = lax.rem(seg + segs - 1, segs)
    next_seg = lax.rem(seg + 1, segs)
    lane_no = lax.broadcasted_iota(jnp.int32, (C, W), 1)

    if n == 2:
        sides = [(None, 1 - slab, 0, 1 - slab)]
        toward = [(None, slab, 0, 1 - slab)]
    else:
        below, above = lax.rem(slab + n - 1, n), lax.rem(slab + 1, n)
        sides = [(slab > 0, 0, 0, below), (slab < n - 1, 1, 1, above)]
        toward = [(slab < n - 1, 0, 0, above), (slab > 0, 1, 1, below)]

    def over(rows, act):
        for there, side, slot, peer in rows:
            if there is None:
                act(side, slot, peer)
            else:
                pl.when(there)(functools.partial(act, side, slot, peer))

    def near_q(side):
        return side * (D + 1) - 1

    barrier = pltpu.get_barrier_semaphore()

    for k in range(1, n):
        pl.semaphore_signal(
            barrier, inc=1, device_id={"slab": lax.rem(slab + k, n)}, device_id_type=MESH
        )

    @pl.when(has_prev)
    def _():
        pl.semaphore_signal(barrier, inc=1, device_id={"segment": prev_seg}, device_id_type=MESH)

    @pl.when(has_next)
    def _():
        pl.semaphore_signal(barrier, inc=1, device_id={"segment": next_seg}, device_id_type=MESH)

    fetches = [
        pltpu.make_async_copy(src, dst, in_s.at[i])
        for i, (src, dst) in enumerate(
            [
                (bgrad_hbm, bgrad), (bout_hbm, bout), (fwd_hbm, fwd),
                (kern_hbm, kern), (nxt_hbm, nxt), (loss_hbm, loss),
            ]
        )
    ]
    for fetch in fetches:
        fetch.start()

    def lanes(at, size):
        return pl.ds(at if isinstance(at, int) else pl.multiple_of(at, W), size)

    def lane(q, hh):
        return ((q + 2) * (H + 2) + hh) * W

    zero = jnp.zeros((C, W), bf16)
    for t in range(2):
        for k in range(6):
            reach = 2 if t == 1 and k in (PH, PD) else 1
            for q in range(-reach, D + reach):
                for hh in (0, H + 1):
                    pad[t, k, :, pl.ds(lane(q, hh), W)] = zero

    for q, missing in ((-1, slab == 0), (D, slab == n - 1)):
        @pl.when(missing)
        def _():
            for t in range(2):
                for k in range(6):
                    pad[t, k, :, pl.ds(lane(q, 1), HW)] = jnp.zeros((C, HW), bf16)

    def load_stage(slot, ref, s):
        stage[slot] = ref[s].astype(f32)

    def staged(slot, r):
        return stage[slot, pl.ds(r, C, stride=DH), :]

    def prepare_weights():
        fetches[3].wait()
        wide = kern[...].astype(f32)
        kt[...] = jnp.concatenate([wide, jnp.zeros((LW - 2 * C, 27 * C), f32)], axis=0).T

        def tap(t):
            return kt[pl.ds(t, C, stride=27), :]

        def set_weights(m, a, c, block):
            here = pl.ds(c * C, C)
            w[m, a, here, :] = block
            if a < 2:
                pairs[m, a, here, 0 : 3 * C] = block
            if a > 0:
                pairs[m, a - 1, here, 3 * C : 6 * C] = block

        for a in range(3):
            for c in range(3):
                block = jnp.concatenate([tap(9 * a + 3 * b + c) for b in range(3)], axis=0).T
                for f in range(2):
                    set_weights(F + f, a, c, block[f * C : (f + 1) * C].astype(bf16))
                for f in range(2):
                    turned = jnp.concatenate(
                        [
                            tap(9 * (2 - a) + 3 * (2 - b) + 2 - c)[:, f * C : (f + 1) * C]
                            for b in range(3)
                        ],
                        axis=1,
                    )
                    set_weights(FT + f, a, c, turned.astype(bf16))

    def load_pair(i, slot, ref):
        fetches[i].wait()
        for s in range(2):
            load_stage(slot + s, ref, s)

    def halo(t, k, side, slot, peer):
        if k == PU:
            src = made.at[t, R2, :, lanes((1 - side) * (D - 1) * HW, HW)]
            dst = rest.at[slot]
        else:
            src = pad.at[t, k, :, lanes(lane((1 - side) * (D - 1), 1), HW)]
            dst = pad.at[t, k, :, lanes(lane(near_q(side), 1), HW)]
        return pltpu.make_async_remote_copy(
            src_ref=src, dst_ref=dst, send_sem=halo_s.at[slot], recv_sem=halo_r.at[6 if t else k, slot],
            device_id={"slab": peer}, device_id_type=MESH,
        )

    def halo_start(t, k):
        over(toward, lambda side, slot, peer: halo(t, k, side, slot, peer).start())

    def halo_arrived(t, k):
        over(sides, lambda side, slot, peer: halo(t, k, side, slot, peer).wait_recv())

    def to_seg(k):
        return pltpu.make_async_remote_copy(
            src_ref=made.at[0, k], dst_ref=second.at[k],
            send_sem=seg_s.at[1 if k <= X2 else 0], recv_sem=seg_r.at[k],
            device_id={"segment": next_seg if k <= X2 else prev_seg}, device_id_type=MESH,
        )

    def edge_at(k, far, side, slot):
        return edge.at[k, slot, :, lanes((side if far else 1 - side) * HW, HW)]

    def edge_copy(src, k, far, target, which, side, slot, peer):
        plane = (1 - side) * (D - 2) + side if far else (1 - side) * (D - 1)
        return pltpu.make_async_remote_copy(
            src_ref=src.at[:, lanes(plane * HW, HW)], dst_ref=edge_at(k, far, side, slot),
            send_sem=edge_s.at[which, slot], recv_sem=edge_r.at[k // 2 + 4 if far else k - 1, slot],
            device_id={"segment": target, "slab": peer}, device_id_type=MESH,
        )

    def edge_start(src, k, far, target, which):
        over(toward, lambda *side: edge_copy(src, k, far, target, which, *side).start())

    def edge_arrived(k, far, *side):
        edge_copy(made.at[0, k], k, far, seg, 0, *side).wait_recv()

    def pass_on(k, side, slot, peer):
        if k == G1:
            src = pad.at[0, PE, :, lanes(lane(near_q(side), 1), HW)]
        else:
            src = rest.at[slot]
        return pltpu.make_async_remote_copy(
            src_ref=src, dst_ref=edge_at(k, False, side, slot),
            send_sem=pass_s.at[slot], recv_sem=edge_r.at[k - 1, slot],
            device_id={"segment": prev_seg}, device_id_type=MESH,
        )

    def drain(sem, src):
        pltpu.make_async_remote_copy(
            src_ref=src, dst_ref=src, send_sem=sem, recv_sem=sem,
            device_id={"slab": lax.rem(slab + 1, n)}, device_id_type=MESH,
        ).wait_send()

    def planes_of(count):
        return pad.at[0, 0, :, pl.ds(0, count * HW)]

    def out_prev(k):
        dst = backs.at[k - R1] if k < E1 else grads.at[k - E1]
        return pltpu.make_async_remote_copy(
            src_ref=nat.at[k], dst_ref=dst, send_sem=back_s.at[0], recv_sem=back_r.at[0],
            device_id={"segment": prev_seg}, device_id_type=MESH,
        )

    def own_out(k):
        return pltpu.make_async_copy(nat.at[k], fout.at[k], out_s.at[0])

    def last_act(k):
        return pltpu.make_async_copy(nat.at[k], backs.at[k], out_s.at[1])

    def last_grad(k):
        return pltpu.make_async_copy(loss.at[2 + k], grads.at[k], out_s.at[1])

    def put(t, k, r, value):
        d, h = divmod(r, H)
        put_at(t, k, d, h, value)

    def put_at(t, k, q, h, value):
        pad[t, k, :, lanes(lane(q, h + 1), W)] = value.astype(bf16)

    def tall(t, k, q):
        return jnp.concatenate([pad[t, k, :, lanes(lane(q, b), HW)] for b in range(3)], axis=0)

    def taps(t, k, m, p, which):
        total, which = None, list(which)
        while which:
            a = which.pop(0)
            lhs, rhs = w[m, a], tall(t, k, p + a - 1)
            if which:
                which.pop(0)
                lhs = pairs[m, a]
                rhs = jnp.concatenate([rhs, tall(t, k, p + a)], axis=0)
            part = jnp.dot(lhs, rhs, preferred_element_type=f32)
            total = part if total is None else total + part
        return total

    def inner(p):
        return [a for a in range(3) if 0 <= p + a - 1 < D]

    def conv_local(t, k, m, slot):
        for p in range(D):
            acc[slot, :, pl.ds(p * HW, HW)] = taps(t, k, m, p, inner(p))

    def rows_of(total):
        for h in range(H):
            y = total[:, h * W : (h + 1) * W]
            left = jnp.where(lane_no == 0, 0.0, pltpu.roll(y[:C], 1, 1))
            right = jnp.where(lane_no == W - 1, 0.0, pltpu.roll(y[2 * C :], W - 1, 1))
            yield h, y[C : 2 * C] + left + right

    def conv_finish(t, k, m, slot, act, then=None):
        def outer(side):
            return jnp.dot(w[m, 2 * side], tall(t, k, near_q(side)), preferred_element_type=f32)

        def add(side, at, peer):
            acc[slot, :, lanes(side * (D - 1) * HW, HW)] += outer(side)

        if n > 2:
            over(sides, add)
        for i in range(D):
            p = (1 - slab) * (D - 1) + i * (2 * slab - 1) if n == 2 else i
            total = acc[slot, :, lanes(p * HW, HW)]
            if n == 2 and i == 0:
                total += outer(1 - slab)
            for h, out in rows_of(total):
                act(p * H + h, p, h, out)
            if then is not None and i == (0 if n == 2 else D - 1):
                then()

    def conv_whole(t, k, m):
        for p in range(D):
            for h, out in rows_of(taps(t, k, m, p, range(3))):
                yield p * H + h, out

    def widen(j, r, v):
        at = pl.ds(r * W, W)
        g3[j, 0:C, at] = jnp.where(lane_no == W - 1, 0.0, pltpu.roll(v, W - 1, 1)).astype(bf16)
        g3[j, C : 2 * C, at] = v.astype(bf16)
        g3[j, 2 * C : 3 * C, at] = jnp.where(lane_no == 0, 0.0, pltpu.roll(v, 1, 1)).astype(bf16)

    def product(lhs, j, p):
        return lax.dot_general(
            lhs, g3[j, :, lanes(p * HW, HW)], (((1,), (1,)), ((), ())), preferred_element_type=f32
        )

    def wgrad_inner(t, k, j):
        parts = [None] * 3
        for p in range(D):
            which = inner(p)
            part = product(jnp.concatenate([tall(t, k, p + a - 1) for a in which], axis=0), j, p)
            for i, a in enumerate(which):
                block = part[i * 3 * C : (i + 1) * 3 * C]
                parts[a] = block if parts[a] is None else parts[a] + block
        for a in range(3):
            here = pl.ds(a * 3 * C, 3 * C)
            if t == 0:
                dsum[j, here] = parts[a]
            else:
                dsum[j, here] += parts[a]

    def wgrad_whole(k, j):
        for p in range(D):
            lhs = jnp.concatenate([tall(1, k, p + a - 1) for a in range(3)], axis=0)
            part = product(lhs, j, p)
            total = part if p == 0 else total + part
        dsum[j] += total

    def wgrad_outer(t, k, j):
        def outer(side, slot, peer):
            at = side * 6 * C
            here = pl.ds(at if isinstance(at, int) else pl.multiple_of(at, 8), 3 * C)
            dsum[j, here] += product(tall(t, k, near_q(side)), j, side * (D - 1))

        over(sides, outer)

    def wgrad_share(j):
        for q in range(1, n):
            first = lax.rem(slab + q, n) * cs
            for ab in range(9):
                part = dsum[j, pl.ds(pl.multiple_of(ab * C + first, 8), cs)].astype(bf16)
                dpart[j, q - 1, ab] = jnp.concatenate(
                    [part, jnp.zeros((cs, LW - 3 * C), bf16)], axis=1
                )
            share(j, q).start()

    def share(j, q):
        target = lax.rem(slab + q, n)
        return pltpu.make_async_remote_copy(
            src_ref=dpart.at[j, q - 1], dst_ref=dgot.at[j, q - 1],
            send_sem=d_s.at[q - 1], recv_sem=d_r.at[j, q - 1],
            device_id={"slab": target}, device_id_type=MESH,
        )

    def keep(t, k, r, value):
        held = value.astype(bf16)
        made[t, k, :, lanes(r * W, W)] = held
        wide = held.astype(f32)
        if t == 1:
            stage[k, pl.ds(r, C, stride=DH), :] = wide
        return wide

    def straight(first, side):
        return lax.rem(seg, 4) == first

    def far_direct(side, slot, peer):
        @pl.when(straight(2, side))
        def _():
            for k in (O1, G2):
                edge_copy(made.at[0, k], k, True, prev_seg, 0, side, slot, peer).start()

    def far_relay(k):
        def act(side, slot, peer):
            @pl.when(jnp.logical_not(straight(1, side)))
            def _():
                edge_copy(second.at[k], k, True, seg, 3, side, slot, peer).start()

        @pl.when(relayed)
        def _():
            over(toward, act)

    def hand_on(k):
        src = made.at[0, k]
        if k <= X2:
            @pl.when(has_next)
            def _():
                if k == Y2:
                    edge_start(src, X2, False, next_seg, 1)
                to_seg(k).start()

            @pl.when(is_last)
            def _():
                edge_start(src, O1 + k, False, seg, 2)
                if k == Y1:
                    edge_start(src, O1, True, seg, 2)
                second[O1 + k] = made[0, k]
        else:
            @pl.when(has_prev)
            def _():
                to_seg(k).start()
                if k == O1:
                    edge_start(src, O1, False, prev_seg, 0)
                    edge_start(made.at[0, G2], G2, False, prev_seg, 0)
                    over(toward, far_direct)

    def hand_on_far():
        @pl.when(odd)
        def _():
            for k in (G2, O1):
                edge_start(made.at[0, k], k, True, prev_seg, 0)
            for k in (G1, O2):
                over(sides, lambda *side: pass_on(k, *side).start())

    def give_out(k):
        nat[k] = stage[k].astype(bf16)
        if k < R1:
            own_out(k).start()

            @pl.when(is_last)
            def _():
                last_act(k).start()
        else:
            @pl.when(has_prev)
            def _():
                out_prev(k).start()

    def arrived(k):
        there = has_prev if k <= X2 else whole if k in (G1, O2) else has_next

        @pl.when(there)
        def _():
            to_seg(k).wait_recv()

    load_pair(0, G1, bgrad)
    for r in range(DH):
        put(0, PD, r, staged(G2, r))
    peers = has_prev.astype(jnp.int32) + has_next.astype(jnp.int32) + n - 1
    pl.semaphore_wait(barrier, peers)
    halo_start(0, PD)

    @pl.when(has_prev)
    def _():
        pl.semaphore_signal(
            ready_s.at[1], inc=1, device_id={"segment": prev_seg}, device_id_type=MESH
        )

    @pl.when(has_next)
    def _():
        pl.semaphore_signal(
            ready_s.at[0], inc=1, device_id={"segment": next_seg}, device_id_type=MESH
        )

    load_pair(1, O1, bout)
    for r in range(DH):
        put(0, PH, r, silu(staged(O1, r)))
    halo_start(0, PH)
    load_pair(2, X1, fwd)
    for r in range(DH):
        put(0, PX, r, silu(staged(X2, r)))
    halo_start(0, PX)
    prepare_weights()
    conv_local(0, PD, GT, 0)
    conv_local(0, PH, G, 1)
    conv_local(0, PX, F, 2)
    for r in range(DH):
        widen(1, r, staged(G2, r))
    wgrad_inner(0, PH, 1)

    fetches[4].wait()
    fetches[5].wait()

    @pl.when(is_first)
    def _():
        for s in range(2):
            load_stage(6 + s, nxt, s)
            for r in range(DH):
                second[X1 + s, :, pl.ds(r * W, W)] = staged(6 + s, r).astype(bf16)
        edge_start(second.at[X2], X2, False, seg, 2)

    @pl.when(is_last)
    def _():
        for s in range(2):
            last_grad(s).start()
            load_stage(6 + s, loss, s)
            for r in range(DH):
                second[G1 + s, :, pl.ds(r * W, W)] = staged(6 + s, r).astype(bf16)
            edge_start(second.at[G1 + s], G1 + s, False, seg, 2)
        edge_start(second.at[G2], G2, True, seg, 2)

    @pl.when(has_prev)
    def _():
        pl.semaphore_wait(ready_s.at[0], 1)

    @pl.when(has_next)
    def _():
        pl.semaphore_wait(ready_s.at[1], 1)

    halo_arrived(0, PD)

    def act(r, p, h, out):
        put_at(0, PE, p, h, keep(0, E1, r, staged(G1, r) + slope(staged(O1, r)) * out))

    conv_finish(0, PD, GT, 0, act, functools.partial(halo_start, 0, PE))
    hand_on(E1)
    halo_arrived(0, PH)

    def act(r, p, h, out):
        put_at(0, PU, p, h, silu(keep(0, R2, r, staged(O2, r) - out)))

    conv_finish(0, PH, G, 1, act, functools.partial(halo_start, 0, PU))
    hand_on(R2)
    conv_local(0, PU, F, 1)
    wgrad_outer(0, PH, 1)
    halo_arrived(0, PX)

    def act(r, p, h, out):
        put_at(0, PY, p, h, silu(keep(0, Y1, r, staged(X1, r) + out)))

    conv_finish(0, PX, F, 2, act, functools.partial(halo_start, 0, PY))
    hand_on(Y1)
    conv_local(0, PE, FT, 0)
    for r in range(DH):
        widen(0, r, made[0, E1, :, pl.ds(r * W, W)].astype(f32))
    conv_local(0, PY, G, 2)
    wgrad_inner(0, PU, 0)

    halo_arrived(0, PE)

    def act(r, p, h, out):
        v = made[0, R2, :, lanes(r * W, W)].astype(f32)
        keep(0, E2, r, staged(G2, r) + slope(v) * out)

    conv_finish(0, PE, FT, 0, act)
    hand_on(E2)
    halo_arrived(0, PU)

    def rest_in(side, slot, peer):
        for h in range(H):
            v = rest[slot, :, pl.ds(h * W, W)].astype(f32)
            put_at(0, PU, near_q(side), h, silu(v))

    over(sides, rest_in)
    conv_finish(0, PU, F, 1, lambda r, p, h, out: keep(0, R1, r, staged(O1, r) - out))
    hand_on(R1)
    halo_arrived(0, PY)
    conv_finish(0, PY, G, 2, lambda r, p, h, out: keep(0, Y2, r, staged(X2, r) + out))
    hand_on(Y2)
    hand_on_far()
    wgrad_outer(0, PU, 0)

    def got(k, r):
        return second[k, :, lanes(r * W, W)].astype(f32)

    def near(k, side, slot, h):
        return edge[k, slot, :, lanes((1 - side) * HW + h * W, W)].astype(f32)

    @pl.when(relayed)
    def _():
        for k in (G1, O2):
            to_seg(k).wait_recv()
            edge_start(second.at[k], k, False, seg, 3)

    def forward_own():
        arrived(X2)
        for r in range(DH):
            put(1, PX, r, silu(got(X2, r)))
        conv_local(1, PX, F, 2)

    def forward():
        arrived(X1)

        def edges(side, slot, peer):
            edge_arrived(X2, False, side, slot, peer)
            for h in range(H):
                put_at(1, PX, near_q(side), h, silu(near(X2, side, slot, h)))

        over(sides, edges)

        def act(r, p, h, out):
            put_at(1, PY, p, h, silu(keep(1, Y1, r, got(X1, r) + out)))

        conv_finish(1, PX, F, 2, act, functools.partial(halo_start, 1, PY))
        conv_local(1, PY, G, 2)

    arrived(G2)
    far_relay(G2)

    pl.when(odd)(forward_own)
    for d in range(D):
        pad[1, PD, :, pl.ds(lane(d, 1), HW)] = second[G2, :, pl.ds(d * HW, HW)]
    conv_local(1, PD, GT, 0)
    arrived(O1)
    far_relay(O1)

    for r in range(DH):
        put(1, PH, r, silu(got(O1, r)))
    conv_local(1, PH, G, 1)
    for r in range(DH):
        widen(1, r, got(G2, r))
    pl.when(odd)(forward)

    def edge_q(far, side):
        return near_q(side) + (2 * side - 1 if far else 0), (side if far else 1 - side) * HW

    def grad_in(far, side, slot, peer):
        q, at = edge_q(far, side)
        edge_arrived(G2, far, side, slot, peer)
        pad[1, PD, :, lanes(lane(q, 1), HW)] = edge[G2, slot, :, lanes(at, HW)]

    def act_in(far, side, slot, peer):
        q, at = edge_q(far, side)
        edge_arrived(O1, far, side, slot, peer)
        for h in range(H):
            put_at(1, PH, q, h, silu(edge[O1, slot, :, lanes(at + h * W, W)].astype(f32)))

    over(sides, functools.partial(act_in, False))
    arrived(O2)

    def act(r, p, h, out):
        put_at(1, PU, p, h, silu(keep(1, R2, r, got(O2, r) - out)))

    conv_finish(1, PH, G, 1, act)
    over(sides, functools.partial(grad_in, False))
    arrived(G1)

    def act(r, p, h, out):
        put_at(1, PE, p, h, keep(1, E1, r, got(G1, r) + slope(got(O1, r)) * out))

    conv_finish(1, PD, GT, 0, act)

    def give_first():
        give_out(E1)
        give_out(R2)

    pl.when(even)(give_first)
    wgrad_whole(PH, 1)
    wgrad_share(1)

    def beyond_act(side, slot, peer):
        act_in(True, side, slot, peer)
        edge_arrived(O2, False, side, slot, peer)
        q = near_q(side)
        for h, out in rows_of(taps(1, PH, G, q, range(3))):
            value = (near(O2, side, slot, h) - out).astype(bf16).astype(f32)
            put_at(1, PU, q, h, silu(value))

    over(sides, beyond_act)
    for r in range(DH):
        widen(0, r, made[1, E1, :, pl.ds(r * W, W)].astype(f32))
    wgrad_whole(PU, 0)
    wgrad_share(0)

    def beyond_grad(side, slot, peer):
        grad_in(True, side, slot, peer)
        edge_arrived(G1, False, side, slot, peer)
        q = near_q(side)
        for h, out in rows_of(taps(1, PD, GT, q, range(3))):
            value = near(G1, side, slot, h) + slope(near(O1, side, slot, h)) * out
            put_at(1, PE, q, h, value)

    over(sides, beyond_grad)

    @pl.when(odd)
    def _():
        give_first()
        give_out(Y1)


    for r, out in conv_whole(1, PE, FT):
        v = made[1, R2, :, pl.ds(r * W, W)].astype(f32)
        keep(1, E2, r, got(G2, r) + slope(v) * out)
    give_out(E2)
    for r, out in conv_whole(1, PU, F):
        keep(1, R1, r, got(O1, r) - out)
    give_out(R1)

    def gradients():
        for j in (1, 0):
            for q in range(1, n):
                share(j, q).wait_recv()
            for ab in range(9):
                own = dsum[j, pl.ds(pl.multiple_of(ab * C + slab * cs, 8), cs)]
                total = jnp.concatenate([own, jnp.zeros((cs, LW - 3 * C), f32)], axis=1)
                for q in range(1, n):
                    total += dgot[j, q - 1, ab].astype(f32)
                total *= scale
                for c in range(3):
                    tap = total if c == 0 else pltpu.roll(total, LW - c * C, 1)
                    dt[j, pl.ds(3 * ab + c, cs, stride=27), :] = tap
            dw[j] = dt[j].T[:C]

    @pl.when(even)
    def _():
        forward_own()
        forward()
        give_out(Y1)
        gradients()

    halo_arrived(1, PY)
    conv_finish(1, PY, G, 2, lambda r, p, h, out: keep(1, Y2, r, got(X2, r) + out))
    give_out(Y2)
    pl.when(odd)(gradients)

    def drain_edges(which, first, fewer, more):
        def act(side, slot, peer):
            direct = straight(first, side)
            sem = edge_s.at[which, slot]
            pl.when(direct)(lambda: drain(sem, planes_of(more)))
            pl.when(jnp.logical_not(direct))(lambda: drain(sem, planes_of(fewer)))

        over(toward, act)

    over(toward, lambda side, slot, peer: drain(halo_s.at[slot], planes_of(7)))
    for q in range(1, n):
        drain(d_s.at[q - 1], dpart.at[:, 0])
    pltpu.make_async_copy(nat.at[pl.ds(Y1, 2)], fout, out_s.at[0]).wait()

    @pl.when(is_first)
    def _():
        over(toward, lambda side, slot, peer: drain(edge_s.at[2, slot], planes_of(1)))

    @pl.when(is_last)
    def _():
        pltpu.make_async_copy(nat.at[pl.ds(0, 4)], nat.at[pl.ds(0, 4)], out_s.at[1]).wait()
        over(toward, lambda side, slot, peer: drain(edge_s.at[2, slot], planes_of(6)))

    @pl.when(has_next)
    def _():
        drain(seg_s.at[1], made.at[0, pl.ds(0, 2)])
        over(toward, lambda side, slot, peer: drain(edge_s.at[1, slot], planes_of(1)))
        drain(back_r.at[0], nat.at[pl.ds(R1, 4)])

    @pl.when(has_prev)
    def _():
        drain(seg_s.at[0], made.at[0, pl.ds(0, 4)])
        drain(back_s.at[0], nat.at[pl.ds(R1, 4)])

        @pl.when(even)
        def _():
            drain_edges(0, 2, 2, 4)

    @pl.when(odd)
    def _():
        over(toward, lambda side, slot, peer: drain(edge_s.at[0, slot], planes_of(4)))
        over(sides, lambda side, slot, peer: drain(pass_s.at[slot], planes_of(2)))

    @pl.when(relayed)
    def _():
        drain_edges(3, 1, 4, 2)


def write_out(*refs):
    srcs, dsts, sems = refs[:4], refs[4:8], refs[8]
    writes = [pltpu.make_async_copy(a, b, sems.at[i]) for i, (a, b) in enumerate(zip(srcs, dsts))]
    for write in writes:
        write.start()
    for write in writes:
        write.wait()


def local(segs, n, fwd_in, back_out, back_grad, batch_next, loss_grad, weights):
    _, _, C, D, H, W = fwd_in.shape
    rows = C * D * H
    cs = C // n
    ends = 1 if n == 2 else 2
    f32, bf16 = jnp.float32, jnp.bfloat16
    scale = float(D * n * H * W) ** (-0.5)
    vmem = pl.BlockSpec(memory_space=pltpu.VMEM)
    hbm = pl.BlockSpec(memory_space=pltpu.HBM)
    wide = pl.cdiv(3 * C, 128) * 128
    anywhere = pl.BlockSpec(memory_space=pl.ANY)
    pair = jax.ShapeDtypeStruct((2, rows, W), bf16)
    share = jax.ShapeDtypeStruct((2, C, 27 * cs), f32)
    dma = pltpu.SemaphoreType.DMA
    fout, backs, grads, dw = pl.pallas_call(
        functools.partial(kernel, (C, D, H, W, segs, n, scale)),
        out_shape=tuple(pltpu.VMEM(x.shape, x.dtype) for x in (pair, pair, pair, share)),
        in_specs=[hbm] * 6,
        out_specs=(vmem, vmem, vmem, vmem),
        scratch_shapes=[
            pltpu.VMEM((2, rows, W), bf16),
            pltpu.VMEM((2, rows, W), bf16),
            pltpu.VMEM((2, rows, W), bf16),
            pltpu.VMEM((2, rows, W), bf16),
            pltpu.VMEM((4, rows, W), bf16),
            pltpu.VMEM((2 * C, 27 * C), bf16),
            pltpu.VMEM((27 * C, wide), f32),
            pltpu.VMEM((4, 3, 3 * C, 3 * C), bf16),
            pltpu.VMEM((4, 2, 3 * C, 6 * C), bf16),
            pltpu.VMEM((2, 27 * cs, wide), f32),
            pltpu.VMEM((2, 6, C, (D + 4) * (H + 2) * W), bf16),
            pltpu.VMEM((8, rows, W), f32),
            pltpu.VMEM((6, C, D * H * W), bf16),
            pltpu.VMEM((6, ends, C, 2 * H * W), bf16),
            pltpu.VMEM((ends, C, H * W), bf16),
            pltpu.VMEM((2, 6, C, D * H * W), bf16),
            pltpu.VMEM((6, rows, W), bf16),
            pltpu.VMEM((3, 3 * C, D * H * W), f32),
            pltpu.VMEM((2, 3 * C, D * H * W), bf16),
            pltpu.VMEM((2, 9 * C, 3 * C), f32),
            pltpu.VMEM((2, n - 1, 9, cs, wide), bf16),
            pltpu.VMEM((2, n - 1, 9, cs, wide), bf16),
            dma((ends,)),
            dma((7, ends)),
            dma((2,)),
            dma((6,)),
            dma((1,)),
            dma((1,)),
            dma((4, ends)),
            dma((7, ends)),
            dma((ends,)),
            dma((2,)),
            dma((n - 1,)),
            dma((2, n - 1)),
            dma((6,)),
            pltpu.SemaphoreType.REGULAR((2,)),
        ],
        compiler_params=pltpu.CompilerParams(
            collective_id=0, has_side_effects=True, vmem_limit_bytes=48 << 20
        ),
        name="petra",
    )(
        *[
            pltpu.with_memory_space_constraint(x, pltpu.HBM)
            for x in (
                fwd_in.reshape(2, rows, W),
                back_out.reshape(2, rows, W),
                back_grad.reshape(2, rows, W),
                batch_next.reshape(2, rows, W),
                loss_grad.reshape(4, rows, W),
                weights.reshape(2 * C, 27 * C),
            )
        ]
    )
    fout, backs, grads, dw = pl.pallas_call(
        write_out,
        out_shape=(pair, pair, pair, share),
        in_specs=[vmem] * 4,
        out_specs=(hbm,) * 4,
        scratch_shapes=[dma((4,))],
        compiler_params=pltpu.CompilerParams(vmem_limit_bytes=4 << 20),
        name="write_out",
    )(fout, backs, grads, dw)
    shape = fwd_in.shape
    return fout.reshape(shape), backs.reshape(shape), grads.reshape(shape), dw[None]


def solution(mesh):
    field = P("segment", None, None, "slab", None, None)
    return jax.shard_map(
        functools.partial(local, mesh.shape["segment"], mesh.shape["slab"]),
        mesh=mesh,
        in_specs=(
            field,
            field,
            field,
            P(None, None, "slab", None, None),
            P(None, None, None, "slab", None, None),
            P("segment", None, None, None),
        ),
        out_specs=(field, field, field, P("segment", None, None, "slab")),
        check_vma=False,
    )
```
